256 devices in a mesh: child: 2 (over core), row: 4 (over x), col: 32 (over y, z).
Axes of the slice: x: 4, y: 4, z: 8, core: 2. Of those that a mesh axis runs over, the one named last changes fastest.
Arguments:
- schur_blocks: bfloat16 [2, 16384, 16384], P('child', 'row', 'col'), may hold values from -2 to 2
- child_map: int32 [2, 16384], replicated, may hold values from 0 to 24575, as said below
- round_seeds: int32 [2], replicated, may hold values from 1 to 999999
Outputs:
- leaf_bases: float32 [24576, 256], P(('row', 'child', 'col'))
- fresh_samples: float32 [24576, 256], P(('row', 'child', 'col'))
The draws below stay inside these ranges and needn't reach their ends.
Inputs may be any that keep to these rules, and one draw needn't show every extreme that they name: For each child c and each block r < 4, the entries child_map[c, r * 4096 : (r + 1) * 4096] rise strictly, lie in parent rows [r * 6144, (r + 1) * 6144), and include both ends of that range.
All inputs are finite; a program needn't handle non-finite values.
Results may differ from the reference program's by a relative error of at most 0.0031.
Values sent between devices are 32-bit elements; how exact they have to be, the bound alone decides.
A program may use at most 64 MiB of HBM per device.

```python
import math
import jax
import jax.numpy as jnp
from jax import lax

NC = 16384
NP = 24576
K = 256
NCB = 4096
NPB = 6144


def draw_schur_blocks(key, part):
    key_main = jax.random.fold_in(key, 101)
    key_base, key_scale = jax.random.split(key_main)
    base_draw = jnp.clip(jax.random.normal(key_base, (2, NC, NC), jnp.float32), -4.0, 4.0)
    spread = jax.random.uniform(key_scale, (2, NC), jnp.float32, 0.0, math.log(10.0 / 3.0))
    within = (jnp.arange(NC) % NCB).astype(jnp.float32) / NCB
    row_scale = jnp.exp(within * math.log(3.0))[None, :] * jnp.exp(spread)
    return (base_draw * row_scale[:, :, None] * NC ** (-0.5)).astype(jnp.bfloat16)


def one_block_map(block_key, block_number):
    interior = jax.random.permutation(block_key, NPB - 2)[:NCB - 2] + 1
    chosen = jnp.concatenate([jnp.zeros((1,), jnp.int32), interior.astype(jnp.int32), jnp.full((1,), NPB - 1, jnp.int32)])
    return jnp.sort(chosen) + block_number * NPB


def draw_child_map(key, part):
    key_main = jax.random.fold_in(key, 23)
    block_total = NC // NCB
    block_keys = jax.random.split(key_main, 2 * block_total)
    block_numbers = jnp.tile(jnp.arange(block_total, dtype=jnp.int32), 2)
    mapped = jax.vmap(one_block_map)(block_keys, block_numbers)
    return mapped.reshape(2, NC).astype(jnp.int32)


def setup_inputs(seed: int = 0) -> dict:
    splits = jax.random.split(jax.random.key(seed), 4)
    schur_blocks = draw_schur_blocks(jax.random.fold_in(splits[3], 71), 0)
    child_map = draw_child_map(jax.random.fold_in(splits[3], 71), 0)
    round_seeds = jax.random.randint(splits[2], (2,), 1, 1000000).astype(jnp.int32)
    return dict(schur_blocks=schur_blocks, child_map=child_map, round_seeds=round_seeds)


def sample_rows(seed_value, parents, sample_width):
    hashed = parents[:, None] * 40503 + lax.iota(jnp.int32, sample_width)[None, :] * 9973 + seed_value * 2654435
    hashed = hashed ^ hashed >> 15 & 131071
    hashed = hashed * 73244475
    hashed = hashed ^ hashed >> 13 & 524287
    hashed = hashed * 1274126177
    hashed = hashed ^ hashed >> 16 & 65535
    unit_value = (hashed & 16777215).astype(jnp.float32) * (1.0 / 16777216.0)
    return (unit_value - 0.5) * 3.4641016

def project_leaf(first_leaf, second_leaf):
    gram_matrix = jnp.dot(first_leaf.T, first_leaf, precision=lax.Precision.HIGHEST) / NPB
    lower_factor = jnp.linalg.cholesky(gram_matrix)
    leaf_basis = lax.linalg.triangular_solve(lower_factor, first_leaf, left_side=False, lower=True, transpose_a=True)
    coefficients = jnp.dot(leaf_basis.T, second_leaf, precision=lax.Precision.HIGHEST) / NPB
    return (leaf_basis, second_leaf - jnp.dot(leaf_basis, coefficients, precision=lax.Precision.HIGHEST))

def reference(schur_blocks, child_map, round_seeds):
    parents = jnp.arange(NP, dtype=jnp.int32)
    samples = jnp.concatenate([sample_rows(round_seeds[0], parents, K), sample_rows(round_seeds[1], parents, K)], axis=1).astype(jnp.bfloat16)
    parent_sketch = jnp.zeros((NP, 2 * K), jnp.float32)
    for child_number in range(2):
        mapped = child_map[child_number]
        child_sketch = jnp.dot(schur_blocks[child_number].astype(jnp.float32), samples[mapped].astype(jnp.float32), preferred_element_type=jnp.float32)
        parent_sketch = parent_sketch.at[mapped].add(child_sketch)
    leaves = parent_sketch.reshape(NP // NPB, NPB, 2 * K)
    leaf_bases, fresh_samples = jax.vmap(project_leaf)(leaves[:, :, :K], leaves[:, :, K:])
    return (leaf_bases.reshape(NP, K), fresh_samples.reshape(NP, K))
```

```python
import functools
import jax
import jax.numpy as jnp
from jax import lax
from jax.experimental import pallas as pl
from jax.experimental.pallas import tpu as pltpu
from jax.sharding import PartitionSpec as P

K = 256
TILE = 128
STEP_TILES = 4
GRIDS = {32: (4, 8), 8: (4, 2), 4: (2, 2), 16: (4, 4)}
MESH = pl.DeviceIdType.MESH
HI = lax.Precision.HIGHEST
F32 = jnp.float32


def hash_values(ids_row, col, seed):
    h = ids_row * 40503 + col * 9973 + seed * 2654435
    h = h ^ ((h >> 15) & 131071)
    h = h * 73244475
    h = h ^ ((h >> 13) & 524287)
    h = h * 1274126177
    h = h ^ ((h >> 16) & 65535)
    unit = (h & 16777215).astype(F32) * (1.0 / 16777216.0)
    return (unit - 0.5) * 3.4641016


def sketch_kernel(base_ref, starts_ref, seeds_ref, ids_ref, map_ref, a_ref, out_ref, st_ref, e_ref):
    step = pl.program_id(0)
    cols = ids_ref.shape[1]

    @pl.when(step == 0)
    def _():
        ids = ids_ref[...]

        def draw(i, carry):
            j0 = pl.multiple_of(i * 32, 32)
            t = j0 // K
            col = lax.broadcasted_iota(jnp.int32, (32, cols), 0) + (j0 - t * K)
            st_ref[pl.ds(j0, 32), :] = hash_values(ids, col, seeds_ref[t]).astype(jnp.bfloat16)
            return carry

        lax.fori_loop(0, 2 * K // 32, draw, 0)

    for q in range(STEP_TILES):
        t = step * STEP_TILES + q
        b = starts_ref[t]
        window = jnp.concatenate([map_ref[pl.ds(b, 1), :], map_ref[pl.ds(b + 1, 1), :]], axis=1)
        wanted = lax.broadcasted_iota(jnp.int32, (TILE, 2 * TILE), 0) + (base_ref[0] + t * TILE)
        pick = jnp.where(window == wanted, 1.0, 0.0).astype(jnp.bfloat16)
        rows = a_ref[pl.ds(pl.multiple_of(b * TILE, TILE), 2 * TILE), :]
        e_ref[q * TILE:(q + 1) * TILE, :] = jnp.dot(
            pick, rows, preferred_element_type=F32
        ).astype(jnp.bfloat16)
    for half in range(2):
        out_ref[half] = lax.dot_general(
            e_ref[...], st_ref[half * K:(half + 1) * K, :], (((1,), (1,)), ((), ())),
            preferred_element_type=F32,
        )


def sketch(child_block, block_map, col_ids, seeds, leaf_base, leaf_rows):
    block_rows, block_cols = child_block.shape
    map2d = block_map.reshape(block_rows // TILE, TILE)
    tiles = leaf_rows // TILE
    firsts = leaf_base + lax.iota(jnp.int32, tiles) * TILE
    starts = jnp.sum((map2d[:, TILE - 1][None, :] < firsts[:, None]).astype(jnp.int32), axis=1)
    starts = jnp.minimum(starts, block_rows // TILE - 2)
    rows = STEP_TILES * TILE
    smem = pl.BlockSpec(memory_space=pltpu.SMEM)
    return pl.pallas_call(
        sketch_kernel,
        grid=(leaf_rows // rows,),
        out_shape=jax.ShapeDtypeStruct((2, leaf_rows, K), F32),
        in_specs=[
            smem, smem, smem,
            pl.BlockSpec((1, block_cols), lambda i: (0, 0)),
            pl.BlockSpec(map2d.shape, lambda i: (0, 0)),
            pl.BlockSpec((block_rows, block_cols), lambda i: (0, 0)),
        ],
        out_specs=pl.BlockSpec((2, rows, K), lambda i: (0, i, 0)),
        scratch_shapes=[
            pltpu.VMEM((2 * K, block_cols), jnp.bfloat16),
            pltpu.VMEM((rows, block_cols), jnp.bfloat16),
        ],
        compiler_params=pltpu.CompilerParams(vmem_limit_bytes=40 << 20),
    )(leaf_base.reshape(1), starts, seeds, col_ids.reshape(1, block_cols), map2d, child_block)


def row_sets(rows):
    if rows == 96:
        return [("Y", 0, 32, 0), ("Z", 32, 16, 0), ("Y", 48, 24, 1), ("Z", 72, 24, 1)]
    q = rows // 4
    return [("Y", 0, q, 0), ("Z", q, q, 0), ("Y", 2 * q, q, 1), ("Z", 3 * q, q, 1)]


def hops(n, orient):
    long, short = n // 2, n - 1 - n // 2
    return (short, long) if orient else (long, short)


def reduce_kernel(ny, nz, rows, p_ref, y_ref, g_ref, *refs):
    sets = row_sets(rows)
    nsets = len(sets)
    h_ref, r_ref = refs[0], refs[1]
    slots1 = refs[2:2 + nsets]
    slots2 = refs[2 + nsets:2 + 2 * nsets]
    (ypad, gloc, gpart, gz, zr, gs, yr, gf,
     load_sem, xs, xr, s1, q1, s2, q2, as_, ar_) = refs[2 + 2 * nsets:]

    c = lax.axis_index("child")
    k = lax.axis_index("col")
    my_y = k // nz
    my_z = k - my_y * nz
    other = 1 - c

    def at_y(y):
        return {"col": y * nz + my_z}

    def at_z(z):
        return {"col": my_y * nz + z}

    pending = []

    def put(src, dst, ssem, rsem, dev):
        cp = pltpu.make_async_remote_copy(
            src_ref=src, dst_ref=dst, send_sem=ssem, recv_sem=rsem,
            device_id=dev, device_id_type=MESH)
        cp.start()
        pending.append(cp)
        return cp

    loads = []
    for h in range(2):
        cp = pltpu.make_async_copy(p_ref.at[h, c], h_ref.at[h], load_sem.at[h])
        cp.start()
        loads.append(cp)

    barrier = pltpu.get_barrier_semaphore()
    peers = [{"child": other}]
    peers += [at_y(lax.rem(my_y + j, ny)) for j in range(1, ny)]
    peers += [at_z(lax.rem(my_z + j, nz)) for j in range(1, nz)]
    for dev in peers:
        pl.semaphore_signal(barrier, inc=1, device_id=dev, device_id_type=MESH)
    pl.semaphore_wait(barrier, len(peers))

    swaps = {}
    for h in range(2):
        for i, (_, r0, nr, _) in enumerate(sets):
            swaps[h, i] = put(
                p_ref.at[h, other, :, :, pl.ds(r0, nr), :],
                r_ref.at[h, :, :, pl.ds(r0, nr), :],
                xs.at[h, i], xr.at[h, i], {"child": other})

    class Ring:
        def __init__(self, n, pos, at, orient, own, own_ix, lead, slot, slot_ix, ssem, rsem):
            self.n, self.pos, self.at = n, pos, at
            self.hp, self.hm = hops(n, orient)
            self.own, self.own_ix, self.lead = own, own_ix, lead
            self.slot, self.slot_ix, self.ssem, self.rsem = slot, slot_ix, ssem, rsem
            self.copies = {}

        def send(self, sign, s):
            n, reach = self.n, self.hp if sign > 0 else self.hm
            base = 0 if sign > 0 else self.hp
            d = lax.rem(self.pos + sign * (reach - s) + n, n)
            dev = self.at(lax.rem(self.pos + sign + n, n))
            if s:
                self.add(base + s - 1, d)
            src = self.slot(base + s - 1) if s else self.own(d)
            m = base + s
            self.copies[m] = put(src, self.slot(m), self.ssem(m), self.rsem(m), dev)

        def add(self, m, d):
            ref, ix = self.slot_ix
            own, oix = self.own_ix
            self.copies[m].wait_recv()

            def body(i, carry):
                ref[ix(m, i)] = ref[ix(m, i)] + own[oix(d, i)]
                return carry
            lax.fori_loop(0, self.lead, body, 0)

        def turn(self, s):
            if s < self.hp:
                self.send(1, s)
            if s < self.hm:
                self.send(-1, s)

        @property
        def turns(self):
            return max(self.hp, self.hm)

        def finish(self):
            ref, ix = self.slot_ix
            own, oix = self.own_ix
            last = [m for m, ok in ((self.hp - 1, self.hp), (self.hp + self.hm - 1, self.hm)) if ok]
            for m in last:
                self.copies[m].wait_recv()

            def body(i, carry):
                total = own[oix(self.pos, i)]
                for m in last:
                    total = total + ref[ix(m, i)]
                own[oix(self.pos, i)] = total
                return carry
            lax.fori_loop(0, self.lead, body, 0)

    def flow(h, i):
        color, r0, nr, orient = sets[i]
        rs = pl.ds(r0, nr)
        sl1, sl2 = slots1[i], slots2[i]
        sems = (lambda m: s1.at[h, i, m], lambda m: q1.at[h, i, m])
        sems2 = (lambda m: s2.at[h, i, m], lambda m: q2.at[h, i, m])
        ring1 = (lambda m: sl1.at[h, m], (sl1, lambda m, j: (h, m, j)))
        ring2 = (lambda m: sl2.at[h, m], (sl2, lambda m, j: (h, m, j)))
        if color == "Y":
            first = Ring(ny, my_y, at_y, orient,
                         lambda d: h_ref.at[h, d, :, rs, :],
                         (h_ref, lambda d, j: (h, d, j, rs, slice(None))), nz,
                         *ring1, *sems)
            second = Ring(nz, my_z, at_z, orient,
                          lambda d: h_ref.at[h, my_y, pl.ds(d, 1), rs, :],
                          (h_ref, lambda d, j: (h, my_y, d, rs, slice(None))), 1,
                          *ring2, *sems2)
        else:
            first = Ring(nz, my_z, at_z, orient,
                         lambda d: h_ref.at[h, :, d, rs, :],
                         (h_ref, lambda d, j: (h, j, d, rs, slice(None))), ny,
                         *ring1, *sems)
            second = Ring(ny, my_y, at_y, orient,
                          lambda d: h_ref.at[h, pl.ds(d, 1), my_z, rs, :],
                          (h_ref, lambda d, j: (h, d, my_z, rs, slice(None))), 1,
                          *ring2, *sems2)

        def begin():
            swaps[h, i].wait_recv()

            def body(y, carry):
                for z in range(nz):
                    ix = (h, y, z, rs, slice(None))
                    h_ref[ix] = h_ref[ix] + r_ref[ix]
                return carry
            lax.fori_loop(0, ny, body, 0)
            first.turn(0)

        def middle():
            first.finish()
            second.turn(0)

        acts = [begin]
        acts += [functools.partial(first.turn, s) for s in range(1, first.turns)]
        acts += [middle]
        acts += [functools.partial(second.turn, s) for s in range(1, second.turns)]
        acts += [second.finish]
        unit1, unit2 = (4.0, 2.0) if color == "Y" else (2.0, 2.0)
        times, t = [], h * 4.0 + 0.1 * i
        for a in range(len(acts)):
            times.append(t)
            t += unit1 if a < first.turns else unit2
        return list(zip(times, acts))

    for cp in loads:
        cp.wait()
    order = []
    for h in range(2):
        for i in range(nsets):
            order += flow(h, i)
    order.sort(key=lambda e: e[0])
    for _, act in order:
        act()

    ypad[...] = jnp.zeros_like(ypad)
    for h in range(2):
        ypad[0:rows, h * K:(h + 1) * K] = h_ref[h, my_y, my_z]
        y_ref[h] = h_ref[h, my_y, my_z]
    first_t = jnp.transpose(ypad[:, 0:K])
    gloc[...] = jnp.dot(first_t, ypad[...], precision=HI, preferred_element_type=F32).reshape(gloc.shape)

    cp = put(gloc.at[other], gpart, as_.at[0], ar_.at[0], {"child": other})
    cp.wait_recv()
    half = gloc[c] + gpart[...]
    gz[...] = half.reshape(gz.shape)
    got = []
    for j in range(1, nz):
        z = lax.rem(my_z + j, nz)
        got.append(put(gz.at[z], zr.at[j - 1], as_.at[j], ar_.at[j], at_z(z)))
    total = gz[my_z]
    for j in range(1, nz):
        got[j - 1].wait_recv()
        total = total + zr[j - 1]
    gs[...] = total
    got = []
    for j in range(1, ny):
        y = lax.rem(my_y + j, ny)
        got.append(put(gs, yr.at[j - 1], as_.at[nz + j - 1], ar_.at[nz + j - 1], at_y(y)))
    for j in range(1, ny):
        got[j - 1].wait_recv()
        total = total + yr[j - 1]
    gf[c, my_z] = total
    off = nz + ny - 1
    got = []
    for j in range(1, nz):
        z = lax.rem(my_z + j, nz)
        got.append(put(gf.at[c, my_z], gf.at[c, my_z], as_.at[off + j], ar_.at[off + j], at_z(z)))
    off2 = off + nz
    gave = [put(gf.at[c, my_z], gf.at[c, my_z], as_.at[off2], ar_.at[off2], {"child": other})]
    for j in range(1, nz):
        got[j - 1].wait_recv()
        z = lax.rem(my_z - j + nz, nz)
        gave.append(put(gf.at[c, z], gf.at[c, z], as_.at[off2 + j], ar_.at[off2 + j], {"child": other}))
    for cp in gave:
        cp.wait_recv()
    g_ref[...] = gf[...].reshape(g_ref.shape)
    for cp in pending:
        cp.wait_send()


def reduce_sketch(partial, ny, nz, rows):
    sets = row_sets(rows)
    cols = ny * nz
    shaped = partial.reshape(2, 2, ny, nz, rows, K)
    vm = pltpu.VMEM
    slots1 = [vm((2, (ny if s[0] == "Y" else nz) - 1, nz if s[0] == "Y" else ny, s[2], K), F32) for s in sets]
    slots2 = [vm((2, (nz if s[0] == "Y" else ny) - 1, 1, s[2], K), F32) for s in sets]
    dma = pltpu.SemaphoreType.DMA
    most = max(ny, nz) - 1
    piece = K // 2 // nz
    n_ar = 3 * nz + ny - 1
    return pl.pallas_call(
        functools.partial(reduce_kernel, ny, nz, rows),
        out_shape=(
            jax.ShapeDtypeStruct((2, rows, K), F32),
            jax.ShapeDtypeStruct((K, 2 * K), F32),
        ),
        in_specs=[pl.BlockSpec(memory_space=pl.ANY)],
        out_specs=[pl.BlockSpec(memory_space=pltpu.VMEM)] * 2,
        scratch_shapes=[
            vm((2, ny, nz, rows, K), F32), vm((2, ny, nz, rows, K), F32),
            *slots1, *slots2,
            vm((128, 2 * K), F32), vm((2, K // 2, 2 * K), F32), vm((K // 2, 2 * K), F32),
            vm((nz, piece, 2 * K), F32), vm((nz - 1, piece, 2 * K), F32), vm((piece, 2 * K), F32),
            vm((ny - 1, piece, 2 * K), F32), vm((2, nz, piece, 2 * K), F32),
            dma((2,)), dma((2, 4)), dma((2, 4)),
            dma((2, 4, most)), dma((2, 4, most)), dma((2, 4, most)), dma((2, 4, most)),
            dma((n_ar,)), dma((n_ar,)),
        ],
        compiler_params=pltpu.CompilerParams(
            collective_id=0, has_side_effects=True, vmem_limit_bytes=48 << 20),
    )(shaped)


BLK = 64


def solve_kernel(scale, y_ref, g_ref, q_ref, f_ref, aug_ref):
    rows = y_ref.shape[1]
    aug_ref[:, 0:K] = g_ref[:, 0:K] * scale
    aug_ref[:, K:2 * K] = g_ref[:, K:2 * K] * scale
    y1 = jnp.concatenate([y_ref[0], jnp.zeros((128 - rows, K), F32)], axis=0)
    aug_ref[:, 2 * K:2 * K + 128] = jnp.transpose(y1)
    sub = lax.broadcasted_iota(jnp.int32, (BLK, BLK), 0)
    lane = lax.broadcasted_iota(jnp.int32, (BLK, BLK), 1)
    for b in range(K // BLK):
        lo, hi = b * BLK, (b + 1) * BLK
        d = aug_ref[lo:hi, lo:hi]
        inv = jnp.where(sub == lane, 1.0, 0.0)
        for j in range(BLK):
            row = d[j:j + 1, :]
            factor = d[:, j:j + 1] * (1.0 / row[:, j:j + 1])
            factor = jnp.where(sub[:, 0:1] > j, factor, 0.0)
            irow = inv[j:j + 1, :]
            d = d - factor * row
            inv = inv - factor * irow
        pivots = jnp.sum(jnp.where(sub == lane, d, 0.0), axis=1, keepdims=True)
        inv = inv * (1.0 / jnp.sqrt(pivots))
        z = jnp.dot(inv, aug_ref[lo:hi, :], precision=HI, preferred_element_type=F32)
        aug_ref[lo:hi, :] = z
        if hi < K:
            u = jnp.transpose(aug_ref[lo:hi, hi // 128 * 128:K])
            u = u[hi - hi // 128 * 128:, :]
            aug_ref[hi:K, :] = aug_ref[hi:K, :] - jnp.dot(
                u, z, precision=HI, preferred_element_type=F32)
    basis = jnp.transpose(aug_ref[:, 2 * K:2 * K + 128])
    coef = aug_ref[:, K:2 * K]
    fit = jnp.dot(basis, coef, precision=HI, preferred_element_type=F32)
    q_ref[...] = basis[0:rows, :]
    f_ref[...] = y_ref[1] - fit[0:rows, :]


def solve(sketch_rows, grams, leaf_rows):
    rows = sketch_rows.shape[1]
    out = jax.ShapeDtypeStruct((rows, K), F32)
    return pl.pallas_call(
        functools.partial(solve_kernel, 1.0 / leaf_rows),
        out_shape=(out, out),
        in_specs=[pl.BlockSpec(memory_space=pltpu.VMEM)] * 2,
        out_specs=[pl.BlockSpec(memory_space=pltpu.VMEM)] * 2,
        scratch_shapes=[pltpu.VMEM((K, 2 * K + 128), F32)],
    )(sketch_rows, grams)


def make_body(parent_rows):
    def body(schur_blocks, child_map, round_seeds):
        child_block = schur_blocks[0]
        block_rows, block_cols = child_block.shape
        col_count = lax.axis_size("col")
        ny, nz = GRIDS[col_count]
        row_count = lax.axis_size("row")
        child, row, col = (lax.axis_index(a) for a in ("child", "row", "col"))
        leaf_rows = parent_rows // row_count
        own_rows = leaf_rows // (2 * col_count)
        own_map = lax.dynamic_index_in_dim(child_map, child, 0, keepdims=False)
        col_ids = lax.dynamic_slice_in_dim(own_map, col * block_cols, block_cols)
        block_map = lax.dynamic_slice_in_dim(own_map, row * block_rows, block_rows)
        partial = sketch(child_block, block_map, col_ids, round_seeds, row * leaf_rows, leaf_rows)
        y, g = reduce_sketch(partial, ny, nz, own_rows)
        return solve(y, g, leaf_rows)
    return body


def solution(mesh, parent_rows=24576):
    placed = (P("child", "row", "col"), P(), P())
    return jax.shard_map(
        make_body(parent_rows),
        mesh=mesh,
        in_specs=placed,
        out_specs=(P(("row", "child", "col"), None), P(("row", "child", "col"), None)),
        check_vma=False,
    )
```

```python
import functools
import jax
import jax.numpy as jnp
from jax import lax
from jax.experimental import pallas as pl
from jax.experimental.pallas import tpu as pltpu
from jax.sharding import PartitionSpec as P

K = 256
TILE = 128
BLK = 32
GRIDS = {32: (4, 8), 8: (2, 4)}
MESH = pl.DeviceIdType.MESH
HI = lax.Precision.HIGHEST
F32 = jnp.float32
RATE = 46.0e3
HOP = 0.75
BASE = 1.0


def mm(a, b):
    return jnp.dot(a, b, precision=HI, preferred_element_type=F32)


def hash_values(ids_row, col, seed):
    h = ids_row * 40503 + col * 9973 + seed * 2654435
    h = h ^ ((h >> 15) & 131071)
    h = h * 73244475
    h = h ^ ((h >> 13) & 524287)
    h = h * 1274126177
    h = h ^ ((h >> 16) & 65535)
    unit = (h & 16777215).astype(F32) * (1.0 / 16777216.0)
    return (unit - 0.5) * 3.4641016


def row_sets(rows):
    if rows == 96:
        return [("Y", 0, 32, 0), ("Z", 32, 16, 0), ("Y", 48, 24, 1), ("Z", 72, 24, 1)]
    q = rows // 4
    return [("Y", 0, q, 0), ("Z", q, q, 0), ("Y", 2 * q, q, 1), ("Z", 3 * q, q, 1)]


def hops(n, orient):
    long, short = n // 2, n - 1 - n // 2
    return (short, long) if orient else (long, short)


class Act:
    def __init__(self, name, run, after=(), deps=(), sends=(), cost=0.15, idle=False, prio=0):
        self.name, self.run, self.after, self.deps = name, run, list(after), list(deps)
        self.sends, self.cost, self.idle, self.prio = list(sends), cost, idle, prio


def arrange(acts, now, arrive):
    arrive, free, done, order = dict(arrive), {}, set(), []
    left = list(acts)
    while left:
        ready = []
        for a in left:
            if all(n in done for n in a.after) and all(d in arrive for d in a.deps):
                ready.append((max([now] + [arrive[d] for d in a.deps]), a.prio, len(ready), a))
        work = [r for r in ready if not r[3].idle]
        spare = [r for r in ready if r[3].idle]
        pick = min(work or spare, key=lambda r: r[:3])
        if work and spare:
            s = min(spare, key=lambda r: r[:3])
            if s[0] + 0.6 * s[3].cost <= pick[0]:
                pick = s
        a = pick[3]
        now = pick[0] + a.cost
        for key, link, size, lag in a.sends:
            free[link] = max(free.get(link, 0.0), now) + size
            arrive[key] = free[link] + lag
        done.add(a.name)
        left.remove(a)
        order.append((now, a))
    return order


STEP_TILES = 4


def expand_kernel(map_ref, a_hbm, e_ref, a_ref, m2_ref, sv_ref, ss_ref, a_sem, sv_sem):
    step = pl.program_id(0)
    block_rows = a_ref.shape[0]
    blocks = block_rows // TILE
    c = lax.axis_index("child")
    row = lax.axis_index("row")
    base = row * (e_ref.shape[0] * pl.num_programs(0))

    @pl.when(step == 0)
    def _():
        load = pltpu.make_async_copy(a_hbm, a_ref, a_sem)
        load.start()

        def fill(j, carry):
            at = pl.multiple_of(row * block_rows + j * TILE, TILE)
            both = map_ref[:, pl.ds(at, TILE)]
            m2_ref[pl.ds(j, 1), :] = jnp.where(c == 0, both[0:1, :], both[1:2, :])
            return carry
        lax.fori_loop(0, blocks, fill, 0)
        firsts = base + lax.broadcasted_iota(jnp.int32, (blocks, TILE), 1) * TILE
        below = (m2_ref[:, TILE - 1:TILE] < firsts).astype(jnp.int32)
        counts = jnp.minimum(jnp.sum(below, axis=0, keepdims=True), blocks - 2)
        sv_ref[...] = jnp.broadcast_to(counts, sv_ref.shape)
        to_scalar = pltpu.make_async_copy(sv_ref, ss_ref, sv_sem)
        to_scalar.start()
        to_scalar.wait()
        load.wait()

    for q in range(STEP_TILES):
        t = step * STEP_TILES + q
        b = ss_ref[0, t]
        window = jnp.concatenate([m2_ref[pl.ds(b, 1), :], m2_ref[pl.ds(b + 1, 1), :]], axis=1)
        wanted = lax.broadcasted_iota(jnp.int32, (TILE, 2 * TILE), 0) + (base + t * TILE)
        pick = jnp.where(window == wanted, 1.0, 0.0).astype(jnp.bfloat16)
        src = a_ref[pl.ds(pl.multiple_of(b * TILE, TILE), 2 * TILE), :]
        e_ref[q * TILE:(q + 1) * TILE, :] = jnp.dot(
            pick, src, preferred_element_type=F32).astype(jnp.bfloat16)


def expand_rows(child_block, child_map, leaf_rows):
    block_rows, block_cols = child_block.shape
    bf = jnp.bfloat16
    rows = STEP_TILES * TILE
    return pl.pallas_call(
        expand_kernel,
        grid=(leaf_rows // rows,),
        out_shape=jax.ShapeDtypeStruct((leaf_rows, block_cols), bf),
        in_specs=[pl.BlockSpec(child_map.shape, lambda i: (0, 0)), pl.BlockSpec(memory_space=pl.ANY)],
        out_specs=pl.BlockSpec((rows, block_cols), lambda i: (i, 0)),
        scratch_shapes=[
            pltpu.VMEM((block_rows, block_cols), bf),
            pltpu.VMEM((block_rows // TILE, TILE), jnp.int32), pltpu.VMEM((8, TILE), jnp.int32),
            pltpu.SMEM((8, TILE), jnp.int32),
            pltpu.SemaphoreType.DMA(()), pltpu.SemaphoreType.DMA(()),
        ],
        compiler_params=pltpu.CompilerParams(vmem_limit_bytes=40 << 20),
    )(child_map, child_block)


def fused_kernel(ny, nz, rows, scale, seeds_ref, map_ref, e_hbm, q_ref, f_ref, *refs):
    sets = row_sets(rows)
    nsets = len(sets)
    slots1, slots2 = refs[:nsets], refs[nsets:2 * nsets]
    (st_ref, eo_ref, em_ref, xb_ref, h_ref, r_ref,
     ypad, gloc, gpart, gz, zr, gs, yr, gf, aug_ref, qw_ref,
     e_sem, xs, xr, s1, q1, s2, q2, as_, ar_) = refs[2 * nsets:]

    block_cols = em_ref.shape[2]

    c = lax.axis_index("child")
    k = lax.axis_index("col")
    my_y = k // nz
    my_z = k - my_y * nz
    other = 1 - c

    def at_y(y):
        return {"col": y * nz + my_z}

    def at_z(z):
        return {"col": my_y * nz + z}

    pending = []

    def remote(src, dst, ssem, rsem, dev):
        return pltpu.make_async_remote_copy(
            src_ref=src, dst_ref=dst, send_sem=ssem, recv_sem=rsem,
            device_id=dev, device_id_type=MESH)

    def put(*args):
        cp = remote(*args)
        cp.start()
        pending.append(cp)
        return cp

    def y_of(j):
        return lax.rem(my_y + ny // 2 - j + ny, ny)

    def fetch(side, j):
        half, dst = ((other, eo_ref), (c, em_ref))[side]
        return pltpu.make_async_copy(e_hbm.at[half, y_of(j)], dst.at[j], e_sem.at[side, j])

    for side in range(2):
        for j in range(ny):
            fetch(side, j).start()
    barrier = pltpu.get_barrier_semaphore()
    peers = [{"child": other}]
    peers += [at_y(lax.rem(my_y + j, ny)) for j in range(1, ny)]
    peers += [at_z(lax.rem(my_z + j, nz)) for j in range(1, nz)]
    for dev in peers:
        pl.semaphore_signal(barrier, inc=1, device_id=dev, device_id_type=MESH)

    both_ids = map_ref[:, pl.ds(pl.multiple_of(k * block_cols, TILE), block_cols)]
    ids = jnp.where(c == 0, both_ids[0:1, :], both_ids[1:2, :])

    def draw(i, carry):
        j0 = pl.multiple_of(i * 32, 32)
        t = j0 // K
        col = lax.broadcasted_iota(jnp.int32, (32, block_cols), 0) + (j0 - t * K)
        st_ref[pl.ds(j0, 32), :] = hash_values(ids, col, seeds_ref[t]).astype(jnp.bfloat16)
        return carry
    lax.fori_loop(0, 2 * K // 32, draw, 0)
    ypad[...] = jnp.zeros_like(ypad)

    def sketch(e, h):
        return lax.dot_general(
            e[...], st_ref[h * K:(h + 1) * K, :], (((1,), (1,)), ((), ())),
            preferred_element_type=F32).reshape(nz, rows, K)

    def swap(h, j):
        y = y_of(j)
        return remote(xb_ref.at[h, y], r_ref.at[h, y], xs.at[h, j], xr.at[h, j], {"child": other})

    pl.semaphore_wait(barrier, len(peers))

    def give0(j, carry):
        y = y_of(j)
        fetch(0, j).wait()
        xb_ref[0, y] = sketch(eo_ref.at[j], 0)
        swap(0, j).start()
        return carry
    lax.fori_loop(0, ny, give0, 0)

    def give1(j, carry):
        xb_ref[1, y_of(j)] = sketch(eo_ref.at[j], 1)
        swap(1, j).start()
        return carry
    lax.fori_loop(0, ny, give1, 0)

    def keep(j, carry):
        y = y_of(j)
        fetch(1, j).wait()
        h_ref[0, y] = sketch(em_ref.at[j], 0)
        h_ref[1, y] = sketch(em_ref.at[j], 1)
        return carry
    lax.fori_loop(0, ny, keep, 0)

    acts = []
    arrive = {("x", h, j): 4.5 + 1.7 * (j + 1 + ny * h) for h in range(2) for j in range(ny)}

    def presum(h, j):
        def run():
            swap(h, j).wait_recv()
            y = y_of(j)

            def body(z, carry):
                h_ref[h, y, z] = h_ref[h, y, z] + r_ref[h, y, z]
                return carry
            lax.fori_loop(0, nz, body, 0)
        acts.append(Act(("pre", h, j), run, deps=[("x", h, j)], cost=0.3, prio=h))

    class Ring:
        def __init__(self, tag, axis, n, pos, at, orient, own, own_ix, lead, slot, ssem, rsem, nr):
            self.tag, self.axis, self.n, self.pos, self.at = tag, axis, n, pos, at
            self.hp, self.hm = hops(n, orient)
            self.own, self.own_ix, self.lead = own, own_ix, lead
            self.slot, self.ssem, self.rsem = slot, ssem, rsem
            self.size = lead * nr * K * 4
            self.copies = {}

        def reach(self, sign):
            return self.hp if sign > 0 else self.hm

        def index(self, sign, s):
            return s if sign > 0 else self.hp + s

        def key(self, sign, s):
            return self.tag + (self.index(sign, s),)

        def load_out(self, sign, s):
            link = self.axis + ("+" if sign > 0 else "-")
            return (self.key(sign, s), link, self.size / RATE, BASE + HOP)

        def send(self, sign, s):
            n = self.n
            d = lax.rem(self.pos + sign * (self.reach(sign) - s) + n, n)
            dev = self.at(lax.rem(self.pos + sign + n, n))
            m = self.index(sign, s)
            if s:
                self.copies[m - 1].wait_recv()
                ref, h = self.slot
                own, oix = self.own_ix

                def body(i, carry):
                    ref[h, m - 1, i] = ref[h, m - 1, i] + own[oix(d, i)]
                    return carry
                lax.fori_loop(0, self.lead, body, 0)
                src = ref.at[h, m - 1]
            else:
                src = self.own(d)
            ref, h = self.slot
            self.copies[m] = put(src, ref.at[h, m], self.ssem(m), self.rsem(m), dev)

        def last(self):
            return [(sign, self.reach(sign) - 1) for sign in (1, -1) if self.reach(sign)]

        def finish(self):
            ref, h = self.slot
            own, oix = self.own_ix
            last = [self.index(*e) for e in self.last()]
            for m in last:
                self.copies[m].wait_recv()

            def body(i, carry):
                total = own[oix(self.pos, i)]
                for m in last:
                    total = total + ref[h, m, i]
                own[oix(self.pos, i)] = total
                return carry
            lax.fori_loop(0, self.lead, body, 0)

        def chain(self, before, prio):
            for sign in (1, -1):
                prev = before
                for s in range(1, self.reach(sign)):
                    name = self.tag + (sign, s)
                    acts.append(Act(name, functools.partial(self.send, sign, s), after=[prev],
                                    deps=[self.key(sign, s - 1)], sends=[self.load_out(sign, s)],
                                    prio=prio))
                    prev = name

        def ends(self):
            return [self.key(*e) for e in self.last()]

    def flow(h, i):
        color, r0, nr, orient = sets[i]
        rs = pl.ds(r0, nr)
        sems = (lambda m: s1.at[h, i, m], lambda m: q1.at[h, i, m])
        sems2 = (lambda m: s2.at[h, i, m], lambda m: q2.at[h, i, m])
        t1, t2 = ("f", h, i, 1), ("f", h, i, 2)
        if color == "Y":
            first = Ring(t1, "y", ny, my_y, at_y, orient,
                         lambda d: h_ref.at[h, d, :, rs, :],
                         (h_ref, lambda d, j: (h, d, j, rs, slice(None))), nz, (slots1[i], h), *sems, nr)
            second = Ring(t2, "z", nz, my_z, at_z, orient,
                          lambda d: h_ref.at[h, my_y, pl.ds(d, 1), rs, :],
                          (h_ref, lambda d, j: (h, my_y, d, rs, slice(None))), 1, (slots2[i], h), *sems2, nr)
        else:
            first = Ring(t1, "z", nz, my_z, at_z, orient,
                         lambda d: h_ref.at[h, :, d, rs, :],
                         (h_ref, lambda d, j: (h, j, d, rs, slice(None))), ny, (slots1[i], h), *sems, nr)
            second = Ring(t2, "y", ny, my_y, at_y, orient,
                          lambda d: h_ref.at[h, pl.ds(d, 1), my_z, rs, :],
                          (h_ref, lambda d, j: (h, d, my_z, rs, slice(None))), 1, (slots2[i], h), *sems2, nr)
        prio = 10 * h
        starts = []
        for sign in (1, -1):
            if not first.reach(sign):
                continue
            if color == "Y":
                rel = (sign * first.reach(sign)) % ny
                need = [("pre", h, (ny // 2 - rel) % ny)]
            else:
                need = [("pre", h, j) for j in range(ny)]
            name = t1 + (sign, 0)
            starts.append(name)
            acts.append(Act(name, functools.partial(first.send, sign, 0), after=need,
                            sends=[first.load_out(sign, 0)], cost=0.02,
                            prio=prio + 1 - 0.1 * first.reach(sign)))
        for sign in (1, -1):
            prev = t1 + (sign, 0)
            for s in range(1, first.reach(sign)):
                name = t1 + (sign, s)
                acts.append(Act(name, functools.partial(first.send, sign, s),
                                after=[prev] + [("pre", h, j) for j in range(ny)],
                                deps=[first.key(sign, s - 1)], sends=[first.load_out(sign, s)], prio=prio))
                prev = name

        def middle():
            first.finish()
            for sign in (1, -1):
                if second.reach(sign):
                    second.send(sign, 0)
        mid = t1 + ("mid",)
        acts.append(Act(mid, middle, after=starts + [("pre", h, j) for j in range(ny)], deps=first.ends(),
                        sends=[second.load_out(sg, 0) for sg in (1, -1) if second.reach(sg)], prio=prio))
        second.chain(mid, prio)
        end = t2 + ("end",)

        def finish():
            second.finish()
            ypad[pl.ds(r0, nr), h * K:(h + 1) * K] = h_ref[h, my_y, my_z, r0:r0 + nr, :]
        acts.append(Act(end, finish, after=[mid], deps=second.ends(), prio=prio))
        return end

    def gram_sum(h, ready):
        t = ("g", h)
        off, off2 = nz + ny - 1, 2 * nz + ny - 1
        cps = {}
        piece = gz.shape[2] * K * 4

        def sem(i):
            return as_.at[h, i], ar_.at[h, i]

        def lag(j, n):
            hop = min(j, n - j)
            return BASE + HOP * hop, hop * piece / RATE

        def zlink(j):
            return "z+" if j <= nz // 2 else "z-"

        def a0():
            first_t = jnp.transpose(ypad[:, 0:K])
            gloc[h] = mm(first_t, ypad[:, h * K:(h + 1) * K]).reshape(gloc.shape[1:])
            cps["p"] = put(gloc.at[h, other], gpart.at[h], *sem(0), {"child": other})

        def a1():
            cps["p"].wait_recv()
            gz[h] = (gloc[h, c] + gpart[h]).reshape(gz.shape[1:])
            for j in zorder:
                z = lax.rem(my_z + j, nz)
                cps["z", j] = put(gz.at[h, z], zr.at[h, j - 1], *sem(j), at_z(z))

        def a2():
            total = gz[h, my_z]
            for j in zorder[::-1]:
                cps["z", j].wait_recv()
                total = total + zr[h, j - 1]
            gs[h] = total
            for j in range(1, ny):
                y = lax.rem(my_y + j, ny)
                cps["y", j] = put(gs.at[h], yr.at[h, j - 1], *sem(nz + j - 1), at_y(y))

        def a3():
            total = gs[h]
            for j in range(1, ny):
                cps["y", j].wait_recv()
                total = total + yr[h, j - 1]
            gf[h, c, my_z] = total
            for j in zorder:
                z = lax.rem(my_z + j, nz)
                cps["w", j] = put(gf.at[h, c, my_z], gf.at[h, c, my_z], *sem(off + j), at_z(z))
            cps["v", 0] = put(gf.at[h, c, my_z], gf.at[h, c, my_z], *sem(off2), {"child": other})

        def a4(j):
            cps["w", j].wait_recv()
            z = lax.rem(my_z - j + nz, nz)
            cps["v", j] = put(gf.at[h, c, z], gf.at[h, c, z], *sem(off2 + j), {"child": other})

        def a5():
            for j in range(nz):
                cps["v", j].wait_recv()

        zorder = sorted(range(1, nz), key=lambda j: -min(j, nz - j))
        acts.append(Act(t + (0,), a0, after=ready, sends=[(t + ("p",), "c", 0.3, 1.0)], cost=1.2, prio=5))
        acts.append(Act(t + (1,), a1, after=[t + (0,)], deps=[t + ("p",)], prio=5,
                        sends=[(t + ("z", j), zlink(j), lag(j, nz)[1], lag(j, nz)[0]) for j in zorder]))
        acts.append(Act(t + (2,), a2, after=[t + (1,)], deps=[t + ("z", j) for j in zorder], prio=5,
                        sends=[(t + ("y", j), "y+" if j <= ny // 2 else "y-", lag(j, ny)[1], lag(j, ny)[0])
                               for j in range(1, ny)]))
        acts.append(Act(t + (3,), a3, after=[t + (2,)], deps=[t + ("y", j) for j in range(1, ny)], prio=5,
                        sends=[(t + ("w", j), zlink(j), lag(j, nz)[1], lag(j, nz)[0]) for j in zorder]
                        + [(t + ("v", 0), "c", 0.1, 1.0)]))
        for j in range(1, nz):
            acts.append(Act(t + (4, j), functools.partial(a4, j), after=[t + (3,)], deps=[t + ("w", j)],
                            sends=[(t + ("v", j), "c", 0.1, 1.0)], cost=0.03, prio=5))
        acts.append(Act(t + (5,), a5, after=[t + (4, j) for j in range(1, nz)],
                        deps=[t + ("v", j) for j in range(nz)], cost=0.02, prio=6))
        return t + (5,)

    sub = lax.broadcasted_iota(jnp.int32, (BLK, BLK), 0)
    lane = lax.broadcasted_iota(jnp.int32, (BLK, BLK), 1)

    def chol_begin():
        aug_ref[:, 0:K] = gf[0].reshape(K, K) * scale
        big = lax.broadcasted_iota(jnp.int32, (K, K), 0) == lax.broadcasted_iota(jnp.int32, (K, K), 1)
        aug_ref[:, K:2 * K] = jnp.where(big, 1.0, 0.0)

    def chol_block(b):
        lo, hi = b * BLK, (b + 1) * BLK
        d = jnp.concatenate([aug_ref[lo:hi, lo:hi], jnp.where(sub == lane, 1.0, 0.0)], axis=1)
        for j in range(BLK):
            one = d[j:j + 1, :]
            factor = d[:, j:j + 1] * (1.0 / one[:, j:j + 1])
            factor = jnp.where(sub[:, 0:1] > j, factor, 0.0)
            d = d - factor * one
        pivots = jnp.sum(jnp.where(sub == lane, d[:, 0:BLK], 0.0), axis=1, keepdims=True)
        inv = d[:, BLK:2 * BLK] * (1.0 / jnp.sqrt(pivots))
        z = mm(inv, aug_ref[lo:hi, :])
        aug_ref[lo:hi, :] = z
        if hi < K:
            base = hi // TILE * TILE
            u = jnp.transpose(aug_ref[lo:hi, base:K])[hi - base:, :]
            aug_ref[hi:K, :] = aug_ref[hi:K, :] - mm(u, z)

    def basis():
        w = aug_ref[:, K:2 * K]
        q = lax.dot_general(ypad[:, 0:K], w, (((1,), (1,)), ((), ())), precision=HI,
                            preferred_element_type=F32)
        q_ref[...] = q[0:rows, :]
        qw_ref[...] = mm(q, w) * scale

    def fresh():
        fit = mm(qw_ref[...], gf[1].reshape(K, K))
        f_ref[...] = ypad[0:rows, K:2 * K] - fit[0:rows, :]

    for h in range(2):
        for j in range(ny):
            presum(h, j)
    ends = [[flow(h, i) for i in range(nsets)] for h in range(2)]
    g1 = gram_sum(0, ends[0])
    g2 = gram_sum(1, ends[0] + ends[1])
    acts.append(Act("chol", chol_begin, after=[g1], cost=0.3, idle=True))
    prev = "chol"
    for b in range(K // BLK):
        acts.append(Act(("chol", b), functools.partial(chol_block, b), after=[prev], cost=1.8, idle=True))
        prev = ("chol", b)
    acts.append(Act("basis", basis, after=[prev], cost=1.5, idle=True))
    acts.append(Act("fresh", fresh, after=["basis", g2], cost=1.0))
    for _, act in arrange(acts, 9.0, arrive):
        act.run()
    for h in range(2):
        for j in range(ny):
            swap(h, j).wait_send()
    for cp in pending:
        cp.wait_send()


def fused(expanded, child_map, seeds, ny, nz, rows, leaf_rows):
    sets = row_sets(rows)
    block_cols = expanded.shape[1]
    vm = pltpu.VMEM
    bf = jnp.bfloat16
    slots1 = [vm((2, (ny if s[0] == "Y" else nz) - 1, nz if s[0] == "Y" else ny, s[2], K), F32) for s in sets]
    slots2 = [vm((2, (nz if s[0] == "Y" else ny) - 1, 1, s[2], K), F32) for s in sets]
    dma = pltpu.SemaphoreType.DMA
    most = max(ny, nz) - 1
    piece = K // 2 // nz
    n_ar = 3 * nz + ny - 1
    chunk = nz * rows
    out = jax.ShapeDtypeStruct((rows, K), F32)
    return pl.pallas_call(
        functools.partial(fused_kernel, ny, nz, rows, 1.0 / leaf_rows),
        out_shape=(out, out),
        in_specs=[
            pl.BlockSpec(memory_space=pltpu.SMEM),
            pl.BlockSpec(memory_space=pltpu.VMEM),
            pl.BlockSpec(memory_space=pl.ANY),
        ],
        out_specs=[pl.BlockSpec(memory_space=pltpu.VMEM)] * 2,
        scratch_shapes=[
            *slots1, *slots2,
            vm((2 * K, block_cols), bf),
            vm((ny, chunk, block_cols), bf), vm((ny, chunk, block_cols), bf),
            vm((2, ny, nz, rows, K), F32), vm((2, ny, nz, rows, K), F32), vm((2, ny, nz, rows, K), F32),
            vm((TILE, 2 * K), F32), vm((2, 2, K // 2, K), F32), vm((2, K // 2, K), F32),
            vm((2, nz, piece, K), F32), vm((2, nz - 1, piece, K), F32), vm((2, piece, K), F32),
            vm((2, ny - 1, piece, K), F32), vm((2, 2, nz, piece, K), F32),
            vm((K, 2 * K), F32), vm((TILE, K), F32),
            dma((2, ny)), dma((2, ny)), dma((2, ny)),
            dma((2, 4, most)), dma((2, 4, most)), dma((2, 4, most)), dma((2, 4, most)),
            dma((2, n_ar)), dma((2, n_ar)),
        ],
        compiler_params=pltpu.CompilerParams(
            collective_id=0, has_side_effects=True, vmem_limit_bytes=56 << 20),
    )(seeds, child_map, expanded.reshape(2, ny, chunk, block_cols))


def make_body(parent_rows):
    def body(schur_blocks, child_map, round_seeds):
        col_count = lax.axis_size("col")
        ny, nz = GRIDS[col_count]
        leaf_rows = parent_rows // lax.axis_size("row")
        own_rows = leaf_rows // (2 * col_count)
        expanded = expand_rows(schur_blocks[0], child_map, leaf_rows)
        return fused(expanded, child_map, round_seeds, ny, nz, own_rows, leaf_rows)
    return body


def solution(mesh, parent_rows=24576):
    placed = (P("child", "row", "col"), P(), P())
    return jax.shard_map(
        make_body(parent_rows),
        mesh=mesh,
        in_specs=placed,
        out_specs=(P(("row", "child", "col"), None), P(("row", "child", "col"), None)),
        check_vma=False,
    )
```

```python
import functools
import jax
import jax.numpy as jnp
from jax import lax
from jax.experimental import pallas as pl
from jax.experimental.pallas import tpu as pltpu
from jax.sharding import PartitionSpec as P

K = 256
TILE = 128
BLK = 32
GRIDS = {32: (4, 8), 8: (2, 4)}
MESH = pl.DeviceIdType.MESH
HI = lax.Precision.HIGHEST
F32 = jnp.float32
RATE = 46.0e3
HOP = 0.8
BASE = 1.4
FAR = 0.15
SETS96 = [("Y", 0, 24, 0), ("Z", 24, 16, 0), ("Y", 40, 24, 1), ("Z", 64, 16, 1), ("Y", 80, 8, 0), ("Z", 88, 8, 1)]


def gate(i, sets):
    return [(i, 1, 'mid')]


def mm(a, b):
    return jnp.dot(a, b, precision=HI, preferred_element_type=F32)


def hash_values(ids_row, col, seed):
    h = ids_row * 40503 + col * 9973 + seed * 2654435
    h = h ^ ((h >> 15) & 131071)
    h = h * 73244475
    h = h ^ ((h >> 13) & 524287)
    h = h * 1274126177
    h = h ^ ((h >> 16) & 65535)
    unit = (h & 16777215).astype(F32) * (1.0 / 16777216.0)
    return (unit - 0.5) * 3.4641016


def row_sets(rows):
    if rows == 96:
        return SETS96
    q = rows // 4
    return [("Y", 0, q, 0), ("Z", q, q, 0), ("Y", 2 * q, q, 1), ("Z", 3 * q, q, 1)]


def hops(n, orient):
    long, short = n // 2, n - 1 - n // 2
    return (short, long) if orient else (long, short)


class Act:
    def __init__(self, name, run, after=(), deps=(), sends=(), cost=0.25, idle=False, prio=0):
        self.name, self.run, self.after, self.deps = name, run, list(after), list(deps)
        self.sends, self.cost, self.idle, self.prio = list(sends), cost, idle, prio


def arrange(acts, now, arrive):
    arrive, free, done, order = dict(arrive), {}, set(), []
    left = list(acts)
    while left:
        ready = []
        for a in left:
            if all(n in done for n in a.after) and all(d in arrive for d in a.deps):
                ready.append((max([now] + [arrive[d] for d in a.deps]), a.prio, len(ready), a))
        work = [r for r in ready if not r[3].idle]
        spare = [r for r in ready if r[3].idle]
        pick = min(work or spare, key=lambda r: r[:3])
        if work and spare:
            s = min(spare, key=lambda r: r[:3])
            if s[0] + 0.6 * s[3].cost <= pick[0]:
                pick = s
        a = pick[3]
        now = pick[0] + a.cost
        for key, link, size, lag in a.sends:
            free[link] = max(free.get(link, 0.0), now) + size
            arrive[key] = free[link] + lag
        done.add(a.name)
        left.remove(a)
        order.append((now, a))
    return order


STEP_TILES = 4


def expand_kernel(map_ref, a_hbm, e_ref, a_ref, m2_ref, sv_ref, ss_ref, a_sem, sv_sem):
    step = pl.program_id(0)
    block_rows = a_ref.shape[0]
    blocks = block_rows // TILE
    c = lax.axis_index("child")
    row = lax.axis_index("row")
    base = row * (e_ref.shape[0] * pl.num_programs(0))

    @pl.when(step == 0)
    def _():
        load = pltpu.make_async_copy(a_hbm, a_ref, a_sem)
        load.start()

        def fill(j, carry):
            at = pl.multiple_of(row * block_rows + j * TILE, TILE)
            both = map_ref[:, pl.ds(at, TILE)]
            m2_ref[pl.ds(j, 1), :] = jnp.where(c == 0, both[0:1, :], both[1:2, :])
            return carry
        lax.fori_loop(0, blocks, fill, 0)
        firsts = base + lax.broadcasted_iota(jnp.int32, (blocks, TILE), 1) * TILE
        below = (m2_ref[:, TILE - 1:TILE] < firsts).astype(jnp.int32)
        counts = jnp.minimum(jnp.sum(below, axis=0, keepdims=True), blocks - 2)
        sv_ref[...] = jnp.broadcast_to(counts, sv_ref.shape)
        to_scalar = pltpu.make_async_copy(sv_ref, ss_ref, sv_sem)
        to_scalar.start()
        to_scalar.wait()
        load.wait()

    for q in range(STEP_TILES):
        t = step * STEP_TILES + q
        b = ss_ref[0, t]
        window = jnp.concatenate([m2_ref[pl.ds(b, 1), :], m2_ref[pl.ds(b + 1, 1), :]], axis=1)
        wanted = lax.broadcasted_iota(jnp.int32, (TILE, 2 * TILE), 0) + (base + t * TILE)
        pick = jnp.where(window == wanted, 1.0, 0.0).astype(jnp.bfloat16)
        src = a_ref[pl.ds(pl.multiple_of(b * TILE, TILE), 2 * TILE), :]
        e_ref[q * TILE:(q + 1) * TILE, :] = jnp.dot(
            pick, src, preferred_element_type=F32).astype(jnp.bfloat16)


def expand_rows(child_block, child_map, leaf_rows):
    block_rows, block_cols = child_block.shape
    bf = jnp.bfloat16
    rows = STEP_TILES * TILE
    return pl.pallas_call(
        expand_kernel,
        grid=(leaf_rows // rows,),
        out_shape=jax.ShapeDtypeStruct((leaf_rows, block_cols), bf),
        in_specs=[pl.BlockSpec(child_map.shape, lambda i: (0, 0)), pl.BlockSpec(memory_space=pl.ANY)],
        out_specs=pl.BlockSpec((rows, block_cols), lambda i: (i, 0)),
        scratch_shapes=[
            pltpu.VMEM((block_rows, block_cols), bf),
            pltpu.VMEM((block_rows // TILE, TILE), jnp.int32), pltpu.VMEM((8, TILE), jnp.int32),
            pltpu.SMEM((8, TILE), jnp.int32),
            pltpu.SemaphoreType.DMA(()), pltpu.SemaphoreType.DMA(()),
        ],
        compiler_params=pltpu.CompilerParams(vmem_limit_bytes=63 << 20),
    )(child_map, child_block)


def fused_kernel(ny, nz, rows, scale, seeds_ref, map_ref, e_hbm, q_ref, f_ref, *refs):
    sets = row_sets(rows)
    nsets = len(sets)
    slots1, slots2 = refs[:nsets], refs[nsets:2 * nsets]
    (st_ref, eo_ref, em_ref, xb_ref, h_ref, r_ref,
     ypad, gloc, gpart, gz, zr, gs, yr, gf, aug_ref, qw_ref,
     e_sem, xs, xr, s1, q1, s2, q2, as_, ar_) = refs[2 * nsets:]

    block_cols = em_ref.shape[2]

    c = lax.axis_index("child")
    k = lax.axis_index("col")
    my_y = k // nz
    my_z = k - my_y * nz
    other = 1 - c

    def at_y(y):
        return {"col": y * nz + my_z}

    def at_z(z):
        return {"col": my_y * nz + z}

    pending = []

    def remote(src, dst, ssem, rsem, dev):
        return pltpu.make_async_remote_copy(
            src_ref=src, dst_ref=dst, send_sem=ssem, recv_sem=rsem,
            device_id=dev, device_id_type=MESH)

    def put(*args):
        cp = remote(*args)
        cp.start()
        pending.append(cp)
        return cp

    def y_of(j):
        return lax.rem(my_y + ny // 2 - j + ny, ny)

    def fetch(side, j):
        half, dst = ((other, eo_ref), (c, em_ref))[side]
        return pltpu.make_async_copy(e_hbm.at[half, y_of(j)], dst.at[j], e_sem.at[side, j])

    for side in range(2):
        for j in range(ny):
            fetch(side, j).start()
    barrier = pltpu.get_barrier_semaphore()
    peers = [{"child": other}]
    peers += [at_y(lax.rem(my_y + j, ny)) for j in range(1, ny)]
    peers += [at_z(lax.rem(my_z + j, nz)) for j in range(1, nz)]
    for dev in peers:
        pl.semaphore_signal(barrier, inc=1, device_id=dev, device_id_type=MESH)

    both_ids = map_ref[:, pl.ds(pl.multiple_of(k * block_cols, TILE), block_cols)]
    ids = jnp.where(c == 0, both_ids[0:1, :], both_ids[1:2, :])

    def draw(i, carry):
        j0 = pl.multiple_of(i * 32, 32)
        t = j0 // K
        col = lax.broadcasted_iota(jnp.int32, (32, block_cols), 0) + (j0 - t * K)
        st_ref[pl.ds(j0, 32), :] = hash_values(ids, col, seeds_ref[t]).astype(jnp.bfloat16)
        return carry
    lax.fori_loop(0, 2 * K // 32, draw, 0)
    ypad[...] = jnp.zeros_like(ypad)

    def sketch(e, h):
        return lax.dot_general(
            e[...], st_ref[h * K:(h + 1) * K, :], (((1,), (1,)), ((), ())),
            preferred_element_type=F32).reshape(nz, rows, K)

    def swap(h, j):
        y = y_of(j)
        return remote(xb_ref.at[h, y], r_ref.at[h, y], xs.at[h, j], xr.at[h, j], {"child": other})

    pl.semaphore_wait(barrier, len(peers))

    def give0(j, carry):
        y = y_of(j)
        fetch(0, j).wait()
        xb_ref[0, y] = sketch(eo_ref.at[j], 0)
        swap(0, j).start()
        return carry
    lax.fori_loop(0, ny, give0, 0)

    def give1():
        def body(j, carry):
            xb_ref[1, y_of(j)] = sketch(eo_ref.at[j], 1)
            swap(1, j).start()
            return carry
        lax.fori_loop(0, ny, body, 0)

    def keep(h):
        def body(j, carry):
            if h == 0:
                fetch(1, j).wait()
            h_ref[h, y_of(j)] = sketch(em_ref.at[j], h)
            return carry
        lax.fori_loop(0, ny, body, 0)

    acts = []
    arrive = {("x", 0, j): 7.0 + 1.4 * j for j in range(ny)}
    acts.append(Act("keep0", functools.partial(keep, 0), cost=2.0, prio=-2))
    acts.append(Act("give1", give1, after=["keep0"], cost=2.0, prio=0.5,
                    sends=[(("x", 1, j), "c", 1.4, 0.5) for j in range(ny)]))
    acts.append(Act("keep1", functools.partial(keep, 1), after=["give1"], cost=2.0, prio=0.6))

    def presum(h, j):
        def run():
            swap(h, j).wait_recv()
            y = y_of(j)

            def body(z, carry):
                h_ref[h, y, z] = h_ref[h, y, z] + r_ref[h, y, z]
                return carry
            lax.fori_loop(0, nz, body, 0)
        acts.append(Act(("pre", h, j), run, after=["keep%d" % h], deps=[("x", h, j)], cost=0.4, prio=h))

    class Ring:
        def __init__(self, tag, axis, n, pos, at, orient, own, own_ix, lead, slot, ssem, rsem, nr):
            self.tag, self.axis, self.n, self.pos, self.at = tag, axis, n, pos, at
            self.hp, self.hm = hops(n, orient)
            self.own, self.own_ix, self.lead = own, own_ix, lead
            self.slot, self.ssem, self.rsem = slot, ssem, rsem
            self.size = lead * nr * K * 4
            self.copies = {}

        def cost(self):
            return 0.06 + 1.6e-3 * self.size / 4096

        def reach(self, sign):
            return self.hp if sign > 0 else self.hm

        def index(self, sign, s):
            return s if sign > 0 else self.hp + s

        def key(self, sign, s):
            return self.tag + (self.index(sign, s),)

        def load_out(self, sign, s):
            link = self.axis + ("+" if sign > 0 else "-")
            return (self.key(sign, s), link, self.size / RATE, BASE + HOP)

        def send(self, sign, s):
            n = self.n
            d = lax.rem(self.pos + sign * (self.reach(sign) - s) + n, n)
            dev = self.at(lax.rem(self.pos + sign + n, n))
            m = self.index(sign, s)
            if s:
                self.copies[m - 1].wait_recv()
                ref, h = self.slot
                own, oix = self.own_ix

                def body(i, carry):
                    ref[h, m - 1, i] = ref[h, m - 1, i] + own[oix(d, i)]
                    return carry
                lax.fori_loop(0, self.lead, body, 0)
                src = ref.at[h, m - 1]
            else:
                src = self.own(d)
            ref, h = self.slot
            self.copies[m] = put(src, ref.at[h, m], self.ssem(m), self.rsem(m), dev)

        def last(self):
            return [(sign, self.reach(sign) - 1) for sign in (1, -1) if self.reach(sign)]

        def finish(self):
            ref, h = self.slot
            own, oix = self.own_ix
            last = self.last_slots()
            for m in last:
                self.copies[m].wait_recv()

            def body(i, carry):
                total = own[oix(self.pos, i)]
                for m in last:
                    total = total + ref[h, m, i]
                own[oix(self.pos, i)] = total
                return carry
            lax.fori_loop(0, self.lead, body, 0)

        def chain(self, before, prio):
            for sign in (1, -1):
                prev = before
                for s in range(1, self.reach(sign)):
                    name = self.tag + (sign, s)
                    acts.append(Act(name, functools.partial(self.send, sign, s), after=[prev],
                                    deps=[self.key(sign, s - 1)], sends=[self.load_out(sign, s)],
                                    cost=self.cost(), prio=prio))
                    prev = name

        def ends(self):
            return [self.tag + (m,) for m in self.last_slots()]

        def start(self):
            for sign in (1, -1):
                if self.reach(sign):
                    self.send(sign, 0)

        def first_sends(self):
            return [self.load_out(sg, 0) for sg in (1, -1) if self.reach(sg)]

        def more(self, before, prio):
            self.chain(before, prio)
            return [before]

        def last_slots(self):
            return [self.index(*e) for e in self.last()]

    class Direct(Ring):
        def start(self):
            ref, h = self.slot
            for j in range(1, self.n):
                d = lax.rem(self.pos + j, self.n)
                self.copies[j - 1] = put(self.own(d), ref.at[h, j - 1], self.ssem(j - 1), self.rsem(j - 1),
                                         self.at(d))

        def first_sends(self):
            out = []
            for j in range(1, self.n):
                hop = min(j, self.n - j)
                link = self.axis + ("+" if j <= self.n // 2 else "-")
                out.append((self.tag + (j - 1,), link, hop * self.size / RATE, BASE + HOP + FAR * (hop - 1)))
            return out

        def more(self, before, prio):
            return [before]

        def last_slots(self):
            return list(range(self.n - 1))

    class Tree(Direct):
        FIRST = ((0, 2, 4), (1, 1, 3), (2, 1, 1), (3, -1, -3), (4, -1, -1))
        SECOND = ((5, 2, (0, 1)), (6, -2, (3,)))

        def sign(self):
            return 1 if self.hp >= self.hm else -1

        def go(self, m, off, src):
            ref, h = self.slot
            dev = lax.rem(self.pos + self.sign() * off + self.n, self.n)
            self.copies[m] = put(src, ref.at[h, m], self.ssem(m), self.rsem(m), self.at(dev))

        def sim(self, m, off):
            link = self.axis + ("+" if off * self.sign() > 0 else "-")
            hop = abs(off)
            return (self.tag + (m,), link, hop * self.size / RATE, BASE + HOP + FAR * (hop - 1))

        def start(self):
            for m, off, piece in self.FIRST:
                d = lax.rem(self.pos + self.sign() * piece + self.n, self.n)
                self.go(m, off, self.own(d))

        def first_sends(self):
            return [self.sim(m, off) for m, off, _ in self.FIRST]

        def second(self, m, off, got):
            ref, h = self.slot
            own, oix = self.own_ix
            d = lax.rem(self.pos + self.sign() * off + self.n, self.n)
            total = own[oix(d, 0)]
            for g in got:
                self.copies[g].wait_recv()
                total = total + ref[h, g, 0]
            ref[h, got[0], 0] = total
            self.go(m, off, ref.at[h, got[0]])

        def more(self, before, prio):
            names = [before]
            for m, off, got in self.SECOND:
                name = self.tag + ("second", m)
                acts.append(Act(name, functools.partial(self.second, m, off, got), after=[before],
                                deps=[self.tag + (g,) for g in got], sends=[self.sim(m, off)],
                                cost=0.08, prio=prio))
                names.append(name)
            return names

        def last_slots(self):
            return [2, 4, 5, 6]

    def flow(h, i):
        color, r0, nr, orient = sets[i]
        rs = pl.ds(r0, nr)
        sems = (lambda m: s1.at[h, i, m], lambda m: q1.at[h, i, m])
        sems2 = (lambda m: s2.at[h, i, m], lambda m: q2.at[h, i, m])
        t1, t2 = ("f", h, i, 1), ("f", h, i, 2)
        if color == "Y":
            first = Ring(t1, "y", ny, my_y, at_y, orient,
                         lambda d: h_ref.at[h, d, :, rs, :],
                         (h_ref, lambda d, j: (h, d, j, rs, slice(None))), nz, (slots1[i], h), *sems, nr)
            second = (Tree if nz == 8 else Ring)(t2, "z", nz, my_z, at_z, orient,
                          lambda d: h_ref.at[h, my_y, pl.ds(d, 1), rs, :],
                          (h_ref, lambda d, j: (h, my_y, d, rs, slice(None))), 1, (slots2[i], h), *sems2, nr)
        else:
            first = Ring(t1, "z", nz, my_z, at_z, orient,
                         lambda d: h_ref.at[h, :, d, rs, :],
                         (h_ref, lambda d, j: (h, j, d, rs, slice(None))), ny, (slots1[i], h), *sems, nr)
            second = Direct(t2, "y", ny, my_y, at_y, orient,
                          lambda d: h_ref.at[h, pl.ds(d, 1), my_z, rs, :],
                          (h_ref, lambda d, j: (h, d, my_z, rs, slice(None))), 1, (slots2[i], h), *sems2, nr)
        prio = 10 * h
        starts = []
        for sign in (1, -1):
            if not first.reach(sign):
                continue
            if color == "Y":
                rel = (sign * first.reach(sign)) % ny
                need = [("pre", h, (ny // 2 - rel) % ny)]
            else:
                need = [("pre", h, j) for j in range(ny)]
            if h:
                need = need + [("f", 0) + g for g in gate(i, sets)]
            name = t1 + (sign, 0)
            starts.append(name)
            acts.append(Act(name, functools.partial(first.send, sign, 0), after=need,
                            sends=[first.load_out(sign, 0)], cost=0.03,
                            prio=prio + 1 - 0.1 * first.reach(sign)))
        for sign in (1, -1):
            prev = t1 + (sign, 0)
            for s in range(1, first.reach(sign)):
                name = t1 + (sign, s)
                acts.append(Act(name, functools.partial(first.send, sign, s),
                                after=[prev] + [("pre", h, j) for j in range(ny)],
                                deps=[first.key(sign, s - 1)], sends=[first.load_out(sign, s)],
                                cost=first.cost(), prio=prio))
                prev = name

        def middle():
            first.finish()
            second.start()
        mid = t1 + ("mid",)
        acts.append(Act(mid, middle, after=starts + [("pre", h, j) for j in range(ny)], deps=first.ends(),
                        sends=second.first_sends(), cost=0.06 + first.cost(), prio=prio))
        before = second.more(mid, prio)
        end = t2 + ("end",)

        def finish():
            second.finish()
            ypad[pl.ds(r0, nr), h * K:(h + 1) * K] = h_ref[h, my_y, my_z, r0:r0 + nr, :]
        acts.append(Act(end, finish, after=before, deps=second.ends(), cost=0.1, prio=prio))
        return end

    def gram_sum(h, ready):
        t = ("g", h)
        off, off2 = nz + ny - 1, 2 * nz + ny - 1
        cps = {}
        piece = gz.shape[2] * K * 4

        def sem(i):
            return as_.at[h, i], ar_.at[h, i]

        def lag(j, n):
            hop = min(j, n - j)
            return BASE + HOP + FAR * (hop - 1), hop * piece / RATE

        def zlink(j):
            return "z+" if j <= nz // 2 else "z-"

        def a0():
            first_t = jnp.transpose(ypad[:, 0:K])
            gloc[h] = mm(first_t, ypad[:, h * K:(h + 1) * K]).reshape(gloc.shape[1:])
            cps["p"] = put(gloc.at[h, other], gpart.at[h], *sem(0), {"child": other})

        def a1():
            cps["p"].wait_recv()
            gz[h] = (gloc[h, c] + gpart[h]).reshape(gz.shape[1:])
            for j in zorder:
                z = lax.rem(my_z + j, nz)
                cps["z", j] = put(gz.at[h, z], zr.at[h, j - 1], *sem(j), at_z(z))

        def a2():
            total = gz[h, my_z]
            for j in zorder[::-1]:
                cps["z", j].wait_recv()
                total = total + zr[h, j - 1]
            gs[h] = total
            for j in range(1, ny):
                y = lax.rem(my_y + j, ny)
                cps["y", j] = put(gs.at[h], yr.at[h, j - 1], *sem(nz + j - 1), at_y(y))

        def a3():
            total = gs[h]
            for j in range(1, ny):
                cps["y", j].wait_recv()
                total = total + yr[h, j - 1]
            gf[h, c, my_z] = total
            for j in zorder:
                z = lax.rem(my_z + j, nz)
                cps["w", j] = put(gf.at[h, c, my_z], gf.at[h, c, my_z], *sem(off + j), at_z(z))
            cps["v", 0] = put(gf.at[h, c, my_z], gf.at[h, c, my_z], *sem(off2), {"child": other})

        def a4(j):
            cps["w", j].wait_recv()
            z = lax.rem(my_z - j + nz, nz)
            cps["v", j] = put(gf.at[h, c, z], gf.at[h, c, z], *sem(off2 + j), {"child": other})

        def a5():
            for j in range(nz):
                cps["v", j].wait_recv()

        zorder = sorted(range(1, nz), key=lambda j: -min(j, nz - j))
        acts.append(Act(t + (0,), a0, after=ready, sends=[(t + ("p",), "c", 0.3, 1.0)], cost=1.8, prio=5))
        acts.append(Act(t + (1,), a1, after=[t + (0,)], deps=[t + ("p",)], prio=5,
                        sends=[(t + ("z", j), zlink(j), lag(j, nz)[1], lag(j, nz)[0]) for j in zorder]))
        acts.append(Act(t + (2,), a2, after=[t + (1,)], deps=[t + ("z", j) for j in zorder], prio=5,
                        sends=[(t + ("y", j), "y+" if j <= ny // 2 else "y-", lag(j, ny)[1], lag(j, ny)[0])
                               for j in range(1, ny)]))
        acts.append(Act(t + (3,), a3, after=[t + (2,)], deps=[t + ("y", j) for j in range(1, ny)], prio=5,
                        sends=[(t + ("w", j), zlink(j), lag(j, nz)[1], lag(j, nz)[0]) for j in zorder]
                        + [(t + ("v", 0), "c", 0.1, 1.0)]))
        for j in range(1, nz):
            acts.append(Act(t + (4, j), functools.partial(a4, j), after=[t + (3,)], deps=[t + ("w", j)],
                            sends=[(t + ("v", j), "c", 0.1, 1.0)], cost=0.03, prio=5))
        acts.append(Act(t + (5,), a5, after=[t + (4, j) for j in range(1, nz)],
                        deps=[t + ("v", j) for j in range(nz)], cost=0.02, prio=6))
        return t + (5,)

    sub = lax.broadcasted_iota(jnp.int32, (BLK, BLK), 0)
    lane = lax.broadcasted_iota(jnp.int32, (BLK, BLK), 1)

    def chol_begin():
        aug_ref[:, 0:K] = gf[0].reshape(K, K) * scale
        big = lax.broadcasted_iota(jnp.int32, (K, K), 0) == lax.broadcasted_iota(jnp.int32, (K, K), 1)
        aug_ref[:, K:2 * K] = jnp.where(big, 1.0, 0.0)

    def chol_block(b):
        lo, hi = b * BLK, (b + 1) * BLK
        both = jnp.concatenate([aug_ref[lo:hi, lo:hi], jnp.where(sub == lane, 1.0, 0.0)], axis=1)
        d = [both[8 * g:8 * g + 8, :] for g in range(BLK // 8)]
        sub8 = lax.broadcasted_iota(jnp.int32, (8, 2 * BLK), 0)
        lane8 = lax.broadcasted_iota(jnp.int32, (8, 2 * BLK), 1)
        for p in range(0, BLK, 2):
            g0, q = p // 8, p % 8
            row0, row1 = d[g0][q:q + 1, :], d[g0][q + 1:q + 2, :]
            col0 = [jnp.broadcast_to(x[:, p:p + 1], x.shape) for x in d[g0:]]
            col1 = [jnp.broadcast_to(x[:, p + 1:p + 2], x.shape) for x in d[g0:]]
            aa, ab, bb = col0[0][q:q + 1, :], col0[0][q + 1:q + 2, :], col1[0][q + 1:q + 2, :]
            inv_det = 1.0 / (aa * bb - ab * ab)
            mix0 = (bb * inv_det) * row0 - (ab * inv_det) * row1
            mix1 = (aa * inv_det) * row1 - (ab * inv_det) * row0
            for g in range(g0, BLK // 8):
                x0, x1 = col0[g - g0], col1[g - g0]
                if g == g0:
                    if q == 6:
                        continue
                    x0 = jnp.where(sub8 > q + 1, x0, 0.0)
                    x1 = jnp.where(sub8 > q + 1, x1, 0.0)
                d[g] = d[g] - (x0 * mix0 + x1 * mix1)
        out = []
        for g in range(BLK // 8):
            me = sub8 + 8 * g
            diag = jnp.sum(jnp.where(lane8 == me, d[g], 0.0), axis=1, keepdims=True)
            side = jnp.where((lane8 == me - 1) & (sub8 % 2 == 1), d[g], 0.0)
            side = jnp.sum(side, axis=1, keepdims=True)
            wide = jnp.broadcast_to(diag, d[g].shape)
            lift = side / pltpu.roll(wide, 1, 0)
            full = d[g] - lift * pltpu.roll(d[g], 1, 0)
            out.append(full * (1.0 / jnp.sqrt(wide - lift * side)))
        inv = jnp.concatenate(out, axis=0)[:, BLK:2 * BLK]
        left, right = (0, K + TILE) if hi <= TILE else (TILE, 2 * K)
        z = mm(inv, aug_ref[lo:hi, left:right])
        aug_ref[lo:hi, left:right] = z
        if hi < K:
            base = hi // TILE * TILE
            u = jnp.transpose(aug_ref[lo:hi, base:K])[hi - base:, :]
            aug_ref[hi:K, left:right] = aug_ref[hi:K, left:right] - mm(u, z)

    def basis():
        w = aug_ref[:, K:2 * K]
        q = lax.dot_general(ypad[:, 0:K], w, (((1,), (1,)), ((), ())), precision=HI,
                            preferred_element_type=F32)
        q_ref[...] = q[0:rows, :]
        qw_ref[...] = mm(q, w) * scale

    def fresh():
        fit = mm(qw_ref[...], gf[1].reshape(K, K))
        f_ref[...] = ypad[0:rows, K:2 * K] - fit[0:rows, :]

    for h in range(2):
        for j in range(ny):
            presum(h, j)
    ends = [[flow(h, i) for i in range(nsets)] for h in range(2)]
    g1 = gram_sum(0, ends[0])
    g2 = gram_sum(1, ends[0] + ends[1])
    acts.append(Act("chol", chol_begin, after=[g1], cost=0.3, idle=True))
    prev = "chol"
    for b in range(K // BLK):
        acts.append(Act(("chol", b), functools.partial(chol_block, b), after=[prev], cost=1.4, idle=True))
        prev = ("chol", b)
    acts.append(Act("basis", basis, after=[prev], cost=2.0, idle=True))
    acts.append(Act("fresh", fresh, after=["basis", g2], cost=1.2))
    for _, act in arrange(acts, 7.0, arrive):
        act.run()
    for h in range(2):
        for j in range(ny):
            swap(h, j).wait_send()
    for cp in pending:
        cp.wait_send()


def fused(expanded, child_map, seeds, ny, nz, rows, leaf_rows):
    sets = row_sets(rows)
    block_cols = expanded.shape[1]
    vm = pltpu.VMEM
    bf = jnp.bfloat16
    slots1 = [vm((2, max(1, (ny if s[0] == "Y" else nz) - 1), nz if s[0] == "Y" else ny, s[2], K), F32) for s in sets]
    slots2 = [vm((2, max(1, (nz if s[0] == "Y" else ny) - 1), 1, s[2], K), F32) for s in sets]
    dma = pltpu.SemaphoreType.DMA
    most = max(ny, nz) - 1
    piece = K // 2 // nz
    n_ar = 3 * nz + ny - 1
    chunk = nz * rows
    out = jax.ShapeDtypeStruct((rows, K), F32)
    return pl.pallas_call(
        functools.partial(fused_kernel, ny, nz, rows, 1.0 / leaf_rows),
        out_shape=(out, out),
        in_specs=[
            pl.BlockSpec(memory_space=pltpu.SMEM),
            pl.BlockSpec(memory_space=pltpu.VMEM),
            pl.BlockSpec(memory_space=pl.ANY),
        ],
        out_specs=[pl.BlockSpec(memory_space=pltpu.VMEM)] * 2,
        scratch_shapes=[
            *slots1, *slots2,
            vm((2 * K, block_cols), bf),
            vm((ny, chunk, block_cols), bf), vm((ny, chunk, block_cols), bf),
            vm((2, ny, nz, rows, K), F32), vm((2, ny, nz, rows, K), F32), vm((2, ny, nz, rows, K), F32),
            vm((TILE, 2 * K), F32), vm((2, 2, K // 2, K), F32), vm((2, K // 2, K), F32),
            vm((2, nz, piece, K), F32), vm((2, nz - 1, piece, K), F32), vm((2, piece, K), F32),
            vm((2, max(1, ny - 1), piece, K), F32), vm((2, 2, nz, piece, K), F32),
            vm((K, 2 * K), F32), vm((TILE, K), F32),
            dma((2, ny)), dma((2, ny)), dma((2, ny)),
            *[dma((2, len(sets), most))] * 4,
            dma((2, n_ar)), dma((2, n_ar)),
        ],
        compiler_params=pltpu.CompilerParams(
            collective_id=0, has_side_effects=True, vmem_limit_bytes=63 << 20),
    )(seeds, child_map, expanded.reshape(2, ny, chunk, block_cols))


def make_body(parent_rows):
    def body(schur_blocks, child_map, round_seeds):
        col_count = lax.axis_size("col")
        ny, nz = GRIDS[col_count]
        leaf_rows = parent_rows // lax.axis_size("row")
        own_rows = leaf_rows // (2 * col_count)
        expanded = expand_rows(schur_blocks[0], child_map, leaf_rows)
        return fused(expanded, child_map, round_seeds, ny, nz, own_rows, leaf_rows)
    return body


def solution(mesh, parent_rows=24576):
    placed = (P("child", "row", "col"), P(), P())
    return jax.shard_map(
        make_body(parent_rows),
        mesh=mesh,
        in_specs=placed,
        out_specs=(P(("row", "child", "col"), None), P(("row", "child", "col"), None)),
        check_vma=False,
    )
```

```python
import functools
import jax
import jax.numpy as jnp
from jax import lax
from jax.experimental import pallas as pl
from jax.experimental.pallas import tpu as pltpu
from jax.sharding import PartitionSpec as P

K = 256
TILE = 128
BLK = 64
GRIDS = {32: (4, 8), 8: (2, 4)}
MESH = pl.DeviceIdType.MESH
F32 = jnp.float32
RATE = 46.0e3
HOP = 0.8
BASE = 1.4
FAR = 0.15
SETS96 = [("Y", 0, 24, 0), ("Z", 24, 16, 0), ("Y", 40, 24, 1), ("Z", 64, 16, 1), ("Y", 80, 8, 0), ("Z", 88, 8, 1)]


def gate(i, sets):
    return [(i, 1, 'mid')]


def split(x):
    high = x.astype(jnp.bfloat16)
    return high, (x - high.astype(F32)).astype(jnp.bfloat16)


def mm(a, b, dims=(((1,), (0,)), ((), ()))):
    (ah, al), (bh, bl) = split(a), split(b)

    def dot(x, y):
        return lax.dot_general(x, y, dims, preferred_element_type=F32)
    return dot(ah, bh) + (dot(ah, bl) + dot(al, bh))


def hash_values(ids_row, col, seed):
    h = ids_row * 40503 + col * 9973 + seed * 2654435
    h = h ^ ((h >> 15) & 131071)
    h = h * 73244475
    h = h ^ ((h >> 13) & 524287)
    h = h * 1274126177
    h = h ^ ((h >> 16) & 65535)
    unit = (h & 16777215).astype(F32) * (1.0 / 16777216.0)
    return (unit - 0.5) * 3.4641016


def row_sets(rows):
    if rows == 96:
        return SETS96
    q = rows // 4
    return [("Y", 0, q, 0), ("Z", q, q, 0), ("Y", 2 * q, q, 1), ("Z", 3 * q, q, 1)]


def hops(n, orient):
    long, short = n // 2, n - 1 - n // 2
    return (short, long) if orient else (long, short)


class Act:
    def __init__(self, name, run, after=(), deps=(), sends=(), cost=0.25, idle=False, prio=0):
        self.name, self.run, self.after, self.deps = name, run, list(after), list(deps)
        self.sends, self.cost, self.idle, self.prio = list(sends), cost, idle, prio


def arrange(acts, now, arrive):
    arrive, free, done, order = dict(arrive), {}, set(), []
    left = list(acts)
    while left:
        ready = []
        for a in left:
            if all(n in done for n in a.after) and all(d in arrive for d in a.deps):
                ready.append((max([now] + [arrive[d] for d in a.deps]), a.prio, len(ready), a))
        work = [r for r in ready if not r[3].idle]
        spare = [r for r in ready if r[3].idle]
        pick = min(work or spare, key=lambda r: r[:3])
        if work and spare:
            s = min(spare, key=lambda r: r[:3])
            if s[0] + 0.6 * s[3].cost <= pick[0]:
                pick = s
        a = pick[3]
        now = pick[0] + a.cost
        for key, link, size, lag in a.sends:
            free[link] = max(free.get(link, 0.0), now) + size
            arrive[key] = free[link] + lag
        done.add(a.name)
        left.remove(a)
        order.append((now, a))
    return order


STEP_TILES = 4


def expand_kernel(map_ref, a_hbm, e_ref, a_ref, m2_ref, sv_ref, ss_ref, a_sem, sv_sem):
    step = pl.program_id(0)
    block_rows = a_ref.shape[0]
    blocks = block_rows // TILE
    c = lax.axis_index("child")
    row = lax.axis_index("row")
    base = row * (e_ref.shape[0] * pl.num_programs(0))

    @pl.when(step == 0)
    def _():
        load = pltpu.make_async_copy(a_hbm, a_ref, a_sem)
        load.start()

        def fill(j, carry):
            at = pl.multiple_of(row * block_rows + j * TILE, TILE)
            both = map_ref[:, pl.ds(at, TILE)]
            m2_ref[pl.ds(j, 1), :] = jnp.where(c == 0, both[0:1, :], both[1:2, :])
            return carry
        lax.fori_loop(0, blocks, fill, 0)
        firsts = base + lax.broadcasted_iota(jnp.int32, (blocks, TILE), 1) * TILE
        below = (m2_ref[:, TILE - 1:TILE] < firsts).astype(jnp.int32)
        counts = jnp.minimum(jnp.sum(below, axis=0, keepdims=True), blocks - 2)
        sv_ref[...] = jnp.broadcast_to(counts, sv_ref.shape)
        to_scalar = pltpu.make_async_copy(sv_ref, ss_ref, sv_sem)
        to_scalar.start()
        to_scalar.wait()
        load.wait()

    for q in range(STEP_TILES):
        t = step * STEP_TILES + q
        b = ss_ref[0, t]
        window = jnp.concatenate([m2_ref[pl.ds(b, 1), :], m2_ref[pl.ds(b + 1, 1), :]], axis=1)
        wanted = lax.broadcasted_iota(jnp.int32, (TILE, 2 * TILE), 0) + (base + t * TILE)
        pick = jnp.where(window == wanted, 1.0, 0.0).astype(jnp.bfloat16)
        src = a_ref[pl.ds(pl.multiple_of(b * TILE, TILE), 2 * TILE), :]
        e_ref[q * TILE:(q + 1) * TILE, :] = jnp.dot(
            pick, src, preferred_element_type=F32).astype(jnp.bfloat16)


def expand_rows(child_block, child_map, leaf_rows):
    block_rows, block_cols = child_block.shape
    bf = jnp.bfloat16
    rows = STEP_TILES * TILE
    return pl.pallas_call(
        expand_kernel,
        grid=(leaf_rows // rows,),
        out_shape=jax.ShapeDtypeStruct((leaf_rows, block_cols), bf),
        in_specs=[pl.BlockSpec(child_map.shape, lambda i: (0, 0)), pl.BlockSpec(memory_space=pl.ANY)],
        out_specs=pl.BlockSpec((rows, block_cols), lambda i: (i, 0)),
        scratch_shapes=[
            pltpu.VMEM((block_rows, block_cols), bf),
            pltpu.VMEM((block_rows // TILE, TILE), jnp.int32), pltpu.VMEM((8, TILE), jnp.int32),
            pltpu.SMEM((8, TILE), jnp.int32),
            pltpu.SemaphoreType.DMA(()), pltpu.SemaphoreType.DMA(()),
        ],
        compiler_params=pltpu.CompilerParams(vmem_limit_bytes=40 << 20),
    )(child_map, child_block)


def fused_kernel(ny, nz, rows, scale, seeds_ref, map_ref, e_hbm, q_ref, f_ref, *refs):
    sets = row_sets(rows)
    nsets = len(sets)
    slots1, slots2 = refs[:nsets], refs[nsets:2 * nsets]
    got1, got2 = refs[2 * nsets:3 * nsets], refs[3 * nsets:4 * nsets]
    (st_ref, eo_ref, em_ref, xb_ref, h_ref, r_ref,
     ypad, gloc, gpart, gz, zr, gs, yr, gf, aug_ref, qw_ref,
     e_sem, xs, xr, s1, s2, as_, ar_) = refs[4 * nsets:]

    block_cols = em_ref.shape[2]

    c = lax.axis_index("child")
    k = lax.axis_index("col")
    my_y = k // nz
    my_z = k - my_y * nz
    other = 1 - c

    def at_y(y):
        return {"col": y * nz + my_z}

    def at_z(z):
        return {"col": my_y * nz + z}

    sent = []

    def remote(src, dst, ssem, rsem, dev):
        return pltpu.make_async_remote_copy(
            src_ref=src, dst_ref=dst, send_sem=ssem, recv_sem=rsem,
            device_id=dev, device_id_type=MESH)

    def put(*args):
        cp = remote(*args)
        cp.start()
        return cp

    def y_of(j):
        return lax.rem(my_y + ny // 2 - j + ny, ny)

    def fetch(side, j):
        half, dst = ((other, eo_ref), (c, em_ref))[side]
        return pltpu.make_async_copy(e_hbm.at[half, y_of(j)], dst.at[j], e_sem.at[ny if side else j])

    for side in range(2):
        for j in range(ny):
            fetch(side, j).start()
    barrier = pltpu.get_barrier_semaphore()
    peers = [{"child": other}]
    peers += [at_y(lax.rem(my_y + j, ny)) for j in range(1, ny)]
    peers += [at_z(lax.rem(my_z + j, nz)) for j in range(1, nz)]
    for dev in peers:
        pl.semaphore_signal(barrier, inc=1, device_id=dev, device_id_type=MESH)

    both_ids = map_ref[:, pl.ds(pl.multiple_of(k * block_cols, TILE), block_cols)]
    ids = jnp.where(c == 0, both_ids[0:1, :], both_ids[1:2, :])

    def draw(i, carry):
        j0 = pl.multiple_of(i * 32, 32)
        t = j0 // K
        col = lax.broadcasted_iota(jnp.int32, (32, block_cols), 0) + (j0 - t * K)
        st_ref[pl.ds(j0, 32), :] = hash_values(ids, col, seeds_ref[t]).astype(jnp.bfloat16)
        return carry
    lax.fori_loop(0, 2 * K // 32, draw, 0)
    ypad[...] = jnp.zeros_like(ypad)

    def sketch(e, h):
        return lax.dot_general(
            e[...], st_ref[h * K:(h + 1) * K, :], (((1,), (1,)), ((), ())),
            preferred_element_type=F32).reshape(nz, rows, K)

    def swap(h, j):
        y = y_of(j)
        return remote(xb_ref.at[h, y], r_ref.at[h, y], xs.at[0], xr.at[h, j], {"child": other})

    pl.semaphore_wait(barrier, len(peers))

    def give0(j, carry):
        y = y_of(j)
        fetch(0, j).wait()
        xb_ref[0, y] = sketch(eo_ref.at[j], 0)
        swap(0, j).start()
        return carry
    lax.fori_loop(0, ny, give0, 0)

    def give1():
        def body(j, carry):
            xb_ref[1, y_of(j)] = sketch(eo_ref.at[j], 1)
            swap(1, j).start()
            return carry
        lax.fori_loop(0, ny, body, 0)

    def keep(h):
        if h == 0:
            pltpu.make_async_copy(em_ref, em_ref, e_sem.at[ny]).wait()

        def body(j, carry):
            h_ref[h, y_of(j)] = sketch(em_ref.at[j], h)
            return carry
        lax.fori_loop(0, ny, body, 0)

    acts = []
    arrive = {("x", 0, j): 7.0 + 1.4 * j for j in range(ny)}
    acts.append(Act("keep0", functools.partial(keep, 0), cost=2.0, prio=-2))
    acts.append(Act("give1", give1, after=["keep0"], cost=2.0, prio=0.5,
                    sends=[(("x", 1, j), "c", 1.4, 0.5) for j in range(ny)]))
    acts.append(Act("keep1", functools.partial(keep, 1), after=["give1"], cost=2.0, prio=0.6))

    def presum(h, j):
        def run():
            swap(h, j).wait_recv()
            y = y_of(j)

            def body(z, carry):
                h_ref[h, y, z] = h_ref[h, y, z] + r_ref[h, y, z]
                return carry
            lax.fori_loop(0, nz, body, 0)
        acts.append(Act(("pre", h, j), run, after=["keep%d" % h], deps=[("x", h, j)], cost=0.4, prio=h))

    class Ring:
        def __init__(self, tag, axis, n, pos, at, orient, own, own_ix, lead, slot, ssem, rsem, nr):
            self.tag, self.axis, self.n, self.pos, self.at = tag, axis, n, pos, at
            self.hp, self.hm = hops(n, orient)
            self.own, self.own_ix, self.lead = own, own_ix, lead
            self.slot, self.ssem, self.rsem = slot, ssem, rsem
            self.size = lead * nr * K * 4
            self.groups = self.group()

        def group(self):
            last = self.last_slots()
            return [last] + [[m] for m in range(self.n - 1) if m not in last]

        def sem_of(self, m):
            return self.rsem([m in g for g in self.groups].index(True))

        def wait(self, which):
            ref, h = self.slot
            if self.groups[which]:
                span = ref.at[h, pl.ds(0, len(self.groups[which]))]
                remote(span, span, self.ssem, self.rsem(which), {"child": other}).wait_recv()

        def wait_for(self, m):
            self.wait([m in g for g in self.groups].index(True))

        def cost(self):
            return 0.06 + 1.6e-3 * self.size / 4096

        def reach(self, sign):
            return self.hp if sign > 0 else self.hm

        def index(self, sign, s):
            return s if sign > 0 else self.hp + s

        def key(self, sign, s):
            return self.tag + (self.index(sign, s),)

        def load_out(self, sign, s):
            link = self.axis + ("+" if sign > 0 else "-")
            return (self.key(sign, s), link, self.size / RATE, BASE + HOP)

        def send(self, sign, s):
            n = self.n
            d = lax.rem(self.pos + sign * (self.reach(sign) - s) + n, n)
            dev = self.at(lax.rem(self.pos + sign + n, n))
            m = self.index(sign, s)
            if s:
                self.wait_for(m - 1)
                ref, h = self.slot
                own, oix = self.own_ix

                def body(i, carry):
                    ref[h, m - 1, i] = ref[h, m - 1, i] + own[oix(d, i)]
                    return carry
                lax.fori_loop(0, self.lead, body, 0)
                src = ref.at[h, m - 1]
            else:
                src = self.own(d)
            ref, h = self.slot
            put(src, ref.at[h, m], self.ssem, self.sem_of(m), dev)

        def last(self):
            return [(sign, self.reach(sign) - 1) for sign in (1, -1) if self.reach(sign)]

        def finish(self):
            ref, h = self.slot
            own, oix = self.own_ix
            last = self.last_slots()
            self.wait(0)

            def body(i, carry):
                total = own[oix(self.pos, i)]
                for m in last:
                    total = total + ref[h, m, i]
                own[oix(self.pos, i)] = total
                return carry
            lax.fori_loop(0, self.lead, body, 0)

        def chain(self, before, prio):
            for sign in (1, -1):
                prev = before
                for s in range(1, self.reach(sign)):
                    name = self.tag + (sign, s)
                    acts.append(Act(name, functools.partial(self.send, sign, s), after=[prev],
                                    deps=[self.key(sign, s - 1)], sends=[self.load_out(sign, s)],
                                    cost=self.cost(), prio=prio))
                    prev = name

        def ends(self):
            return [self.tag + (m,) for m in self.last_slots()]

        def start(self):
            for sign in (1, -1):
                if self.reach(sign):
                    self.send(sign, 0)

        def first_sends(self):
            return [self.load_out(sg, 0) for sg in (1, -1) if self.reach(sg)]

        def more(self, before, prio):
            self.chain(before, prio)
            return [before]

        def last_slots(self):
            return [self.index(*e) for e in self.last()]

    class Direct(Ring):
        def start(self):
            ref, h = self.slot
            for j in range(1, self.n):
                d = lax.rem(self.pos + j, self.n)
                put(self.own(d), ref.at[h, j - 1], self.ssem, self.sem_of(j - 1), self.at(d))

        def first_sends(self):
            out = []
            for j in range(1, self.n):
                hop = min(j, self.n - j)
                link = self.axis + ("+" if j <= self.n // 2 else "-")
                out.append((self.tag + (j - 1,), link, hop * self.size / RATE, BASE + HOP + FAR * (hop - 1)))
            return out

        def more(self, before, prio):
            return [before]

        def last_slots(self):
            return list(range(self.n - 1))

    class Tree(Direct):
        FIRST = ((0, 2, 4), (1, 1, 3), (2, 1, 1), (3, -1, -3), (4, -1, -1))
        SECOND = ((5, 2, (0, 1)), (6, -2, (3,)))

        def sign(self):
            return 1 if self.hp >= self.hm else -1

        def go(self, m, off, src):
            ref, h = self.slot
            dev = lax.rem(self.pos + self.sign() * off + self.n, self.n)
            put(src, ref.at[h, m], self.ssem, self.sem_of(m), self.at(dev))

        def sim(self, m, off):
            link = self.axis + ("+" if off * self.sign() > 0 else "-")
            hop = abs(off)
            return (self.tag + (m,), link, hop * self.size / RATE, BASE + HOP + FAR * (hop - 1))

        def start(self):
            for m, off, piece in self.FIRST:
                d = lax.rem(self.pos + self.sign() * piece + self.n, self.n)
                self.go(m, off, self.own(d))

        def first_sends(self):
            return [self.sim(m, off) for m, off, _ in self.FIRST]

        def second(self, m, off, got):
            ref, h = self.slot
            own, oix = self.own_ix
            d = lax.rem(self.pos + self.sign() * off + self.n, self.n)
            total = own[oix(d, 0)]
            self.wait_for(got[0])
            for g in got:
                total = total + ref[h, g, 0]
            ref[h, got[0], 0] = total
            self.go(m, off, ref.at[h, got[0]])

        def more(self, before, prio):
            names = [before]
            for m, off, got in self.SECOND:
                name = self.tag + ("second", m)
                acts.append(Act(name, functools.partial(self.second, m, off, got), after=[before],
                                deps=[self.tag + (g,) for g in got], sends=[self.sim(m, off)],
                                cost=0.08, prio=prio))
                names.append(name)
            return names

        def last_slots(self):
            return [2, 4, 5, 6]

        def group(self):
            return [self.last_slots(), [0, 1], [3]]

    def flow(h, i):
        color, r0, nr, orient = sets[i]
        rs = pl.ds(r0, nr)
        sems = (s1.at[i], lambda m: got1[i].at[h, m])
        sems2 = (s2.at[i], lambda m: got2[i].at[h, m])
        t1, t2 = ("f", h, i, 1), ("f", h, i, 2)
        if color == "Y":
            first = Ring(t1, "y", ny, my_y, at_y, orient,
                         lambda d: h_ref.at[h, d, :, rs, :],
                         (h_ref, lambda d, j: (h, d, j, rs, slice(None))), nz, (slots1[i], h), *sems, nr)
            second = (Tree if nz == 8 else Ring)(t2, "z", nz, my_z, at_z, orient,
                          lambda d: h_ref.at[h, my_y, pl.ds(d, 1), rs, :],
                          (h_ref, lambda d, j: (h, my_y, d, rs, slice(None))), 1, (slots2[i], h), *sems2, nr)
        else:
            first = Ring(t1, "z", nz, my_z, at_z, orient,
                         lambda d: h_ref.at[h, :, d, rs, :],
                         (h_ref, lambda d, j: (h, j, d, rs, slice(None))), ny, (slots1[i], h), *sems, nr)
            second = Direct(t2, "y", ny, my_y, at_y, orient,
                          lambda d: h_ref.at[h, pl.ds(d, 1), my_z, rs, :],
                          (h_ref, lambda d, j: (h, d, my_z, rs, slice(None))), 1, (slots2[i], h), *sems2, nr)
        if h:
            sent.extend((ring.ssem, buf) for ring, buf in ((first, slots1[i]), (second, slots2[i])) if ring.n > 1)
        prio = 10 * h
        starts = []
        for sign in (1, -1):
            if not first.reach(sign):
                continue
            if color == "Y":
                rel = (sign * first.reach(sign)) % ny
                need = [("pre", h, (ny // 2 - rel) % ny)]
            else:
                need = [("pre", h, j) for j in range(ny)]
            if h:
                need = need + [("f", 0) + g for g in gate(i, sets)]
            name = t1 + (sign, 0)
            starts.append(name)
            acts.append(Act(name, functools.partial(first.send, sign, 0), after=need,
                            sends=[first.load_out(sign, 0)], cost=0.03,
                            prio=prio + 1 - 0.1 * first.reach(sign)))
        for sign in (1, -1):
            prev = t1 + (sign, 0)
            for s in range(1, first.reach(sign)):
                name = t1 + (sign, s)
                acts.append(Act(name, functools.partial(first.send, sign, s),
                                after=[prev] + [("pre", h, j) for j in range(ny)],
                                deps=[first.key(sign, s - 1)], sends=[first.load_out(sign, s)],
                                cost=first.cost(), prio=prio))
                prev = name

        def middle():
            first.finish()
            second.start()
        mid = t1 + ("mid",)
        acts.append(Act(mid, middle, after=starts + [("pre", h, j) for j in range(ny)], deps=first.ends(),
                        sends=second.first_sends(), cost=0.06 + first.cost(), prio=prio))
        before = second.more(mid, prio)
        end = t2 + ("end",)

        def finish():
            second.finish()
            ypad[pl.ds(r0, nr), h * K:(h + 1) * K] = h_ref[h, my_y, my_z, r0:r0 + nr, :]
        acts.append(Act(end, finish, after=before, deps=second.ends(), cost=0.1, prio=prio))
        return end

    def gram_sum(h, ready):
        t = ("g", h)
        piece = gz.shape[2] * K * 4

        def sem(i):
            return as_.at[h, i], ar_.at[h, i]

        def wait(i, buf):
            remote(buf, buf, *sem(i), {"child": other}).wait_recv()

        def total_of(start, parts, count):
            for j in range(count):
                start = start + parts[h, j]
            return start

        def lag(j, n):
            hop = min(j, n - j)
            return BASE + HOP + FAR * (hop - 1), hop * piece / RATE

        def zlink(j):
            return "z+" if j <= nz // 2 else "z-"

        def a0():
            first_t = jnp.transpose(ypad[:, 0:K])
            gloc[h] = mm(first_t, ypad[:, h * K:(h + 1) * K]).reshape(gloc.shape[1:])
            put(gloc.at[h, other], gpart.at[h], *sem(0), {"child": other})

        def a1():
            wait(0, gpart.at[h])
            gz[h] = (gloc[h, c] + gpart[h]).reshape(gz.shape[1:])
            for j in zorder:
                z = lax.rem(my_z + j, nz)
                put(gz.at[h, z], zr.at[h, j - 1], *sem(1), at_z(z))

        def a2():
            wait(1, zr.at[h])
            total = total_of(gz[h, my_z], zr, nz - 1)
            gs[h] = total
            for j in range(1, ny):
                y = lax.rem(my_y + j, ny)
                put(gs.at[h], yr.at[h, j - 1], *sem(2), at_y(y))

        def a3():
            if ny > 1:
                wait(2, yr.at[h])
            total = total_of(gs[h], yr, ny - 1)
            gf[h, c, my_z] = total
            for j in zorder:
                z = lax.rem(my_z + j, nz)
                put(gf.at[h, c, my_z], gf.at[h, c, my_z], *sem(3), at_z(z))

        def a4():
            wait(3, zr.at[h])
            put(gf.at[h, c], gf.at[h, c], *sem(4), {"child": other})

        def a5():
            wait(4, gf.at[h, c])

        for i, buf in enumerate((gpart, zr, yr, zr, gpart)):
            if i != 2 or ny > 1:
                sent.append((as_.at[h, i], buf.at[h]))
        zorder = sorted(range(1, nz), key=lambda j: -min(j, nz - j))
        acts.append(Act(t + (0,), a0, after=ready, sends=[(t + ("p",), "c", 0.3, 1.0)], cost=1.2, prio=5))
        acts.append(Act(t + (1,), a1, after=[t + (0,)], deps=[t + ("p",)], prio=5,
                        sends=[(t + ("z", j), zlink(j), lag(j, nz)[1], lag(j, nz)[0]) for j in zorder]))
        acts.append(Act(t + (2,), a2, after=[t + (1,)], deps=[t + ("z", j) for j in zorder], prio=5,
                        sends=[(t + ("y", j), "y+" if j <= ny // 2 else "y-", lag(j, ny)[1], lag(j, ny)[0])
                               for j in range(1, ny)]))
        acts.append(Act(t + (3,), a3, after=[t + (2,)], deps=[t + ("y", j) for j in range(1, ny)], prio=5,
                        sends=[(t + ("w", j), zlink(j), lag(j, nz)[1], lag(j, nz)[0]) for j in zorder]))
        acts.append(Act(t + (4,), a4, after=[t + (3,)], deps=[t + ("w", j) for j in zorder],
                        sends=[(t + ("v",), "c", 0.3, 1.0)], cost=0.05, prio=5))
        acts.append(Act(t + (5,), a5, after=[t + (4,)], deps=[t + ("v",)], cost=0.02, prio=6))
        return t + (5,)

    sub = lax.broadcasted_iota(jnp.int32, (BLK, BLK), 0)
    lane = lax.broadcasted_iota(jnp.int32, (BLK, BLK), 1)

    def chol_begin():
        aug_ref[:, 0:K] = gf[0].reshape(K, K) * scale
        big = lax.broadcasted_iota(jnp.int32, (K, K), 0) == lax.broadcasted_iota(jnp.int32, (K, K), 1)
        aug_ref[:, K:2 * K] = jnp.where(big, 1.0, 0.0)

    def chol_block(b):
        lo, hi = b * BLK, (b + 1) * BLK
        both = jnp.concatenate([aug_ref[lo:hi, lo:hi], jnp.where(sub == lane, 1.0, 0.0)], axis=1)
        d = [both[8 * g:8 * g + 8, :] for g in range(BLK // 8)]
        sub8 = lax.broadcasted_iota(jnp.int32, (8, 2 * BLK), 0)
        lane8 = lax.broadcasted_iota(jnp.int32, (8, 2 * BLK), 1)
        for p in range(0, BLK, 2):
            g0, q = p // 8, p % 8
            row0, row1 = d[g0][q:q + 1, :], d[g0][q + 1:q + 2, :]
            col0 = [jnp.broadcast_to(x[:, p:p + 1], x.shape) for x in d[g0:]]
            col1 = [jnp.broadcast_to(x[:, p + 1:p + 2], x.shape) for x in d[g0:]]
            aa, ab, bb = col0[0][q:q + 1, :], col0[0][q + 1:q + 2, :], col1[0][q + 1:q + 2, :]
            inv_det = 1.0 / (aa * bb - ab * ab)
            mix0 = (bb * inv_det) * row0 - (ab * inv_det) * row1
            mix1 = (aa * inv_det) * row1 - (ab * inv_det) * row0
            for g in range(g0, BLK // 8):
                x0, x1 = col0[g - g0], col1[g - g0]
                if g == g0:
                    if q == 6:
                        continue
                    x0 = jnp.where(sub8 > q + 1, x0, 0.0)
                    x1 = jnp.where(sub8 > q + 1, x1, 0.0)
                d[g] = d[g] - (x0 * mix0 + x1 * mix1)
        out = []
        for g in range(BLK // 8):
            me = sub8 + 8 * g
            diag = jnp.sum(jnp.where(lane8 == me, d[g], 0.0), axis=1, keepdims=True)
            side = jnp.where((lane8 == me - 1) & (sub8 % 2 == 1), d[g], 0.0)
            side = jnp.sum(side, axis=1, keepdims=True)
            wide = jnp.broadcast_to(diag, d[g].shape)
            lift = side / pltpu.roll(wide, 1, 0)
            full = d[g] - lift * pltpu.roll(d[g], 1, 0)
            out.append(full * (1.0 / jnp.sqrt(wide - lift * side)))
        inv = jnp.concatenate(out, axis=0)[:, BLK:2 * BLK]
        left, right = (0, K + TILE) if hi <= TILE else (TILE, 2 * K)
        z = mm(inv, aug_ref[lo:hi, left:right])
        aug_ref[lo:hi, left:right] = z
        if hi < K:
            base = hi // TILE * TILE
            u = jnp.transpose(aug_ref[lo:hi, base:K])[hi - base:, :]
            aug_ref[hi:K, left:right] = aug_ref[hi:K, left:right] - mm(u, z)

    def basis():
        w = aug_ref[:, K:2 * K]
        q = mm(ypad[:, 0:K], w, (((1,), (1,)), ((), ())))
        q_ref[...] = q[0:rows, :]
        qw_ref[...] = mm(q, w) * scale

    def fresh():
        fit = mm(qw_ref[...], gf[1].reshape(K, K))
        f_ref[...] = ypad[0:rows, K:2 * K] - fit[0:rows, :]

    for h in range(2):
        for j in range(ny):
            presum(h, j)
    ends = [[flow(h, i) for i in range(nsets)] for h in range(2)]
    g1 = gram_sum(0, ends[0])
    g2 = gram_sum(1, ends[0] + ends[1])
    acts.append(Act("chol", chol_begin, after=[g1], cost=0.3, idle=True))
    prev = "chol"
    for b in range(K // BLK):
        acts.append(Act(("chol", b), functools.partial(chol_block, b), after=[prev], cost=3.3, idle=True))
        prev = ("chol", b)
    acts.append(Act("basis", basis, after=[prev], cost=2.0, idle=True))
    acts.append(Act("fresh", fresh, after=["basis", g2], cost=1.2))
    for _, act in arrange(acts, 7.0, arrive):
        act.run()
    sent.append((xs.at[0], xb_ref))
    for sem, buf in sent:
        remote(buf, buf, sem, sem, {"child": other}).wait_send()


def fused(expanded, child_map, seeds, ny, nz, rows, leaf_rows):
    sets = row_sets(rows)
    block_cols = expanded.shape[1]
    vm = pltpu.VMEM
    bf = jnp.bfloat16
    slots1 = [vm((2, max(1, (ny if s[0] == "Y" else nz) - 1), nz if s[0] == "Y" else ny, s[2], K), F32) for s in sets]
    slots2 = [vm((2, max(1, (nz if s[0] == "Y" else ny) - 1), 1, s[2], K), F32) for s in sets]
    dma = pltpu.SemaphoreType.DMA

    def groups(n):
        return max(1, n - 1 - sum(1 for r in hops(n, 0) if r) + 1)

    piece = K // 2 // nz
    chunk = nz * rows
    out = jax.ShapeDtypeStruct((rows, K), F32)
    return pl.pallas_call(
        functools.partial(fused_kernel, ny, nz, rows, 1.0 / leaf_rows),
        out_shape=(out, out),
        in_specs=[
            pl.BlockSpec(memory_space=pltpu.SMEM),
            pl.BlockSpec(memory_space=pltpu.VMEM),
            pl.BlockSpec(memory_space=pl.ANY),
        ],
        out_specs=[pl.BlockSpec(memory_space=pltpu.VMEM)] * 2,
        scratch_shapes=[
            *slots1, *slots2,
            *[dma((2, groups(ny if s[0] == "Y" else nz))) for s in sets],
            *[dma((2, 3 if s[0] == "Y" and nz == 8 else groups(nz) if s[0] == "Y" else 1)) for s in sets],
            vm((2 * K, block_cols), bf),
            vm((ny, chunk, block_cols), bf), vm((ny, chunk, block_cols), bf),
            vm((2, ny, nz, rows, K), F32), vm((2, ny, nz, rows, K), F32), vm((2, ny, nz, rows, K), F32),
            vm((TILE, 2 * K), F32), vm((2, 2, K // 2, K), F32), vm((2, K // 2, K), F32),
            vm((2, nz, piece, K), F32), vm((2, nz - 1, piece, K), F32), vm((2, piece, K), F32),
            vm((2, max(1, ny - 1), piece, K), F32), vm((2, 2, nz, piece, K), F32),
            vm((K, 2 * K), F32), vm((TILE, K), F32),
            dma((ny + 1,)), dma((1,)), dma((2, ny)),
            dma((len(sets),)), dma((len(sets),)), dma((2, 5)), dma((2, 5)),
        ],
        compiler_params=pltpu.CompilerParams(
            collective_id=0, has_side_effects=True, vmem_limit_bytes=63 << 20),
    )(seeds, child_map, expanded.reshape(2, ny, chunk, block_cols))


def make_body(parent_rows):
    def body(schur_blocks, child_map, round_seeds):
        col_count = lax.axis_size("col")
        ny, nz = GRIDS[col_count]
        leaf_rows = parent_rows // lax.axis_size("row")
        own_rows = leaf_rows // (2 * col_count)
        expanded = expand_rows(schur_blocks[0], child_map, leaf_rows)
        return fused(expanded, child_map, round_seeds, ny, nz, own_rows, leaf_rows)
    return body


def solution(mesh, parent_rows=24576):
    placed = (P("child", "row", "col"), P(), P())
    return jax.shard_map(
        make_body(parent_rows),
        mesh=mesh,
        in_specs=placed,
        out_specs=(P(("row", "child", "col"), None), P(("row", "child", "col"), None)),
        check_vma=False,
    )
```

```python
import functools
import jax
import jax.numpy as jnp
from jax import lax
from jax.experimental import pallas as pl
from jax.experimental.pallas import tpu as pltpu
from jax.sharding import PartitionSpec as P

K = 256
TILE = 128
BLK = 64
GRIDS = {32: (4, 8), 8: (2, 4)}
MESH = pl.DeviceIdType.MESH
F32 = jnp.float32
RATE = 46.0e3
HOP = 0.8
BASE = 1.4
FAR = 0.15
SETS96 = [("Z", 0, 16, 1), ("Y", 16, 8, 1), ("Y", 24, 8, 0), ("Y", 32, 24, 1), ("Z", 56, 8, 1), ("Z", 64, 16, 0), ("Y", 80, 16, 0)]
GATES96 = [[(0, 1, "mid")], [(0, 2, "end")], [(2, 1, "mid")], [(3, 1, "mid")], [(2, 2, "end")], [(5, 1, "mid")], [(5, 2, "end")]]


def gate(i, sets):
    return GATES96[i] if sets == SETS96 else [(i, 1, 'mid')]


def split(x):
    high = x.astype(jnp.bfloat16)
    return high, (x - high.astype(F32)).astype(jnp.bfloat16)


def mm(a, b, dims=(((1,), (0,)), ((), ()))):
    (ah, al), (bh, bl) = split(a), split(b)

    def dot(x, y):
        return lax.dot_general(x, y, dims, preferred_element_type=F32)
    return dot(ah, bh) + (dot(ah, bl) + dot(al, bh))


def hash_values(ids_row, col, seed):
    h = ids_row * 40503 + col * 9973 + seed * 2654435
    h = h ^ ((h >> 15) & 131071)
    h = h * 73244475
    h = h ^ ((h >> 13) & 524287)
    h = h * 1274126177
    h = h ^ ((h >> 16) & 65535)
    unit = (h & 16777215).astype(F32) * (1.0 / 16777216.0)
    return (unit - 0.5) * 3.4641016


def row_sets(rows):
    if rows == 96:
        return SETS96
    q = rows // 4
    return [("Y", 0, q, 0), ("Z", q, q, 0), ("Y", 2 * q, q, 1), ("Z", 3 * q, q, 1)]


def hops(n, orient):
    long, short = n // 2, n - 1 - n // 2
    return (short, long) if orient else (long, short)


class Act:
    def __init__(self, name, run, after=(), deps=(), sends=(), cost=0.25, idle=False, prio=0):
        self.name, self.run, self.after, self.deps = name, run, list(after), list(deps)
        self.sends, self.cost, self.idle, self.prio = list(sends), cost, idle, prio


def arrange(acts, now, arrive):
    arrive, free, done, order = dict(arrive), {}, set(), []
    left = list(acts)
    while left:
        ready = []
        for a in left:
            if all(n in done for n in a.after) and all(d in arrive for d in a.deps):
                ready.append((max([now] + [arrive[d] for d in a.deps]), a.prio, len(ready), a))
        work = [r for r in ready if not r[3].idle]
        spare = [r for r in ready if r[3].idle]
        pick = min(work or spare, key=lambda r: r[:3])
        if work and spare:
            s = min(spare, key=lambda r: r[:3])
            if s[0] + 0.6 * s[3].cost <= pick[0]:
                pick = s
        a = pick[3]
        now = pick[0] + a.cost
        for key, link, size, lag in a.sends:
            free[link] = max(free.get(link, 0.0), now) + size
            arrive[key] = free[link] + lag
        done.add(a.name)
        left.remove(a)
        order.append((now, a))
    return order


STEP_TILES = 4


def expand_kernel(map_ref, a_hbm, e_ref, a_ref, m2_ref, sv_ref, ss_ref, a_sem, sv_sem):
    step = pl.program_id(0)
    block_rows = a_ref.shape[0]
    blocks = block_rows // TILE
    c = lax.axis_index("child")
    row = lax.axis_index("row")
    base = row * (e_ref.shape[0] * pl.num_programs(0))

    @pl.when(step == 0)
    def _():
        load = pltpu.make_async_copy(a_hbm, a_ref, a_sem)
        load.start()

        def fill(j, carry):
            at = pl.multiple_of(row * block_rows + j * TILE, TILE)
            both = map_ref[:, pl.ds(at, TILE)]
            m2_ref[pl.ds(j, 1), :] = jnp.where(c == 0, both[0:1, :], both[1:2, :])
            return carry
        lax.fori_loop(0, blocks, fill, 0)
        firsts = base + lax.broadcasted_iota(jnp.int32, (blocks, TILE), 1) * TILE
        below = (m2_ref[:, TILE - 1:TILE] < firsts).astype(jnp.int32)
        counts = jnp.minimum(jnp.sum(below, axis=0, keepdims=True), blocks - 2)
        sv_ref[...] = jnp.broadcast_to(counts, sv_ref.shape)
        to_scalar = pltpu.make_async_copy(sv_ref, ss_ref, sv_sem)
        to_scalar.start()
        to_scalar.wait()
        load.wait()

    for q in range(STEP_TILES):
        t = step * STEP_TILES + q
        b = ss_ref[0, t]
        window = jnp.concatenate([m2_ref[pl.ds(b, 1), :], m2_ref[pl.ds(b + 1, 1), :]], axis=1)
        wanted = lax.broadcasted_iota(jnp.int32, (TILE, 2 * TILE), 0) + (base + t * TILE)
        pick = jnp.where(window == wanted, 1.0, 0.0).astype(jnp.bfloat16)
        src = a_ref[pl.ds(pl.multiple_of(b * TILE, TILE), 2 * TILE), :]
        e_ref[q * TILE:(q + 1) * TILE, :] = jnp.dot(
            pick, src, preferred_element_type=F32).astype(jnp.bfloat16)


def expand_rows(child_block, child_map, leaf_rows):
    block_rows, block_cols = child_block.shape
    bf = jnp.bfloat16
    rows = STEP_TILES * TILE
    return pl.pallas_call(
        expand_kernel,
        grid=(leaf_rows // rows,),
        out_shape=jax.ShapeDtypeStruct((leaf_rows, block_cols), bf),
        in_specs=[pl.BlockSpec(child_map.shape, lambda i: (0, 0)), pl.BlockSpec(memory_space=pl.ANY)],
        out_specs=pl.BlockSpec((rows, block_cols), lambda i: (i, 0)),
        scratch_shapes=[
            pltpu.VMEM((block_rows, block_cols), bf),
            pltpu.VMEM((block_rows // TILE, TILE), jnp.int32), pltpu.VMEM((8, TILE), jnp.int32),
            pltpu.SMEM((8, TILE), jnp.int32),
            pltpu.SemaphoreType.DMA(()), pltpu.SemaphoreType.DMA(()),
        ],
        compiler_params=pltpu.CompilerParams(vmem_limit_bytes=48 << 20),
    )(child_map, child_block)


def fused_kernel(ny, nz, rows, scale, seeds_ref, map_ref, e_hbm, q_ref, y2_ref, qw_ref, g_ref, *refs):
    sets = row_sets(rows)
    nsets = len(sets)
    slots1, slots2 = refs[:nsets], refs[nsets:2 * nsets]
    got1, got2 = refs[2 * nsets:3 * nsets], refs[3 * nsets:4 * nsets]
    (st_ref, eo_ref, em_ref, xb_ref, h_ref, r_ref,
     ypad, gloc, gpart, gz, zr, gs, yr, gf, aug_ref,
     e_sem, xs, xr, s1, s2, as_, ar_) = refs[4 * nsets:]

    block_cols = em_ref.shape[2]

    c = lax.axis_index("child")
    k = lax.axis_index("col")
    my_y = k // nz
    my_z = k - my_y * nz
    other = 1 - c

    def at_y(y):
        return {"col": y * nz + my_z}

    def at_z(z):
        return {"col": my_y * nz + z}

    sent = []

    def remote(src, dst, ssem, rsem, dev):
        return pltpu.make_async_remote_copy(
            src_ref=src, dst_ref=dst, send_sem=ssem, recv_sem=rsem,
            device_id=dev, device_id_type=MESH)

    def put(*args):
        cp = remote(*args)
        cp.start()
        return cp

    def y_of(j):
        return lax.rem(my_y + ny // 2 - j + ny, ny)

    def fetch(side, j):
        half, dst = ((other, eo_ref), (c, em_ref))[side]
        return pltpu.make_async_copy(e_hbm.at[half, y_of(j)], dst.at[j], e_sem.at[ny if side else j])

    for side in range(2):
        for j in range(ny):
            fetch(side, j).start()
    barrier = pltpu.get_barrier_semaphore()
    peers = [{"child": other}]
    peers += [at_y(lax.rem(my_y + j, ny)) for j in range(1, ny)]
    peers += [at_z(lax.rem(my_z + j, nz)) for j in range(1, nz)]
    for dev in peers:
        pl.semaphore_signal(barrier, inc=1, device_id=dev, device_id_type=MESH)

    both_ids = map_ref[:, pl.ds(pl.multiple_of(k * block_cols, TILE), block_cols)]
    ids = jnp.where(c == 0, both_ids[0:1, :], both_ids[1:2, :])

    def draw(i, carry):
        j0 = pl.multiple_of(i * 32, 32)
        t = j0 // K
        col = lax.broadcasted_iota(jnp.int32, (32, block_cols), 0) + (j0 - t * K)
        st_ref[pl.ds(j0, 32), :] = hash_values(ids, col, seeds_ref[t]).astype(jnp.bfloat16)
        return carry
    lax.fori_loop(0, 2 * K // 32, draw, 0)
    ypad[...] = jnp.zeros_like(ypad)

    def sketch(e, h):
        return lax.dot_general(
            e[...], st_ref[h * K:(h + 1) * K, :], (((1,), (1,)), ((), ())),
            preferred_element_type=F32).reshape(nz, rows, K)

    def swap(h, j):
        y = y_of(j)
        return remote(xb_ref.at[h, y], r_ref.at[h, y], xs.at[0], xr.at[h, j], {"child": other})

    pl.semaphore_wait(barrier, len(peers))

    def give0(j, carry):
        y = y_of(j)
        fetch(0, j).wait()
        xb_ref[0, y] = sketch(eo_ref.at[j], 0)
        swap(0, j).start()
        return carry
    lax.fori_loop(0, ny, give0, 0)

    def give1():
        def body(j, carry):
            xb_ref[1, y_of(j)] = sketch(eo_ref.at[j], 1)
            swap(1, j).start()
            return carry
        lax.fori_loop(0, ny, body, 0)

    def keep(h):
        if h == 0:
            pltpu.make_async_copy(em_ref, em_ref, e_sem.at[ny]).wait()

        def body(j, carry):
            h_ref[h, y_of(j)] = sketch(em_ref.at[j], h)
            return carry
        lax.fori_loop(0, ny, body, 0)

    acts = []
    arrive = {("x", 0, j): 7.0 + 1.4 * j for j in range(ny)}
    acts.append(Act("keep0", functools.partial(keep, 0), cost=2.0, prio=-2))
    acts.append(Act("give1", give1, after=["keep0"], cost=2.0, prio=0.5,
                    sends=[(("x", 1, j), "c", 1.4, 0.5) for j in range(ny)]))
    acts.append(Act("keep1", functools.partial(keep, 1), after=["give1"], cost=2.0, prio=0.6))

    def presum(h, j):
        def run():
            swap(h, j).wait_recv()
            y = y_of(j)

            def body(z, carry):
                h_ref[h, y, z] = h_ref[h, y, z] + r_ref[h, y, z]
                return carry
            lax.fori_loop(0, nz, body, 0)
        acts.append(Act(("pre", h, j), run, after=["keep%d" % h], deps=[("x", h, j)], cost=0.4, prio=h))

    class Ring:
        def __init__(self, tag, axis, n, pos, at, orient, own, own_ix, lead, slot, ssem, rsem, nr):
            self.tag, self.axis, self.n, self.pos, self.at = tag, axis, n, pos, at
            self.hp, self.hm = hops(n, orient)
            self.own, self.own_ix, self.lead = own, own_ix, lead
            self.slot, self.ssem, self.rsem = slot, ssem, rsem
            self.size = lead * nr * K * 4
            self.groups = self.group()

        def group(self):
            last = self.last_slots()
            return [last] + [[m] for m in range(self.n - 1) if m not in last]

        def sem_of(self, m):
            return self.rsem([m in g for g in self.groups].index(True))

        def wait(self, which):
            ref, h = self.slot
            if self.groups[which]:
                span = ref.at[h, pl.ds(0, len(self.groups[which]))]
                remote(span, span, self.ssem, self.rsem(which), {"child": other}).wait_recv()

        def wait_for(self, m):
            self.wait([m in g for g in self.groups].index(True))

        def cost(self):
            return 0.06 + 1.6e-3 * self.size / 4096

        def reach(self, sign):
            return self.hp if sign > 0 else self.hm

        def index(self, sign, s):
            return s if sign > 0 else self.hp + s

        def key(self, sign, s):
            return self.tag + (self.index(sign, s),)

        def load_out(self, sign, s):
            link = self.axis + ("+" if sign > 0 else "-")
            return (self.key(sign, s), link, self.size / RATE, BASE + HOP)

        def send(self, sign, s):
            n = self.n
            d = lax.rem(self.pos + sign * (self.reach(sign) - s) + n, n)
            dev = self.at(lax.rem(self.pos + sign + n, n))
            m = self.index(sign, s)
            if s:
                self.wait_for(m - 1)
                ref, h = self.slot
                own, oix = self.own_ix

                def body(i, carry):
                    ref[h, m - 1, i] = ref[h, m - 1, i] + own[oix(d, i)]
                    return carry
                lax.fori_loop(0, self.lead, body, 0)
                src = ref.at[h, m - 1]
            else:
                src = self.own(d)
            ref, h = self.slot
            put(src, ref.at[h, m], self.ssem, self.sem_of(m), dev)

        def last(self):
            return [(sign, self.reach(sign) - 1) for sign in (1, -1) if self.reach(sign)]

        def finish(self):
            ref, h = self.slot
            own, oix = self.own_ix
            last = self.last_slots()
            self.wait(0)

            def body(i, carry):
                total = own[oix(self.pos, i)]
                for m in last:
                    total = total + ref[h, m, i]
                own[oix(self.pos, i)] = total
                return carry
            lax.fori_loop(0, self.lead, body, 0)

        def chain(self, before, prio):
            for sign in (1, -1):
                prev = before
                for s in range(1, self.reach(sign)):
                    name = self.tag + (sign, s)
                    acts.append(Act(name, functools.partial(self.send, sign, s), after=[prev],
                                    deps=[self.key(sign, s - 1)], sends=[self.load_out(sign, s)],
                                    cost=self.cost(), prio=prio))
                    prev = name

        def ends(self):
            return [self.tag + (m,) for m in self.last_slots()]

        def start(self):
            for sign in (1, -1):
                if self.reach(sign):
                    self.send(sign, 0)

        def first_sends(self):
            return [self.load_out(sg, 0) for sg in (1, -1) if self.reach(sg)]

        def more(self, before, prio):
            self.chain(before, prio)
            return [before]

        def last_slots(self):
            return [self.index(*e) for e in self.last()]

    class Direct(Ring):
        def start(self):
            ref, h = self.slot
            for j in range(1, self.n):
                d = lax.rem(self.pos + j, self.n)
                put(self.own(d), ref.at[h, j - 1], self.ssem, self.sem_of(j - 1), self.at(d))

        def first_sends(self):
            out = []
            for j in range(1, self.n):
                hop = min(j, self.n - j)
                link = self.axis + ("+" if j <= self.n // 2 else "-")
                out.append((self.tag + (j - 1,), link, hop * self.size / RATE, BASE + HOP + FAR * (hop - 1)))
            return out

        def more(self, before, prio):
            return [before]

        def last_slots(self):
            return list(range(self.n - 1))

    class Tree(Direct):
        FIRST = ((0, 2, 4), (1, 1, 3), (2, 1, 1), (3, -1, -3), (4, -1, -1))
        SECOND = ((5, 2, (0, 1)), (6, -2, (3,)))

        def sign(self):
            return 1 if self.hp >= self.hm else -1

        def go(self, m, off, src):
            ref, h = self.slot
            dev = lax.rem(self.pos + self.sign() * off + self.n, self.n)
            put(src, ref.at[h, m], self.ssem, self.sem_of(m), self.at(dev))

        def sim(self, m, off):
            link = self.axis + ("+" if off * self.sign() > 0 else "-")
            hop = abs(off)
            return (self.tag + (m,), link, hop * self.size / RATE, BASE + HOP + FAR * (hop - 1))

        def start(self):
            for m, off, piece in self.FIRST:
                d = lax.rem(self.pos + self.sign() * piece + self.n, self.n)
                self.go(m, off, self.own(d))

        def first_sends(self):
            return [self.sim(m, off) for m, off, _ in self.FIRST]

        def second(self, m, off, got):
            ref, h = self.slot
            own, oix = self.own_ix
            d = lax.rem(self.pos + self.sign() * off + self.n, self.n)
            total = own[oix(d, 0)]
            self.wait_for(got[0])
            for g in got:
                total = total + ref[h, g, 0]
            ref[h, got[0], 0] = total
            self.go(m, off, ref.at[h, got[0]])

        def more(self, before, prio):
            names = [before]
            for m, off, got in self.SECOND:
                name = self.tag + ("second", m)
                acts.append(Act(name, functools.partial(self.second, m, off, got), after=[before],
                                deps=[self.tag + (g,) for g in got], sends=[self.sim(m, off)],
                                cost=0.08, prio=prio))
                names.append(name)
            return names

        def last_slots(self):
            return [2, 4, 5, 6]

        def group(self):
            return [self.last_slots(), [0, 1], [3]]

    def flow(h, i):
        color, r0, nr, orient = sets[i]
        rs = pl.ds(r0, nr)
        sems = (s1.at[i], lambda m: got1[i].at[h, m])
        sems2 = (s2.at[i], lambda m: got2[i].at[h, m])
        t1, t2 = ("f", h, i, 1), ("f", h, i, 2)
        if color == "Y":
            first = Ring(t1, "y", ny, my_y, at_y, orient,
                         lambda d: h_ref.at[h, d, :, rs, :],
                         (h_ref, lambda d, j: (h, d, j, rs, slice(None))), nz, (slots1[i], h), *sems, nr)
            second = (Tree if nz == 8 else Ring)(t2, "z", nz, my_z, at_z, orient,
                          lambda d: h_ref.at[h, my_y, pl.ds(d, 1), rs, :],
                          (h_ref, lambda d, j: (h, my_y, d, rs, slice(None))), 1, (slots2[i], h), *sems2, nr)
        else:
            first = Ring(t1, "z", nz, my_z, at_z, orient,
                         lambda d: h_ref.at[h, :, d, rs, :],
                         (h_ref, lambda d, j: (h, j, d, rs, slice(None))), ny, (slots1[i], h), *sems, nr)
            second = Direct(t2, "y", ny, my_y, at_y, orient,
                          lambda d: h_ref.at[h, pl.ds(d, 1), my_z, rs, :],
                          (h_ref, lambda d, j: (h, d, my_z, rs, slice(None))), 1, (slots2[i], h), *sems2, nr)
        if h:
            sent.extend((ring.ssem, buf) for ring, buf in ((first, slots1[i]), (second, slots2[i])) if ring.n > 1)
        prio = 10 * h
        starts = []
        for sign in (1, -1):
            if not first.reach(sign):
                continue
            if color == "Y":
                rel = (sign * first.reach(sign)) % ny
                need = [("pre", h, (ny // 2 - rel) % ny)]
            else:
                need = [("pre", h, j) for j in range(ny)]
            if h:
                need = need + [("f", 0) + g for g in gate(i, sets)]
            name = t1 + (sign, 0)
            starts.append(name)
            acts.append(Act(name, functools.partial(first.send, sign, 0), after=need,
                            sends=[first.load_out(sign, 0)], cost=0.03,
                            prio=prio + 1 - 0.1 * first.reach(sign)))
        for sign in (1, -1):
            prev = t1 + (sign, 0)
            for s in range(1, first.reach(sign)):
                name = t1 + (sign, s)
                acts.append(Act(name, functools.partial(first.send, sign, s),
                                after=[prev] + [("pre", h, j) for j in range(ny)],
                                deps=[first.key(sign, s - 1)], sends=[first.load_out(sign, s)],
                                cost=first.cost(), prio=prio))
                prev = name

        def middle():
            first.finish()
            second.start()
        mid = t1 + ("mid",)
        acts.append(Act(mid, middle, after=starts + [("pre", h, j) for j in range(ny)], deps=first.ends(),
                        sends=second.first_sends(), cost=0.06 + first.cost(), prio=prio))
        before = second.more(mid, prio)
        end = t2 + ("end",)

        def finish():
            second.finish()
            ypad[pl.ds(r0, nr), h * K:(h + 1) * K] = h_ref[h, my_y, my_z, r0:r0 + nr, :]
        acts.append(Act(end, finish, after=before, deps=second.ends(), cost=0.1, prio=prio))
        return end

    def gram_sum(h, ready):
        t = ("g", h)
        piece = gz.shape[2] * K * 4

        def sem(i):
            return as_.at[h, i], ar_.at[h, i]

        def wait(i, buf):
            remote(buf, buf, *sem(i), {"child": other}).wait_recv()

        def total_of(start, parts, count):
            for j in range(count):
                start = start + parts[h, j]
            return start

        def lag(j, n):
            hop = min(j, n - j)
            return BASE + HOP + FAR * (hop - 1), hop * piece / RATE

        def zlink(j):
            return "z+" if j <= nz // 2 else "z-"

        def a0():
            first_t = jnp.transpose(ypad[:, 0:K])
            gloc[h] = mm(first_t, ypad[:, h * K:(h + 1) * K]).reshape(gloc.shape[1:])
            put(gloc.at[h, other], gpart.at[h], *sem(0), {"child": other})

        def a1():
            wait(0, gpart.at[h])
            gz[h] = (gloc[h, c] + gpart[h]).reshape(gz.shape[1:])
            for j in zorder:
                z = lax.rem(my_z + j, nz)
                put(gz.at[h, z], zr.at[h, j - 1], *sem(1), at_z(z))

        def a2():
            wait(1, zr.at[h])
            total = total_of(gz[h, my_z], zr, nz - 1)
            gs[h] = total
            for j in range(1, ny):
                y = lax.rem(my_y + j, ny)
                put(gs.at[h], yr.at[h, j - 1], *sem(2), at_y(y))

        def a3():
            if ny > 1:
                wait(2, yr.at[h])
            total = total_of(gs[h], yr, ny - 1)
            gf[h, c, my_z] = total
            for j in zorder:
                z = lax.rem(my_z + j, nz)
                put(gf.at[h, c, my_z], gf.at[h, c, my_z], *sem(3), at_z(z))

        def a4():
            wait(3, zr.at[h])
            put(gf.at[h, c], gf.at[h, c], *sem(4), {"child": other})

        def a5():
            wait(4, gf.at[h, c])

        for i, buf in enumerate((gpart, zr, yr, zr, gpart)):
            if i != 2 or ny > 1:
                sent.append((as_.at[h, i], buf.at[h]))
        zorder = sorted(range(1, nz), key=lambda j: -min(j, nz - j))
        acts.append(Act(t + (0,), a0, after=ready, sends=[(t + ("p",), "c", 0.3, 1.0)], cost=1.2, prio=5))
        acts.append(Act(t + (1,), a1, after=[t + (0,)], deps=[t + ("p",)], prio=5,
                        sends=[(t + ("z", j), zlink(j), lag(j, nz)[1], lag(j, nz)[0]) for j in zorder]))
        acts.append(Act(t + (2,), a2, after=[t + (1,)], deps=[t + ("z", j) for j in zorder], prio=5,
                        sends=[(t + ("y", j), "y+" if j <= ny // 2 else "y-", lag(j, ny)[1], lag(j, ny)[0])
                               for j in range(1, ny)]))
        acts.append(Act(t + (3,), a3, after=[t + (2,)], deps=[t + ("y", j) for j in range(1, ny)], prio=5,
                        sends=[(t + ("w", j), zlink(j), lag(j, nz)[1], lag(j, nz)[0]) for j in zorder]))
        acts.append(Act(t + (4,), a4, after=[t + (3,)], deps=[t + ("w", j) for j in zorder],
                        sends=[(t + ("v",), "c", 0.3, 1.0)], cost=0.05, prio=5))
        acts.append(Act(t + (5,), a5, after=[t + (4,)], deps=[t + ("v",)], cost=0.02, prio=6))
        return t + (5,)

    sub = lax.broadcasted_iota(jnp.int32, (BLK, BLK), 0)
    lane = lax.broadcasted_iota(jnp.int32, (BLK, BLK), 1)

    def chol_begin():
        aug_ref[:, 0:K] = gf[0].reshape(K, K) * scale
        big = lax.broadcasted_iota(jnp.int32, (K, K), 0) == lax.broadcasted_iota(jnp.int32, (K, K), 1)
        aug_ref[:, K:2 * K] = jnp.where(big, 1.0, 0.0)

    def chol_block(b):
        lo, hi = b * BLK, (b + 1) * BLK
        both = jnp.concatenate([aug_ref[lo:hi, lo:hi], jnp.where(sub == lane, 1.0, 0.0)], axis=1)
        d = [both[8 * g:8 * g + 8, :] for g in range(BLK // 8)]
        sub8 = lax.broadcasted_iota(jnp.int32, (8, 2 * BLK), 0)
        lane8 = lax.broadcasted_iota(jnp.int32, (8, 2 * BLK), 1)
        for p in range(0, BLK, 2):
            g0, q = p // 8, p % 8
            row0, row1 = d[g0][q:q + 1, :], d[g0][q + 1:q + 2, :]
            col0 = [jnp.broadcast_to(x[:, p:p + 1], x.shape) for x in d[g0:]]
            col1 = [jnp.broadcast_to(x[:, p + 1:p + 2], x.shape) for x in d[g0:]]
            aa, ab, bb = col0[0][q:q + 1, :], col0[0][q + 1:q + 2, :], col1[0][q + 1:q + 2, :]
            inv_det = 1.0 / (aa * bb - ab * ab)
            mix0 = (bb * inv_det) * row0 - (ab * inv_det) * row1
            mix1 = (aa * inv_det) * row1 - (ab * inv_det) * row0
            for g in range(g0, BLK // 8):
                x0, x1 = col0[g - g0], col1[g - g0]
                if g == g0:
                    if q == 6:
                        continue
                    x0 = jnp.where(sub8 > q + 1, x0, 0.0)
                    x1 = jnp.where(sub8 > q + 1, x1, 0.0)
                d[g] = d[g] - (x0 * mix0 + x1 * mix1)
        out = []
        for g in range(BLK // 8):
            me = sub8 + 8 * g
            diag = jnp.sum(jnp.where(lane8 == me, d[g], 0.0), axis=1, keepdims=True)
            side = jnp.where((lane8 == me - 1) & (sub8 % 2 == 1), d[g], 0.0)
            side = jnp.sum(side, axis=1, keepdims=True)
            wide = jnp.broadcast_to(diag, d[g].shape)
            lift = side / pltpu.roll(wide, 1, 0)
            full = d[g] - lift * pltpu.roll(d[g], 1, 0)
            out.append(full * (1.0 / jnp.sqrt(wide - lift * side)))
        inv = jnp.concatenate(out, axis=0)[:, BLK:2 * BLK]
        left, right = (0, K + TILE) if hi <= TILE else (TILE, 2 * K)
        z = mm(inv, aug_ref[lo:hi, left:right])
        aug_ref[lo:hi, left:right] = z
        if hi < K:
            base = hi // TILE * TILE
            u = jnp.transpose(aug_ref[lo:hi, base:K])[hi - base:, :]
            aug_ref[hi:K, left:right] = aug_ref[hi:K, left:right] - mm(u, z)

    def basis():
        w = aug_ref[:, K:2 * K]
        q = mm(ypad[:, 0:K], w, (((1,), (1,)), ((), ())))
        q_ref[...] = q[0:rows, :]
        qw_ref[...] = mm(q[0:rows, :], w) * scale

    def fresh():
        g_ref[...] = gf[1].reshape(K, K)
        y2_ref[...] = ypad[0:rows, K:2 * K]

    for h in range(2):
        for j in range(ny):
            presum(h, j)
    ends = [[flow(h, i) for i in range(nsets)] for h in range(2)]
    g1 = gram_sum(0, ends[0])
    g2 = gram_sum(1, ends[0] + ends[1])
    acts.append(Act("chol", chol_begin, after=[g1], cost=0.3, idle=True))
    prev = "chol"
    for b in range(K // BLK):
        acts.append(Act(("chol", b), functools.partial(chol_block, b), after=[prev], cost=3.3, idle=True))
        prev = ("chol", b)
    acts.append(Act("basis", basis, after=[prev], cost=2.0, idle=True))
    acts.append(Act("fresh", fresh, after=["basis", g2], cost=0.3))
    for _, act in arrange(acts, 7.0, arrive):
        act.run()
    sent.append((xs.at[0], xb_ref))
    for sem, buf in sent:
        remote(buf, buf, sem, sem, {"child": other}).wait_send()


def fused(expanded, child_map, seeds, ny, nz, rows, leaf_rows):
    sets = row_sets(rows)
    block_cols = expanded.shape[1]
    vm = pltpu.VMEM
    bf = jnp.bfloat16
    slots1 = [vm((2, max(1, (ny if s[0] == "Y" else nz) - 1), nz if s[0] == "Y" else ny, s[2], K), F32) for s in sets]
    slots2 = [vm((2, max(1, (nz if s[0] == "Y" else ny) - 1), 1, s[2], K), F32) for s in sets]
    dma = pltpu.SemaphoreType.DMA

    def groups(n):
        return max(1, n - 1 - sum(1 for r in hops(n, 0) if r) + 1)

    piece = K // 2 // nz
    chunk = nz * rows
    out = jax.ShapeDtypeStruct((rows, K), F32)
    return pl.pallas_call(
        functools.partial(fused_kernel, ny, nz, rows, 1.0 / leaf_rows),
        out_shape=(out, out, out, jax.ShapeDtypeStruct((K, K), F32)),
        in_specs=[
            pl.BlockSpec(memory_space=pltpu.SMEM),
            pl.BlockSpec(memory_space=pltpu.VMEM),
            pl.BlockSpec(memory_space=pl.ANY),
        ],
        out_specs=[pl.BlockSpec(memory_space=pltpu.VMEM)] * 4,
        scratch_shapes=[
            *slots1, *slots2,
            *[dma((2, groups(ny if s[0] == "Y" else nz))) for s in sets],
            *[dma((2, 3 if s[0] == "Y" and nz == 8 else groups(nz) if s[0] == "Y" else 1)) for s in sets],
            vm((2 * K, block_cols), bf),
            vm((ny, chunk, block_cols), bf), vm((ny, chunk, block_cols), bf),
            vm((2, ny, nz, rows, K), F32), vm((2, ny, nz, rows, K), F32), vm((2, ny, nz, rows, K), F32),
            vm((TILE, 2 * K), F32), vm((2, 2, K // 2, K), F32), vm((2, K // 2, K), F32),
            vm((2, nz, piece, K), F32), vm((2, nz - 1, piece, K), F32), vm((2, piece, K), F32),
            vm((2, max(1, ny - 1), piece, K), F32), vm((2, 2, nz, piece, K), F32),
            vm((K, 2 * K), F32),
            dma((ny + 1,)), dma((1,)), dma((2, ny)),
            dma((len(sets),)), dma((len(sets),)), dma((2, 5)), dma((2, 5)),
        ],
        compiler_params=pltpu.CompilerParams(
            collective_id=0, has_side_effects=True, vmem_limit_bytes=63 << 20),
    )(seeds, child_map, expanded.reshape(2, ny, chunk, block_cols))


def finish_kernel(q_ref, y2_ref, qw_ref, g_ref, q_out, f_out):
    q_out[...] = q_ref[...]
    f_out[...] = y2_ref[...] - mm(qw_ref[...], g_ref[...])


def finish(q, y2, qw, g):
    out = jax.ShapeDtypeStruct(q.shape, F32)
    return pl.pallas_call(
        finish_kernel,
        out_shape=(out, out),
        in_specs=[pl.BlockSpec(memory_space=pltpu.VMEM)] * 4,
        out_specs=[pl.BlockSpec(memory_space=pltpu.VMEM)] * 2,
        compiler_params=pltpu.CompilerParams(vmem_limit_bytes=63 << 20),
    )(q, y2, qw, g)


def make_body(parent_rows):
    def body(schur_blocks, child_map, round_seeds):
        col_count = lax.axis_size("col")
        ny, nz = GRIDS[col_count]
        leaf_rows = parent_rows // lax.axis_size("row")
        own_rows = leaf_rows // (2 * col_count)
        expanded = expand_rows(schur_blocks[0], child_map, leaf_rows)
        return finish(*fused(expanded, child_map, round_seeds, ny, nz, own_rows, leaf_rows))
    return body


def solution(mesh, parent_rows=24576):
    placed = (P("child", "row", "col"), P(), P())
    return jax.shard_map(
        make_body(parent_rows),
        mesh=mesh,
        in_specs=placed,
        out_specs=(P(("row", "child", "col"), None), P(("row", "child", "col"), None)),
        check_vma=False,
    )
```

```python
import functools
import jax
import jax.numpy as jnp
from jax import lax
from jax.experimental import pallas as pl
from jax.experimental.pallas import tpu as pltpu
from jax.sharding import PartitionSpec as P

K = 256
TILE = 128
BLK = 64
GRIDS = {32: (4, 8), 8: (2, 4)}
MESH = pl.DeviceIdType.MESH
F32 = jnp.float32
RATE = 46.0e3
HOP = 0.8
BASE = 1.4
FAR = 0.15
SETS96 = [("Z", 0, 16, 1), ("Y", 16, 8, 1), ("Y", 24, 8, 0), ("Y", 32, 24, 1), ("Z", 56, 8, 1), ("Z", 64, 16, 0), ("Y", 80, 16, 0)]
GATES96 = [[(0, 1, "mid")], [(0, 2, "end")], [(2, 1, "mid")], [(3, 1, "mid")], [(2, 2, "end")], [(5, 1, "mid")], [(5, 2, "end")]]


def gate(i, sets):
    return GATES96[i] if sets == SETS96 else [(i, 1, 'mid')]


def split(x):
    high = x.astype(jnp.bfloat16)
    return high, (x - high.astype(F32)).astype(jnp.bfloat16)


def mm(a, b, dims=(((1,), (0,)), ((), ()))):
    (ah, al), (bh, bl) = split(a), split(b)

    def dot(x, y):
        return lax.dot_general(x, y, dims, preferred_element_type=F32)
    return dot(ah, bh) + (dot(ah, bl) + dot(al, bh))


def hash_values(ids_row, col, seed):
    h = ids_row * 40503 + col * 9973 + seed * 2654435
    h = h ^ ((h >> 15) & 131071)
    h = h * 73244475
    h = h ^ ((h >> 13) & 524287)
    h = h * 1274126177
    h = h ^ ((h >> 16) & 65535)
    unit = (h & 16777215).astype(F32) * (1.0 / 16777216.0)
    return (unit - 0.5) * 3.4641016


def row_sets(rows):
    if rows == 96:
        return SETS96
    q = rows // 4
    return [("Y", 0, q, 0), ("Z", q, q, 0), ("Y", 2 * q, q, 1), ("Z", 3 * q, q, 1)]


def hops(n, orient):
    long, short = n // 2, n - 1 - n // 2
    return (short, long) if orient else (long, short)


class Act:
    def __init__(self, name, run, after=(), deps=(), sends=(), cost=0.25, idle=False, prio=0):
        self.name, self.run, self.after, self.deps = name, run, list(after), list(deps)
        self.sends, self.cost, self.idle, self.prio = list(sends), cost, idle, prio


def arrange(acts, now, arrive):
    arrive, free, done, order = dict(arrive), {}, set(), []
    left = list(acts)
    while left:
        ready = []
        for a in left:
            if all(n in done for n in a.after) and all(d in arrive for d in a.deps):
                ready.append((max([now] + [arrive[d] for d in a.deps]), a.prio, len(ready), a))
        work = [r for r in ready if not r[3].idle]
        spare = [r for r in ready if r[3].idle]
        pick = min(work or spare, key=lambda r: r[:3])
        if work and spare:
            s = min(spare, key=lambda r: r[:3])
            if s[0] + 0.6 * s[3].cost <= pick[0]:
                pick = s
        a = pick[3]
        now = pick[0] + a.cost
        for key, link, size, lag in a.sends:
            free[link] = max(free.get(link, 0.0), now) + size
            arrive[key] = free[link] + lag
        done.add(a.name)
        left.remove(a)
        order.append((now, a))
    return order


STEP_TILES = 4


def expand_kernel(map_ref, a_hbm, e_ref, a_ref, m2_ref, sv_ref, ss_ref, a_sem, sv_sem):
    step = pl.program_id(0)
    block_rows = a_ref.shape[0]
    blocks = block_rows // TILE
    c = lax.axis_index("child")
    row = lax.axis_index("row")
    base = row * (e_ref.shape[0] * pl.num_programs(0))

    size = STEP_TILES * TILE
    parts = block_rows // size

    def load(n):
        rows = pl.ds(n * size, size)
        return pltpu.make_async_copy(a_hbm.at[rows, :], a_ref.at[rows, :], a_sem.at[n])

    @pl.when(step == 0)
    def _():
        for n in range(parts):
            load(n).start()

        def fill(j, carry):
            at = pl.multiple_of(row * block_rows + j * TILE, TILE)
            both = map_ref[:, pl.ds(at, TILE)]
            m2_ref[pl.ds(j, 1), :] = jnp.where(c == 0, both[0:1, :], both[1:2, :])
            return carry
        lax.fori_loop(0, blocks, fill, 0)
        firsts = base + lax.broadcasted_iota(jnp.int32, (blocks, TILE), 1) * TILE
        below = (m2_ref[:, TILE - 1:TILE] < firsts).astype(jnp.int32)
        counts = jnp.minimum(jnp.sum(below, axis=0, keepdims=True), blocks - 2)
        sv_ref[...] = jnp.broadcast_to(counts, sv_ref.shape)
        to_scalar = pltpu.make_async_copy(sv_ref, ss_ref, sv_sem)
        to_scalar.start()
        to_scalar.wait()
        load(0).wait()

    for n in range(1, parts):
        @pl.when(step == n - 1)
        def _():
            load(n).wait()

    for q in range(STEP_TILES):
        t = step * STEP_TILES + q
        b = ss_ref[0, t]
        window = jnp.concatenate([m2_ref[pl.ds(b, 1), :], m2_ref[pl.ds(b + 1, 1), :]], axis=1)
        wanted = lax.broadcasted_iota(jnp.int32, (TILE, 2 * TILE), 0) + (base + t * TILE)
        pick = jnp.where(window == wanted, 1.0, 0.0).astype(jnp.bfloat16)
        src = a_ref[pl.ds(pl.multiple_of(b * TILE, TILE), 2 * TILE), :]
        e_ref[q * TILE:(q + 1) * TILE, :] = jnp.dot(
            pick, src, preferred_element_type=F32).astype(jnp.bfloat16)


def expand_rows(child_block, child_map, leaf_rows):
    block_rows, block_cols = child_block.shape
    bf = jnp.bfloat16
    rows = STEP_TILES * TILE
    return pl.pallas_call(
        expand_kernel,
        grid=(leaf_rows // rows,),
        out_shape=jax.ShapeDtypeStruct((leaf_rows, block_cols), bf),
        in_specs=[pl.BlockSpec(child_map.shape, lambda i: (0, 0)), pl.BlockSpec(memory_space=pl.ANY)],
        out_specs=pl.BlockSpec((rows, block_cols), lambda i: (i, 0)),
        scratch_shapes=[
            pltpu.VMEM((block_rows, block_cols), bf),
            pltpu.VMEM((block_rows // TILE, TILE), jnp.int32), pltpu.VMEM((8, TILE), jnp.int32),
            pltpu.SMEM((8, TILE), jnp.int32),
            pltpu.SemaphoreType.DMA((block_rows // rows,)), pltpu.SemaphoreType.DMA(()),
        ],
        compiler_params=pltpu.CompilerParams(vmem_limit_bytes=63 << 20),
    )(child_map, child_block)


def fused_kernel(ny, nz, rows, scale, seeds_ref, map_ref, e_hbm, q_ref, y2_ref, qw_ref, g_ref, *refs):
    sets = row_sets(rows)
    nsets = len(sets)
    slots1, slots2 = refs[:nsets], refs[nsets:2 * nsets]
    got1, got2 = refs[2 * nsets:3 * nsets], refs[3 * nsets:4 * nsets]
    (st_ref, eo_ref, em_ref, xb_ref, h_ref, r_ref,
     ypad, gloc, gpart, gz, zr, gs, yr, gf, aug_ref,
     e_sem, xs, xr, s1, s2, as_, ar_) = refs[4 * nsets:]

    block_cols = em_ref.shape[2]

    c = lax.axis_index("child")
    k = lax.axis_index("col")
    my_y = k // nz
    my_z = k - my_y * nz
    other = 1 - c

    def at_y(y):
        return {"col": y * nz + my_z}

    def at_z(z):
        return {"col": my_y * nz + z}

    sent = []

    def remote(src, dst, ssem, rsem, dev):
        return pltpu.make_async_remote_copy(
            src_ref=src, dst_ref=dst, send_sem=ssem, recv_sem=rsem,
            device_id=dev, device_id_type=MESH)

    def put(*args):
        cp = remote(*args)
        cp.start()
        return cp

    def y_of(j):
        return lax.rem(my_y + ny // 2 - j + ny, ny)

    def fetch(side, j):
        half, dst = ((other, eo_ref), (c, em_ref))[side]
        return pltpu.make_async_copy(e_hbm.at[half, y_of(j)], dst.at[j], e_sem.at[ny if side else j])

    for side in range(2):
        for j in range(ny):
            fetch(side, j).start()
    barrier = pltpu.get_barrier_semaphore()
    peers = [{"child": other}]
    peers += [at_y(lax.rem(my_y + j, ny)) for j in range(1, ny)]
    peers += [at_z(lax.rem(my_z + j, nz)) for j in range(1, nz)]
    for dev in peers:
        pl.semaphore_signal(barrier, inc=1, device_id=dev, device_id_type=MESH)

    both_ids = map_ref[:, pl.ds(pl.multiple_of(k * block_cols, TILE), block_cols)]
    ids = jnp.where(c == 0, both_ids[0:1, :], both_ids[1:2, :])

    def draw(i, carry):
        j0 = pl.multiple_of(i * 32, 32)
        t = j0 // K
        col = lax.broadcasted_iota(jnp.int32, (32, block_cols), 0) + (j0 - t * K)
        st_ref[pl.ds(j0, 32), :] = hash_values(ids, col, seeds_ref[t]).astype(jnp.bfloat16)
        return carry
    lax.fori_loop(0, 2 * K // 32, draw, 0)
    ypad[...] = jnp.zeros_like(ypad)

    def sketch(e, h):
        return lax.dot_general(
            e[...], st_ref[h * K:(h + 1) * K, :], (((1,), (1,)), ((), ())),
            preferred_element_type=F32).reshape(nz, rows, K)

    def swap(h, j):
        y = y_of(j)
        return remote(xb_ref.at[h, y], r_ref.at[h, y], xs.at[0], xr.at[h, j], {"child": other})

    pl.semaphore_wait(barrier, len(peers))

    def give0(j, carry):
        y = y_of(j)
        fetch(0, j).wait()
        xb_ref[0, y] = sketch(eo_ref.at[j], 0)
        swap(0, j).start()
        return carry
    lax.fori_loop(0, ny, give0, 0)

    def give1():
        def body(j, carry):
            xb_ref[1, y_of(j)] = sketch(eo_ref.at[j], 1)
            swap(1, j).start()
            return carry
        lax.fori_loop(0, ny, body, 0)

    def keep(h):
        if h == 0:
            pltpu.make_async_copy(em_ref, em_ref, e_sem.at[ny]).wait()

        def body(j, carry):
            h_ref[h, y_of(j)] = sketch(em_ref.at[j], h)
            return carry
        lax.fori_loop(0, ny, body, 0)

    acts = []
    arrive = {("x", 0, j): 7.0 + 1.4 * j for j in range(ny)}
    acts.append(Act("keep0", functools.partial(keep, 0), cost=2.0, prio=-2))
    acts.append(Act("give1", give1, after=["keep0"], cost=2.0, prio=0.5,
                    sends=[(("x", 1, j), "c", 1.4, 0.5) for j in range(ny)]))
    acts.append(Act("keep1", functools.partial(keep, 1), after=["give1"], cost=2.0, prio=0.6))

    def presum(h, j):
        def run():
            swap(h, j).wait_recv()
            y = y_of(j)

            def body(z, carry):
                h_ref[h, y, z] = h_ref[h, y, z] + r_ref[h, y, z]
                return carry
            lax.fori_loop(0, nz, body, 0)
        acts.append(Act(("pre", h, j), run, after=["keep%d" % h], deps=[("x", h, j)], cost=0.4, prio=h))

    class Ring:
        def __init__(self, tag, axis, n, pos, at, orient, own, own_ix, lead, slot, ssem, rsem, nr):
            self.tag, self.axis, self.n, self.pos, self.at = tag, axis, n, pos, at
            self.hp, self.hm = hops(n, orient)
            self.own, self.own_ix, self.lead = own, own_ix, lead
            self.slot, self.ssem, self.rsem = slot, ssem, rsem
            self.size = lead * nr * K * 4
            self.groups = self.group()

        def group(self):
            last = self.last_slots()
            return [last] + [[m] for m in range(self.n - 1) if m not in last]

        def sem_of(self, m):
            return self.rsem([m in g for g in self.groups].index(True))

        def wait(self, which):
            ref, h = self.slot
            if self.groups[which]:
                span = ref.at[h, pl.ds(0, len(self.groups[which]))]
                remote(span, span, self.ssem, self.rsem(which), {"child": other}).wait_recv()

        def wait_for(self, m):
            self.wait([m in g for g in self.groups].index(True))

        def cost(self):
            return 0.06 + 1.6e-3 * self.size / 4096

        def reach(self, sign):
            return self.hp if sign > 0 else self.hm

        def index(self, sign, s):
            return s if sign > 0 else self.hp + s

        def key(self, sign, s):
            return self.tag + (self.index(sign, s),)

        def load_out(self, sign, s):
            link = self.axis + ("+" if sign > 0 else "-")
            return (self.key(sign, s), link, self.size / RATE, BASE + HOP)

        def send(self, sign, s):
            n = self.n
            d = lax.rem(self.pos + sign * (self.reach(sign) - s) + n, n)
            dev = self.at(lax.rem(self.pos + sign + n, n))
            m = self.index(sign, s)
            if s:
                self.wait_for(m - 1)
                ref, h = self.slot
                own, oix = self.own_ix

                def body(i, carry):
                    ref[h, m - 1, i] = ref[h, m - 1, i] + own[oix(d, i)]
                    return carry
                lax.fori_loop(0, self.lead, body, 0)
                src = ref.at[h, m - 1]
            else:
                src = self.own(d)
            ref, h = self.slot
            put(src, ref.at[h, m], self.ssem, self.sem_of(m), dev)

        def last(self):
            return [(sign, self.reach(sign) - 1) for sign in (1, -1) if self.reach(sign)]

        def finish(self):
            ref, h = self.slot
            own, oix = self.own_ix
            last = self.last_slots()
            self.wait(0)

            def body(i, carry):
                total = own[oix(self.pos, i)]
                for m in last:
                    total = total + ref[h, m, i]
                own[oix(self.pos, i)] = total
                return carry
            lax.fori_loop(0, self.lead, body, 0)

        def chain(self, before, prio):
            for sign in (1, -1):
                prev = before
                for s in range(1, self.reach(sign)):
                    name = self.tag + (sign, s)
                    acts.append(Act(name, functools.partial(self.send, sign, s), after=[prev],
                                    deps=[self.key(sign, s - 1)], sends=[self.load_out(sign, s)],
                                    cost=self.cost(), prio=prio))
                    prev = name

        def ends(self):
            return [self.tag + (m,) for m in self.last_slots()]

        def start(self):
            for sign in (1, -1):
                if self.reach(sign):
                    self.send(sign, 0)

        def first_sends(self):
            return [self.load_out(sg, 0) for sg in (1, -1) if self.reach(sg)]

        def more(self, before, prio):
            self.chain(before, prio)
            return [before]

        def last_slots(self):
            return [self.index(*e) for e in self.last()]

    class Direct(Ring):
        def start(self):
            ref, h = self.slot
            for j in range(1, self.n):
                d = lax.rem(self.pos + j, self.n)
                put(self.own(d), ref.at[h, j - 1], self.ssem, self.sem_of(j - 1), self.at(d))

        def first_sends(self):
            out = []
            for j in range(1, self.n):
                hop = min(j, self.n - j)
                link = self.axis + ("+" if j <= self.n // 2 else "-")
                out.append((self.tag + (j - 1,), link, hop * self.size / RATE, BASE + HOP + FAR * (hop - 1)))
            return out

        def more(self, before, prio):
            return [before]

        def last_slots(self):
            return list(range(self.n - 1))

    class Tree(Direct):
        FIRST = ((0, 2, 4), (1, 1, 3), (2, 1, 1), (3, -1, -3), (4, -1, -1))
        SECOND = ((5, 2, (0, 1)), (6, -2, (3,)))

        def sign(self):
            return 1 if self.hp >= self.hm else -1

        def go(self, m, off, src):
            ref, h = self.slot
            dev = lax.rem(self.pos + self.sign() * off + self.n, self.n)
            put(src, ref.at[h, m], self.ssem, self.sem_of(m), self.at(dev))

        def sim(self, m, off):
            link = self.axis + ("+" if off * self.sign() > 0 else "-")
            hop = abs(off)
            return (self.tag + (m,), link, hop * self.size / RATE, BASE + HOP + FAR * (hop - 1))

        def start(self):
            for m, off, piece in self.FIRST:
                d = lax.rem(self.pos + self.sign() * piece + self.n, self.n)
                self.go(m, off, self.own(d))

        def first_sends(self):
            return [self.sim(m, off) for m, off, _ in self.FIRST]

        def second(self, m, off, got):
            ref, h = self.slot
            own, oix = self.own_ix
            d = lax.rem(self.pos + self.sign() * off + self.n, self.n)
            total = own[oix(d, 0)]
            self.wait_for(got[0])
            for g in got:
                total = total + ref[h, g, 0]
            ref[h, got[0], 0] = total
            self.go(m, off, ref.at[h, got[0]])

        def more(self, before, prio):
            names = [before]
            for m, off, got in self.SECOND:
                name = self.tag + ("second", m)
                acts.append(Act(name, functools.partial(self.second, m, off, got), after=[before],
                                deps=[self.tag + (g,) for g in got], sends=[self.sim(m, off)],
                                cost=0.08, prio=prio))
                names.append(name)
            return names

        def last_slots(self):
            return [2, 4, 5, 6]

        def group(self):
            return [self.last_slots(), [0, 1], [3]]

    def flow(h, i):
        color, r0, nr, orient = sets[i]
        rs = pl.ds(r0, nr)
        sems = (s1.at[i], lambda m: got1[i].at[h, m])
        sems2 = (s2.at[i], lambda m: got2[i].at[h, m])
        t1, t2 = ("f", h, i, 1), ("f", h, i, 2)
        if color == "Y":
            first = Ring(t1, "y", ny, my_y, at_y, orient,
                         lambda d: h_ref.at[h, d, :, rs, :],
                         (h_ref, lambda d, j: (h, d, j, rs, slice(None))), nz, (slots1[i], h), *sems, nr)
            second = (Tree if nz == 8 else Ring)(t2, "z", nz, my_z, at_z, orient,
                          lambda d: h_ref.at[h, my_y, pl.ds(d, 1), rs, :],
                          (h_ref, lambda d, j: (h, my_y, d, rs, slice(None))), 1, (slots2[i], h), *sems2, nr)
        else:
            first = Ring(t1, "z", nz, my_z, at_z, orient,
                         lambda d: h_ref.at[h, :, d, rs, :],
                         (h_ref, lambda d, j: (h, j, d, rs, slice(None))), ny, (slots1[i], h), *sems, nr)
            second = Direct(t2, "y", ny, my_y, at_y, orient,
                          lambda d: h_ref.at[h, pl.ds(d, 1), my_z, rs, :],
                          (h_ref, lambda d, j: (h, d, my_z, rs, slice(None))), 1, (slots2[i], h), *sems2, nr)
        if h:
            sent.extend((ring.ssem, buf) for ring, buf in ((first, slots1[i]), (second, slots2[i])) if ring.n > 1)
        prio = 10 * h
        starts = []
        for sign in (1, -1):
            if not first.reach(sign):
                continue
            if color == "Y":
                rel = (sign * first.reach(sign)) % ny
                need = [("pre", h, (ny // 2 - rel) % ny)]
            else:
                need = [("pre", h, j) for j in range(ny)]
            if h:
                need = need + [("f", 0) + g for g in gate(i, sets)]
            name = t1 + (sign, 0)
            starts.append(name)
            acts.append(Act(name, functools.partial(first.send, sign, 0), after=need,
                            sends=[first.load_out(sign, 0)], cost=0.03,
                            prio=prio + 1 - 0.1 * first.reach(sign)))
        for sign in (1, -1):
            prev = t1 + (sign, 0)
            for s in range(1, first.reach(sign)):
                name = t1 + (sign, s)
                acts.append(Act(name, functools.partial(first.send, sign, s),
                                after=[prev] + [("pre", h, j) for j in range(ny)],
                                deps=[first.key(sign, s - 1)], sends=[first.load_out(sign, s)],
                                cost=first.cost(), prio=prio))
                prev = name

        def middle():
            first.finish()
            second.start()
        mid = t1 + ("mid",)
        acts.append(Act(mid, middle, after=starts + [("pre", h, j) for j in range(ny)], deps=first.ends(),
                        sends=second.first_sends(), cost=0.06 + first.cost(), prio=prio))
        before = second.more(mid, prio)
        end = t2 + ("end",)

        def finish():
            second.finish()
            ypad[pl.ds(r0, nr), h * K:(h + 1) * K] = h_ref[h, my_y, my_z, r0:r0 + nr, :]
        acts.append(Act(end, finish, after=before, deps=second.ends(), cost=0.1, prio=prio))
        return end

    def gram_sum(h, ready):
        t = ("g", h)
        piece = gz.shape[2] * K * 4

        def sem(i):
            return as_.at[h, i], ar_.at[h, i]

        def wait(i, buf):
            remote(buf, buf, *sem(i), {"child": other}).wait_recv()

        def total_of(start, parts, count):
            for j in range(count):
                start = start + parts[h, j]
            return start

        def lag(j, n):
            hop = min(j, n - j)
            return BASE + HOP + FAR * (hop - 1), hop * piece / RATE

        def zlink(j):
            return "z+" if j <= nz // 2 else "z-"

        def a0():
            first_t = jnp.transpose(ypad[:, 0:K])
            gloc[h] = mm(first_t, ypad[:, h * K:(h + 1) * K]).reshape(gloc.shape[1:])
            put(gloc.at[h, other], gpart.at[h], *sem(0), {"child": other})

        def a1():
            wait(0, gpart.at[h])
            gz[h] = (gloc[h, c] + gpart[h]).reshape(gz.shape[1:])
            for j in zorder:
                z = lax.rem(my_z + j, nz)
                put(gz.at[h, z], zr.at[h, j - 1], *sem(1), at_z(z))

        def a2():
            wait(1, zr.at[h])
            total = total_of(gz[h, my_z], zr, nz - 1)
            gs[h] = total
            for j in range(1, ny):
                y = lax.rem(my_y + j, ny)
                put(gs.at[h], yr.at[h, j - 1], *sem(2), at_y(y))

        def a3():
            if ny > 1:
                wait(2, yr.at[h])
            total = total_of(gs[h], yr, ny - 1)
            gf[h, c, my_z] = total
            for j in zorder:
                z = lax.rem(my_z + j, nz)
                put(gf.at[h, c, my_z], gf.at[h, c, my_z], *sem(3), at_z(z))

        def a4():
            wait(3, zr.at[h])
            put(gf.at[h, c], gf.at[h, c], *sem(4), {"child": other})

        def a5():
            wait(4, gf.at[h, c])

        for i, buf in enumerate((gpart, zr, yr, zr, gpart)):
            if i != 2 or ny > 1:
                sent.append((as_.at[h, i], buf.at[h]))
        zorder = sorted(range(1, nz), key=lambda j: -min(j, nz - j))
        acts.append(Act(t + (0,), a0, after=ready, sends=[(t + ("p",), "c", 0.3, 1.0)], cost=1.2, prio=5))
        acts.append(Act(t + (1,), a1, after=[t + (0,)], deps=[t + ("p",)], prio=5,
                        sends=[(t + ("z", j), zlink(j), lag(j, nz)[1], lag(j, nz)[0]) for j in zorder]))
        acts.append(Act(t + (2,), a2, after=[t + (1,)], deps=[t + ("z", j) for j in zorder], prio=5,
                        sends=[(t + ("y", j), "y+" if j <= ny // 2 else "y-", lag(j, ny)[1], lag(j, ny)[0])
                               for j in range(1, ny)]))
        acts.append(Act(t + (3,), a3, after=[t + (2,)], deps=[t + ("y", j) for j in range(1, ny)], prio=5,
                        sends=[(t + ("w", j), zlink(j), lag(j, nz)[1], lag(j, nz)[0]) for j in zorder]))
        acts.append(Act(t + (4,), a4, after=[t + (3,)], deps=[t + ("w", j) for j in zorder],
                        sends=[(t + ("v",), "c", 0.3, 1.0)], cost=0.05, prio=5))
        acts.append(Act(t + (5,), a5, after=[t + (4,)], deps=[t + ("v",)], cost=0.02, prio=6))
        return t + (5,)

    sub = lax.broadcasted_iota(jnp.int32, (BLK, BLK), 0)
    lane = lax.broadcasted_iota(jnp.int32, (BLK, BLK), 1)

    def chol_begin():
        aug_ref[:, 0:K] = gf[0].reshape(K, K) * scale
        big = lax.broadcasted_iota(jnp.int32, (K, K), 0) == lax.broadcasted_iota(jnp.int32, (K, K), 1)
        aug_ref[:, K:2 * K] = jnp.where(big, 1.0, 0.0)

    def chol_block(b):
        lo, hi = b * BLK, (b + 1) * BLK
        both = jnp.concatenate([aug_ref[lo:hi, lo:hi], jnp.where(sub == lane, 1.0, 0.0)], axis=1)
        d = [both[8 * g:8 * g + 8, :] for g in range(BLK // 8)]
        sub8 = lax.broadcasted_iota(jnp.int32, (8, 2 * BLK), 0)
        lane8 = lax.broadcasted_iota(jnp.int32, (8, 2 * BLK), 1)
        for p in range(0, BLK, 2):
            g0, q = p // 8, p % 8
            row0, row1 = d[g0][q:q + 1, :], d[g0][q + 1:q + 2, :]
            col0 = [jnp.broadcast_to(x[:, p:p + 1], x.shape) for x in d[g0:]]
            col1 = [jnp.broadcast_to(x[:, p + 1:p + 2], x.shape) for x in d[g0:]]
            aa, ab, bb = col0[0][q:q + 1, :], col0[0][q + 1:q + 2, :], col1[0][q + 1:q + 2, :]
            inv_det = 1.0 / (aa * bb - ab * ab)
            mix0 = (bb * inv_det) * row0 - (ab * inv_det) * row1
            mix1 = (aa * inv_det) * row1 - (ab * inv_det) * row0
            for g in range(g0, BLK // 8):
                x0, x1 = col0[g - g0], col1[g - g0]
                if g == g0:
                    if q == 6:
                        continue
                    x0 = jnp.where(sub8 > q + 1, x0, 0.0)
                    x1 = jnp.where(sub8 > q + 1, x1, 0.0)
                d[g] = d[g] - (x0 * mix0 + x1 * mix1)
        out = []
        for g in range(BLK // 8):
            me = sub8 + 8 * g
            diag = jnp.sum(jnp.where(lane8 == me, d[g], 0.0), axis=1, keepdims=True)
            side = jnp.where((lane8 == me - 1) & (sub8 % 2 == 1), d[g], 0.0)
            side = jnp.sum(side, axis=1, keepdims=True)
            wide = jnp.broadcast_to(diag, d[g].shape)
            lift = side / pltpu.roll(wide, 1, 0)
            full = d[g] - lift * pltpu.roll(d[g], 1, 0)
            out.append(full * (1.0 / jnp.sqrt(wide - lift * side)))
        inv = jnp.concatenate(out, axis=0)[:, BLK:2 * BLK]
        left, right = (0, K + TILE) if hi <= TILE else (TILE, 2 * K)
        z = mm(inv, aug_ref[lo:hi, left:right])
        aug_ref[lo:hi, left:right] = z
        if hi < K:
            base = hi // TILE * TILE
            u = jnp.transpose(aug_ref[lo:hi, base:K])[hi - base:, :]
            aug_ref[hi:K, left:right] = aug_ref[hi:K, left:right] - mm(u, z)

    def basis():
        w = aug_ref[:, K:2 * K]
        q = mm(ypad[:, 0:K], w, (((1,), (1,)), ((), ())))
        q_ref[...] = q[0:rows, :]
        qw_ref[...] = mm(q[0:rows, :], w) * scale

    def fresh():
        g_ref[...] = gf[1].reshape(K, K)
        y2_ref[...] = ypad[0:rows, K:2 * K]

    for h in range(2):
        for j in range(ny):
            presum(h, j)
    ends = [[flow(h, i) for i in range(nsets)] for h in range(2)]
    g1 = gram_sum(0, ends[0])
    g2 = gram_sum(1, ends[0] + ends[1])
    acts.append(Act("chol", chol_begin, after=[g1], cost=0.3, idle=True))
    prev = "chol"
    for b in range(K // BLK):
        acts.append(Act(("chol", b), functools.partial(chol_block, b), after=[prev], cost=3.3, idle=True))
        prev = ("chol", b)
    acts.append(Act("basis", basis, after=[prev], cost=2.0, idle=True))
    acts.append(Act("fresh", fresh, after=["basis", g2], cost=0.3))
    for _, act in arrange(acts, 7.0, arrive):
        act.run()
    sent.append((xs.at[0], xb_ref))
    for sem, buf in sent:
        remote(buf, buf, sem, sem, {"child": other}).wait_send()


def fused(expanded, child_map, seeds, ny, nz, rows, leaf_rows):
    sets = row_sets(rows)
    block_cols = expanded.shape[1]
    vm = pltpu.VMEM
    bf = jnp.bfloat16
    slots1 = [vm((2, max(1, (ny if s[0] == "Y" else nz) - 1), nz if s[0] == "Y" else ny, s[2], K), F32) for s in sets]
    slots2 = [vm((2, max(1, (nz if s[0] == "Y" else ny) - 1), 1, s[2], K), F32) for s in sets]
    dma = pltpu.SemaphoreType.DMA

    def groups(n):
        return max(1, n - 1 - sum(1 for r in hops(n, 0) if r) + 1)

    piece = K // 2 // nz
    chunk = nz * rows
    out = jax.ShapeDtypeStruct((rows, K), F32)
    return pl.pallas_call(
        functools.partial(fused_kernel, ny, nz, rows, 1.0 / leaf_rows),
        out_shape=(out, out, out, jax.ShapeDtypeStruct((K, K), F32)),
        in_specs=[
            pl.BlockSpec(memory_space=pltpu.SMEM),
            pl.BlockSpec(memory_space=pltpu.VMEM),
            pl.BlockSpec(memory_space=pl.ANY),
        ],
        out_specs=[pl.BlockSpec(memory_space=pltpu.VMEM)] * 4,
        scratch_shapes=[
            *slots1, *slots2,
            *[dma((2, groups(ny if s[0] == "Y" else nz))) for s in sets],
            *[dma((2, 3 if s[0] == "Y" and nz == 8 else groups(nz) if s[0] == "Y" else 1)) for s in sets],
            vm((2 * K, block_cols), bf),
            vm((ny, chunk, block_cols), bf), vm((ny, chunk, block_cols), bf),
            vm((2, ny, nz, rows, K), F32), vm((2, ny, nz, rows, K), F32), vm((2, ny, nz, rows, K), F32),
            vm((TILE, 2 * K), F32), vm((2, 2, K // 2, K), F32), vm((2, K // 2, K), F32),
            vm((2, nz, piece, K), F32), vm((2, nz - 1, piece, K), F32), vm((2, piece, K), F32),
            vm((2, max(1, ny - 1), piece, K), F32), vm((2, 2, nz, piece, K), F32),
            vm((K, 2 * K), F32),
            dma((ny + 1,)), dma((1,)), dma((2, ny)),
            dma((len(sets),)), dma((len(sets),)), dma((2, 5)), dma((2, 5)),
        ],
        compiler_params=pltpu.CompilerParams(
            collective_id=0, has_side_effects=True, vmem_limit_bytes=63 << 20),
    )(seeds, child_map, expanded.reshape(2, ny, chunk, block_cols))


def finish_kernel(q_ref, y2_ref, qw_ref, g_ref, q_out, f_out):
    q_out[...] = q_ref[...]
    f_out[...] = y2_ref[...] - mm(qw_ref[...], g_ref[...])


def finish(q, y2, qw, g):
    out = jax.ShapeDtypeStruct(q.shape, F32)
    return pl.pallas_call(
        finish_kernel,
        out_shape=(out, out),
        in_specs=[pl.BlockSpec(memory_space=pltpu.VMEM)] * 4,
        out_specs=[pl.BlockSpec(memory_space=pltpu.VMEM)] * 2,
        compiler_params=pltpu.CompilerParams(vmem_limit_bytes=63 << 20),
    )(q, y2, qw, g)


def make_body(parent_rows):
    def body(schur_blocks, child_map, round_seeds):
        col_count = lax.axis_size("col")
        ny, nz = GRIDS[col_count]
        leaf_rows = parent_rows // lax.axis_size("row")
        own_rows = leaf_rows // (2 * col_count)
        expanded = expand_rows(schur_blocks[0], child_map, leaf_rows)
        return finish(*fused(expanded, child_map, round_seeds, ny, nz, own_rows, leaf_rows))
    return body


def solution(mesh, parent_rows=24576):
    placed = (P("child", "row", "col"), P(), P())
    return jax.shard_map(
        make_body(parent_rows),
        mesh=mesh,
        in_specs=placed,
        out_specs=(P(("row", "child", "col"), None), P(("row", "child", "col"), None)),
        check_vma=False,
    )
```

```python
import functools
import jax
import jax.numpy as jnp
from jax import lax
from jax.experimental import pallas as pl
from jax.experimental.pallas import tpu as pltpu
from jax.sharding import PartitionSpec as P

K = 256
TILE = 128
BLK = 64
GRIDS = {32: (4, 8), 8: (2, 4)}
MESH = pl.DeviceIdType.MESH
F32 = jnp.float32
RATE = 46.0e3
HOP = 0.8
BASE = 1.4
FAR = 0.15
SETS96 = [("Z", 0, 16, 1), ("Y", 16, 8, 1), ("Y", 24, 8, 0), ("Y", 32, 24, 1), ("Z", 56, 8, 1), ("Z", 64, 16, 0), ("Y", 80, 16, 0)]
GATES96 = [[(0, 1, "mid")], [(0, 2, "end")], [(2, 1, "mid")], [(3, 1, "mid")], [(2, 2, "end")], [(5, 1, "mid")], [(5, 2, "end")]]


def gate(i, sets):
    return GATES96[i] if sets == SETS96 else [(i, 1, 'mid')]


def split(x):
    high = x.astype(jnp.bfloat16)
    return high, (x - high.astype(F32)).astype(jnp.bfloat16)


def mm(a, b, dims=(((1,), (0,)), ((), ()))):
    (ah, al), (bh, bl) = split(a), split(b)

    def dot(x, y):
        return lax.dot_general(x, y, dims, preferred_element_type=F32)
    return dot(ah, bh) + (dot(ah, bl) + dot(al, bh))


def hash_values(ids_row, col, seed):
    h = ids_row * 40503 + col * 9973 + seed * 2654435
    h = h ^ ((h >> 15) & 131071)
    h = h * 73244475
    h = h ^ ((h >> 13) & 524287)
    h = h * 1274126177
    h = h ^ ((h >> 16) & 65535)
    unit = (h & 16777215).astype(F32) * (1.0 / 16777216.0)
    return (unit - 0.5) * 3.4641016


def row_sets(rows):
    if rows == 96:
        return SETS96
    q = rows // 4
    return [("Y", 0, q, 0), ("Z", q, q, 0), ("Y", 2 * q, q, 1), ("Z", 3 * q, q, 1)]


def hops(n, orient):
    long, short = n // 2, n - 1 - n // 2
    return (short, long) if orient else (long, short)


class Act:
    def __init__(self, name, run, after=(), deps=(), sends=(), cost=0.25, idle=False, prio=0):
        self.name, self.run, self.after, self.deps = name, run, list(after), list(deps)
        self.sends, self.cost, self.idle, self.prio = list(sends), cost, idle, prio


def arrange(acts, now, arrive):
    arrive, free, done, order = dict(arrive), {}, set(), []
    left = list(acts)
    while left:
        ready = []
        for a in left:
            if all(n in done for n in a.after) and all(d in arrive for d in a.deps):
                ready.append((max([now] + [arrive[d] for d in a.deps]), a.prio, len(ready), a))
        work = [r for r in ready if not r[3].idle]
        spare = [r for r in ready if r[3].idle]
        pick = min(work or spare, key=lambda r: r[:3])
        if work and spare:
            s = min(spare, key=lambda r: r[:3])
            if s[0] + 0.6 * s[3].cost <= pick[0]:
                pick = s
        a = pick[3]
        now = pick[0] + a.cost
        for key, link, size, lag in a.sends:
            free[link] = max(free.get(link, 0.0), now) + size
            arrive[key] = free[link] + lag
        done.add(a.name)
        left.remove(a)
        order.append((now, a))
    return order


STEP_TILES = 8


def expand_kernel(map_ref, a_hbm, e_ref, a_ref, m2_ref, sv_ref, ss_ref, a_sem, sv_sem):
    step = pl.program_id(0)
    block_rows = a_ref.shape[0]
    blocks = block_rows // TILE
    c = lax.axis_index("child")
    row = lax.axis_index("row")
    base = row * (e_ref.shape[0] * pl.num_programs(0))

    size = STEP_TILES * TILE
    parts = block_rows // size

    def load(n):
        rows = pl.ds(n * size, size)
        return pltpu.make_async_copy(a_hbm.at[rows, :], a_ref.at[rows, :], a_sem.at[n])

    @pl.when(step == 0)
    def _():
        for n in range(parts):
            load(n).start()

        def fill(j, carry):
            at = pl.multiple_of(row * block_rows + j * TILE, TILE)
            both = map_ref[:, pl.ds(at, TILE)]
            m2_ref[pl.ds(j, 1), :] = jnp.where(c == 0, both[0:1, :], both[1:2, :])
            return carry
        lax.fori_loop(0, blocks, fill, 0)
        firsts = base + lax.broadcasted_iota(jnp.int32, (blocks, TILE), 1) * TILE
        below = (m2_ref[:, TILE - 1:TILE] < firsts).astype(jnp.int32)
        counts = jnp.minimum(jnp.sum(below, axis=0, keepdims=True), blocks - 2)
        sv_ref[...] = jnp.broadcast_to(counts, sv_ref.shape)
        to_scalar = pltpu.make_async_copy(sv_ref, ss_ref, sv_sem)
        to_scalar.start()
        to_scalar.wait()
        load(0).wait()

    for n in range(1, parts):
        @pl.when(step == n - 1)
        def _():
            load(n).wait()

    for q in range(STEP_TILES):
        t = step * STEP_TILES + q
        b = ss_ref[0, t]
        window = jnp.concatenate([m2_ref[pl.ds(b, 1), :], m2_ref[pl.ds(b + 1, 1), :]], axis=1)
        wanted = lax.broadcasted_iota(jnp.int32, (TILE, 2 * TILE), 0) + (base + t * TILE)
        pick = jnp.where(window == wanted, 1.0, 0.0).astype(jnp.bfloat16)
        src = a_ref[pl.ds(pl.multiple_of(b * TILE, TILE), 2 * TILE), :]
        e_ref[q * TILE:(q + 1) * TILE, :] = jnp.dot(
            pick, src, preferred_element_type=F32).astype(jnp.bfloat16)


def expand_rows(child_block, child_map, leaf_rows):
    block_rows, block_cols = child_block.shape
    bf = jnp.bfloat16
    rows = STEP_TILES * TILE
    return pl.pallas_call(
        expand_kernel,
        grid=(leaf_rows // rows,),
        out_shape=jax.ShapeDtypeStruct((leaf_rows, block_cols), bf),
        in_specs=[pl.BlockSpec(child_map.shape, lambda i: (0, 0)), pl.BlockSpec(memory_space=pl.ANY)],
        out_specs=pl.BlockSpec((rows, block_cols), lambda i: (i, 0)),
        scratch_shapes=[
            pltpu.VMEM((block_rows, block_cols), bf),
            pltpu.VMEM((block_rows // TILE, TILE), jnp.int32), pltpu.VMEM((8, TILE), jnp.int32),
            pltpu.SMEM((8, TILE), jnp.int32),
            pltpu.SemaphoreType.DMA((block_rows // rows,)), pltpu.SemaphoreType.DMA(()),
        ],
        compiler_params=pltpu.CompilerParams(vmem_limit_bytes=63 << 20),
    )(child_map, child_block)


def fused_kernel(ny, nz, rows, scale, seeds_ref, map_ref, e_hbm, q_ref, y2_ref, qw_ref, g_ref, *refs):
    sets = row_sets(rows)
    nsets = len(sets)
    slots1, slots2 = refs[:nsets], refs[nsets:2 * nsets]
    got1, got2 = refs[2 * nsets:3 * nsets], refs[3 * nsets:4 * nsets]
    (st_ref, eo_ref, em_ref, xb_ref, h_ref, r_ref,
     ypad, gloc, gpart, gz, zr, gs, yr, gf, aug_ref,
     e_sem, xs, xr, s1, s2, as_, ar_) = refs[4 * nsets:]

    block_cols = em_ref.shape[2]

    c = lax.axis_index("child")
    k = lax.axis_index("col")
    my_y = k // nz
    my_z = k - my_y * nz
    other = 1 - c

    def at_y(y):
        return {"col": y * nz + my_z}

    def at_z(z):
        return {"col": my_y * nz + z}

    sent = []

    def remote(src, dst, ssem, rsem, dev):
        return pltpu.make_async_remote_copy(
            src_ref=src, dst_ref=dst, send_sem=ssem, recv_sem=rsem,
            device_id=dev, device_id_type=MESH)

    def put(*args):
        cp = remote(*args)
        cp.start()
        return cp

    def y_of(j):
        return lax.rem(my_y + ny // 2 - j + ny, ny)

    def fetch(side, j):
        half, dst = ((other, eo_ref), (c, em_ref))[side]
        return pltpu.make_async_copy(e_hbm.at[half, y_of(j)], dst.at[j], e_sem.at[ny if side else j])

    for side in range(2):
        for j in range(ny):
            fetch(side, j).start()
    barrier = pltpu.get_barrier_semaphore()
    peers = [{"child": other}]
    peers += [at_y(lax.rem(my_y + j, ny)) for j in range(1, ny)]
    peers += [at_z(lax.rem(my_z + j, nz)) for j in range(1, nz)]
    for dev in peers:
        pl.semaphore_signal(barrier, inc=1, device_id=dev, device_id_type=MESH)

    both_ids = map_ref[:, pl.ds(pl.multiple_of(k * block_cols, TILE), block_cols)]
    ids = jnp.where(c == 0, both_ids[0:1, :], both_ids[1:2, :])

    def draw(i, carry):
        j0 = pl.multiple_of(i * 32, 32)
        t = j0 // K
        col = lax.broadcasted_iota(jnp.int32, (32, block_cols), 0) + (j0 - t * K)
        st_ref[pl.ds(j0, 32), :] = hash_values(ids, col, seeds_ref[t]).astype(jnp.bfloat16)
        return carry
    lax.fori_loop(0, 2 * K // 32, draw, 0)
    ypad[...] = jnp.zeros_like(ypad)

    def sketch(e, h):
        return lax.dot_general(
            e[...], st_ref[h * K:(h + 1) * K, :], (((1,), (1,)), ((), ())),
            preferred_element_type=F32).reshape(nz, rows, K)

    def swap(h, j):
        y = y_of(j)
        return remote(xb_ref.at[h, y], r_ref.at[h, y], xs.at[0], xr.at[h, j], {"child": other})

    pl.semaphore_wait(barrier, len(peers))

    def give0(j, carry):
        y = y_of(j)
        fetch(0, j).wait()
        xb_ref[0, y] = sketch(eo_ref.at[j], 0)
        swap(0, j).start()
        return carry
    lax.fori_loop(0, ny, give0, 0)

    def give1():
        def body(j, carry):
            xb_ref[1, y_of(j)] = sketch(eo_ref.at[j], 1)
            swap(1, j).start()
            return carry
        lax.fori_loop(0, ny, body, 0)

    def keep(h):
        if h == 0:
            pltpu.make_async_copy(em_ref, em_ref, e_sem.at[ny]).wait()

        def body(j, carry):
            h_ref[h, y_of(j)] = sketch(em_ref.at[j], h)
            return carry
        lax.fori_loop(0, ny, body, 0)

    acts = []
    arrive = {("x", 0, j): 7.0 + 1.4 * j for j in range(ny)}
    acts.append(Act("keep0", functools.partial(keep, 0), cost=2.0, prio=-2))
    acts.append(Act("give1", give1, after=["keep0"], cost=2.0, prio=0.5,
                    sends=[(("x", 1, j), "c", 1.4, 0.5) for j in range(ny)]))
    acts.append(Act("keep1", functools.partial(keep, 1), after=["give1"], cost=2.0, prio=0.6))

    def presum(h, j):
        def run():
            swap(h, j).wait_recv()
            y = y_of(j)

            def body(z, carry):
                h_ref[h, y, z] = h_ref[h, y, z] + r_ref[h, y, z]
                return carry
            lax.fori_loop(0, nz, body, 0)
        acts.append(Act(("pre", h, j), run, after=["keep%d" % h], deps=[("x", h, j)], cost=0.4, prio=h))

    class Ring:
        def __init__(self, tag, axis, n, pos, at, orient, own, own_ix, lead, slot, ssem, rsem, nr):
            self.tag, self.axis, self.n, self.pos, self.at = tag, axis, n, pos, at
            self.hp, self.hm = hops(n, orient)
            self.own, self.own_ix, self.lead = own, own_ix, lead
            self.slot, self.ssem, self.rsem = slot, ssem, rsem
            self.size = lead * nr * K * 4
            self.groups = self.group()

        def group(self):
            last = self.last_slots()
            return [last] + [[m] for m in range(self.n - 1) if m not in last]

        def sem_of(self, m):
            return self.rsem([m in g for g in self.groups].index(True))

        def wait(self, which):
            ref, h = self.slot
            if self.groups[which]:
                span = ref.at[h, pl.ds(0, len(self.groups[which]))]
                remote(span, span, self.ssem, self.rsem(which), {"child": other}).wait_recv()

        def wait_for(self, m):
            self.wait([m in g for g in self.groups].index(True))

        def cost(self):
            return 0.06 + 1.6e-3 * self.size / 4096

        def reach(self, sign):
            return self.hp if sign > 0 else self.hm

        def index(self, sign, s):
            return s if sign > 0 else self.hp + s

        def key(self, sign, s):
            return self.tag + (self.index(sign, s),)

        def load_out(self, sign, s):
            link = self.axis + ("+" if sign > 0 else "-")
            return (self.key(sign, s), link, self.size / RATE, BASE + HOP)

        def send(self, sign, s):
            n = self.n
            d = lax.rem(self.pos + sign * (self.reach(sign) - s) + n, n)
            dev = self.at(lax.rem(self.pos + sign + n, n))
            m = self.index(sign, s)
            if s:
                self.wait_for(m - 1)
                ref, h = self.slot
                own, oix = self.own_ix

                def body(i, carry):
                    ref[h, m - 1, i] = ref[h, m - 1, i] + own[oix(d, i)]
                    return carry
                lax.fori_loop(0, self.lead, body, 0)
                src = ref.at[h, m - 1]
            else:
                src = self.own(d)
            ref, h = self.slot
            put(src, ref.at[h, m], self.ssem, self.sem_of(m), dev)

        def last(self):
            return [(sign, self.reach(sign) - 1) for sign in (1, -1) if self.reach(sign)]

        def finish(self):
            ref, h = self.slot
            own, oix = self.own_ix
            last = self.last_slots()
            self.wait(0)

            def body(i, carry):
                total = own[oix(self.pos, i)]
                for m in last:
                    total = total + ref[h, m, i]
                own[oix(self.pos, i)] = total
                return carry
            lax.fori_loop(0, self.lead, body, 0)

        def chain(self, before, prio):
            for sign in (1, -1):
                prev = before
                for s in range(1, self.reach(sign)):
                    name = self.tag + (sign, s)
                    acts.append(Act(name, functools.partial(self.send, sign, s), after=[prev],
                                    deps=[self.key(sign, s - 1)], sends=[self.load_out(sign, s)],
                                    cost=self.cost(), prio=prio))
                    prev = name

        def ends(self):
            return [self.tag + (m,) for m in self.last_slots()]

        def start(self):
            for sign in (1, -1):
                if self.reach(sign):
                    self.send(sign, 0)

        def first_sends(self):
            return [self.load_out(sg, 0) for sg in (1, -1) if self.reach(sg)]

        def more(self, before, prio):
            self.chain(before, prio)
            return [before]

        def last_slots(self):
            return [self.index(*e) for e in self.last()]

    class Direct(Ring):
        def start(self):
            ref, h = self.slot
            for j in range(1, self.n):
                d = lax.rem(self.pos + j, self.n)
                put(self.own(d), ref.at[h, j - 1], self.ssem, self.sem_of(j - 1), self.at(d))

        def first_sends(self):
            out = []
            for j in range(1, self.n):
                hop = min(j, self.n - j)
                link = self.axis + ("+" if j <= self.n // 2 else "-")
                out.append((self.tag + (j - 1,), link, hop * self.size / RATE, BASE + HOP + FAR * (hop - 1)))
            return out

        def more(self, before, prio):
            return [before]

        def last_slots(self):
            return list(range(self.n - 1))

    class Tree(Direct):
        FIRST = ((0, 2, 4), (1, 1, 3), (2, 1, 1), (3, -1, -3), (4, -1, -1))
        SECOND = ((5, 2, (0, 1)), (6, -2, (3,)))

        def sign(self):
            return 1 if self.hp >= self.hm else -1

        def go(self, m, off, src):
            ref, h = self.slot
            dev = lax.rem(self.pos + self.sign() * off + self.n, self.n)
            put(src, ref.at[h, m], self.ssem, self.sem_of(m), self.at(dev))

        def sim(self, m, off):
            link = self.axis + ("+" if off * self.sign() > 0 else "-")
            hop = abs(off)
            return (self.tag + (m,), link, hop * self.size / RATE, BASE + HOP + FAR * (hop - 1))

        def start(self):
            for m, off, piece in self.FIRST:
                d = lax.rem(self.pos + self.sign() * piece + self.n, self.n)
                self.go(m, off, self.own(d))

        def first_sends(self):
            return [self.sim(m, off) for m, off, _ in self.FIRST]

        def second(self, m, off, got):
            ref, h = self.slot
            own, oix = self.own_ix
            d = lax.rem(self.pos + self.sign() * off + self.n, self.n)
            total = own[oix(d, 0)]
            self.wait_for(got[0])
            for g in got:
                total = total + ref[h, g, 0]
            ref[h, got[0], 0] = total
            self.go(m, off, ref.at[h, got[0]])

        def more(self, before, prio):
            names = [before]
            for m, off, got in self.SECOND:
                name = self.tag + ("second", m)
                acts.append(Act(name, functools.partial(self.second, m, off, got), after=[before],
                                deps=[self.tag + (g,) for g in got], sends=[self.sim(m, off)],
                                cost=0.08, prio=prio))
                names.append(name)
            return names

        def last_slots(self):
            return [2, 4, 5, 6]

        def group(self):
            return [self.last_slots(), [0, 1], [3]]

    def flow(h, i):
        color, r0, nr, orient = sets[i]
        rs = pl.ds(r0, nr)
        sems = (s1.at[i], lambda m: got1[i].at[h, m])
        sems2 = (s2.at[i], lambda m: got2[i].at[h, m])
        t1, t2 = ("f", h, i, 1), ("f", h, i, 2)
        if color == "Y":
            first = Ring(t1, "y", ny, my_y, at_y, orient,
                         lambda d: h_ref.at[h, d, :, rs, :],
                         (h_ref, lambda d, j: (h, d, j, rs, slice(None))), nz, (slots1[i], h), *sems, nr)
            second = (Tree if nz == 8 else Ring)(t2, "z", nz, my_z, at_z, orient,
                          lambda d: h_ref.at[h, my_y, pl.ds(d, 1), rs, :],
                          (h_ref, lambda d, j: (h, my_y, d, rs, slice(None))), 1, (slots2[i], h), *sems2, nr)
        else:
            first = Ring(t1, "z", nz, my_z, at_z, orient,
                         lambda d: h_ref.at[h, :, d, rs, :],
                         (h_ref, lambda d, j: (h, j, d, rs, slice(None))), ny, (slots1[i], h), *sems, nr)
            second = Direct(t2, "y", ny, my_y, at_y, orient,
                          lambda d: h_ref.at[h, pl.ds(d, 1), my_z, rs, :],
                          (h_ref, lambda d, j: (h, d, my_z, rs, slice(None))), 1, (slots2[i], h), *sems2, nr)
        if h:
            sent.extend((ring.ssem, buf) for ring, buf in ((first, slots1[i]), (second, slots2[i])) if ring.n > 1)
        prio = 10 * h
        starts = []
        for sign in (1, -1):
            if not first.reach(sign):
                continue
            if color == "Y":
                rel = (sign * first.reach(sign)) % ny
                need = [("pre", h, (ny // 2 - rel) % ny)]
            else:
                need = [("pre", h, j) for j in range(ny)]
            if h:
                need = need + [("f", 0) + g for g in gate(i, sets)]
            name = t1 + (sign, 0)
            starts.append(name)
            acts.append(Act(name, functools.partial(first.send, sign, 0), after=need,
                            sends=[first.load_out(sign, 0)], cost=0.03,
                            prio=prio + 1 - 0.1 * first.reach(sign)))
        for sign in (1, -1):
            prev = t1 + (sign, 0)
            for s in range(1, first.reach(sign)):
                name = t1 + (sign, s)
                acts.append(Act(name, functools.partial(first.send, sign, s),
                                after=[prev] + [("pre", h, j) for j in range(ny)],
                                deps=[first.key(sign, s - 1)], sends=[first.load_out(sign, s)],
                                cost=first.cost(), prio=prio))
                prev = name

        def middle():
            first.finish()
            second.start()
        mid = t1 + ("mid",)
        acts.append(Act(mid, middle, after=starts + [("pre", h, j) for j in range(ny)], deps=first.ends(),
                        sends=second.first_sends(), cost=0.06 + first.cost(), prio=prio))
        before = second.more(mid, prio)
        end = t2 + ("end",)

        def finish():
            second.finish()
            ypad[pl.ds(r0, nr), h * K:(h + 1) * K] = h_ref[h, my_y, my_z, r0:r0 + nr, :]
        acts.append(Act(end, finish, after=before, deps=second.ends(), cost=0.1, prio=prio))
        return end

    def gram_sum(h, ready):
        t = ("g", h)
        piece = gz.shape[2] * K * 4

        def sem(i):
            return as_.at[h, i], ar_.at[h, i]

        def wait(i, buf):
            remote(buf, buf, *sem(i), {"child": other}).wait_recv()

        def total_of(start, parts, count):
            for j in range(count):
                start = start + parts[h, j]
            return start

        def lag(j, n):
            hop = min(j, n - j)
            return BASE + HOP + FAR * (hop - 1), hop * piece / RATE

        def zlink(j):
            return "z+" if j <= nz // 2 else "z-"

        def a0():
            first_t = jnp.transpose(ypad[:, 0:K])
            gloc[h] = mm(first_t, ypad[:, h * K:(h + 1) * K]).reshape(gloc.shape[1:])
            put(gloc.at[h, other], gpart.at[h], *sem(0), {"child": other})

        def a1():
            wait(0, gpart.at[h])
            gz[h] = (gloc[h, c] + gpart[h]).reshape(gz.shape[1:])
            for j in zorder:
                z = lax.rem(my_z + j, nz)
                put(gz.at[h, z], zr.at[h, j - 1], *sem(1), at_z(z))

        def a2():
            wait(1, zr.at[h])
            total = total_of(gz[h, my_z], zr, nz - 1)
            gs[h] = total
            for j in range(1, ny):
                y = lax.rem(my_y + j, ny)
                put(gs.at[h], yr.at[h, j - 1], *sem(2), at_y(y))

        def a3():
            if ny > 1:
                wait(2, yr.at[h])
            total = total_of(gs[h], yr, ny - 1)
            gf[h, c, my_z] = total
            for j in zorder:
                z = lax.rem(my_z + j, nz)
                put(gf.at[h, c, my_z], gf.at[h, c, my_z], *sem(3), at_z(z))

        def a4():
            wait(3, zr.at[h])
            put(gf.at[h, c], gf.at[h, c], *sem(4), {"child": other})

        def a5():
            wait(4, gf.at[h, c])

        for i, buf in enumerate((gpart, zr, yr, zr, gpart)):
            if i != 2 or ny > 1:
                sent.append((as_.at[h, i], buf.at[h]))
        zorder = sorted(range(1, nz), key=lambda j: -min(j, nz - j))
        acts.append(Act(t + (0,), a0, after=ready, sends=[(t + ("p",), "c", 0.3, 1.0)], cost=1.2, prio=5))
        acts.append(Act(t + (1,), a1, after=[t + (0,)], deps=[t + ("p",)], prio=5,
                        sends=[(t + ("z", j), zlink(j), lag(j, nz)[1], lag(j, nz)[0]) for j in zorder]))
        acts.append(Act(t + (2,), a2, after=[t + (1,)], deps=[t + ("z", j) for j in zorder], prio=5,
                        sends=[(t + ("y", j), "y+" if j <= ny // 2 else "y-", lag(j, ny)[1], lag(j, ny)[0])
                               for j in range(1, ny)]))
        acts.append(Act(t + (3,), a3, after=[t + (2,)], deps=[t + ("y", j) for j in range(1, ny)], prio=5,
                        sends=[(t + ("w", j), zlink(j), lag(j, nz)[1], lag(j, nz)[0]) for j in zorder]))
        acts.append(Act(t + (4,), a4, after=[t + (3,)], deps=[t + ("w", j) for j in zorder],
                        sends=[(t + ("v",), "c", 0.3, 1.0)], cost=0.05, prio=5))
        acts.append(Act(t + (5,), a5, after=[t + (4,)], deps=[t + ("v",)], cost=0.02, prio=6))
        return t + (5,)

    sub = lax.broadcasted_iota(jnp.int32, (BLK, BLK), 0)
    lane = lax.broadcasted_iota(jnp.int32, (BLK, BLK), 1)

    def chol_begin():
        aug_ref[:, 0:K] = gf[0].reshape(K, K) * scale
        big = lax.broadcasted_iota(jnp.int32, (K, K), 0) == lax.broadcasted_iota(jnp.int32, (K, K), 1)
        aug_ref[:, K:2 * K] = jnp.where(big, 1.0, 0.0)

    def chol_block(b):
        lo, hi = b * BLK, (b + 1) * BLK
        both = jnp.concatenate([aug_ref[lo:hi, lo:hi], jnp.where(sub == lane, 1.0, 0.0)], axis=1)
        d = [both[8 * g:8 * g + 8, :] for g in range(BLK // 8)]
        sub8 = lax.broadcasted_iota(jnp.int32, (8, 2 * BLK), 0)
        lane8 = lax.broadcasted_iota(jnp.int32, (8, 2 * BLK), 1)
        for p in range(0, BLK, 2):
            g0, q = p // 8, p % 8
            row0, row1 = d[g0][q:q + 1, :], d[g0][q + 1:q + 2, :]
            col0 = [jnp.broadcast_to(x[:, p:p + 1], x.shape) for x in d[g0:]]
            col1 = [jnp.broadcast_to(x[:, p + 1:p + 2], x.shape) for x in d[g0:]]
            aa, ab, bb = col0[0][q:q + 1, :], col0[0][q + 1:q + 2, :], col1[0][q + 1:q + 2, :]
            inv_det = 1.0 / (aa * bb - ab * ab)
            mix0 = (bb * inv_det) * row0 - (ab * inv_det) * row1
            mix1 = (aa * inv_det) * row1 - (ab * inv_det) * row0
            for g in range(g0, BLK // 8):
                x0, x1 = col0[g - g0], col1[g - g0]
                if g == g0:
                    if q == 6:
                        continue
                    x0 = jnp.where(sub8 > q + 1, x0, 0.0)
                    x1 = jnp.where(sub8 > q + 1, x1, 0.0)
                d[g] = d[g] - (x0 * mix0 + x1 * mix1)
        out = []
        for g in range(BLK // 8):
            me = sub8 + 8 * g
            diag = jnp.sum(jnp.where(lane8 == me, d[g], 0.0), axis=1, keepdims=True)
            side = jnp.where((lane8 == me - 1) & (sub8 % 2 == 1), d[g], 0.0)
            side = jnp.sum(side, axis=1, keepdims=True)
            wide = jnp.broadcast_to(diag, d[g].shape)
            lift = side / pltpu.roll(wide, 1, 0)
            full = d[g] - lift * pltpu.roll(d[g], 1, 0)
            out.append(full * (1.0 / jnp.sqrt(wide - lift * side)))
        inv = jnp.concatenate(out, axis=0)[:, BLK:2 * BLK]
        left, right = (0, K + TILE) if hi <= TILE else (TILE, 2 * K)
        z = mm(inv, aug_ref[lo:hi, left:right])
        aug_ref[lo:hi, left:right] = z
        if hi < K:
            base = hi // TILE * TILE
            u = jnp.transpose(aug_ref[lo:hi, base:K])[hi - base:, :]
            aug_ref[hi:K, left:right] = aug_ref[hi:K, left:right] - mm(u, z)

    def basis():
        w = aug_ref[:, K:2 * K]
        q = mm(ypad[:, 0:K], w, (((1,), (1,)), ((), ())))
        q_ref[...] = q[0:rows, :]
        qw_ref[...] = mm(q[0:rows, :], w) * scale

    def fresh():
        g_ref[...] = gf[1].reshape(K, K)
        y2_ref[...] = ypad[0:rows, K:2 * K]

    for h in range(2):
        for j in range(ny):
            presum(h, j)
    ends = [[flow(h, i) for i in range(nsets)] for h in range(2)]
    g1 = gram_sum(0, ends[0])
    g2 = gram_sum(1, ends[0] + ends[1])
    acts.append(Act("chol", chol_begin, after=[g1], cost=0.3, idle=True))
    prev = "chol"
    for b in range(K // BLK):
        acts.append(Act(("chol", b), functools.partial(chol_block, b), after=[prev], cost=3.3, idle=True))
        prev = ("chol", b)
    acts.append(Act("basis", basis, after=[prev], cost=2.0, idle=True))
    acts.append(Act("fresh", fresh, after=["basis", g2], cost=0.3))
    for _, act in arrange(acts, 7.0, arrive):
        act.run()
    sent.append((xs.at[0], xb_ref))
    for sem, buf in sent:
        remote(buf, buf, sem, sem, {"child": other}).wait_send()


def fused(expanded, child_map, seeds, ny, nz, rows, leaf_rows):
    sets = row_sets(rows)
    block_cols = expanded.shape[1]
    vm = pltpu.VMEM
    bf = jnp.bfloat16
    slots1 = [vm((2, max(1, (ny if s[0] == "Y" else nz) - 1), nz if s[0] == "Y" else ny, s[2], K), F32) for s in sets]
    slots2 = [vm((2, max(1, (nz if s[0] == "Y" else ny) - 1), 1, s[2], K), F32) for s in sets]
    dma = pltpu.SemaphoreType.DMA

    def groups(n):
        return max(1, n - 1 - sum(1 for r in hops(n, 0) if r) + 1)

    piece = K // 2 // nz
    chunk = nz * rows
    out = jax.ShapeDtypeStruct((rows, K), F32)
    return pl.pallas_call(
        functools.partial(fused_kernel, ny, nz, rows, 1.0 / leaf_rows),
        out_shape=(out, out, out, jax.ShapeDtypeStruct((K, K), F32)),
        in_specs=[
            pl.BlockSpec(memory_space=pltpu.SMEM),
            pl.BlockSpec(memory_space=pltpu.VMEM),
            pl.BlockSpec(memory_space=pl.ANY),
        ],
        out_specs=[pl.BlockSpec(memory_space=pltpu.VMEM)] * 4,
        scratch_shapes=[
            *slots1, *slots2,
            *[dma((2, groups(ny if s[0] == "Y" else nz))) for s in sets],
            *[dma((2, 3 if s[0] == "Y" and nz == 8 else groups(nz) if s[0] == "Y" else 1)) for s in sets],
            vm((2 * K, block_cols), bf),
            vm((ny, chunk, block_cols), bf), vm((ny, chunk, block_cols), bf),
            vm((2, ny, nz, rows, K), F32), vm((2, ny, nz, rows, K), F32), vm((2, ny, nz, rows, K), F32),
            vm((TILE, 2 * K), F32), vm((2, 2, K // 2, K), F32), vm((2, K // 2, K), F32),
            vm((2, nz, piece, K), F32), vm((2, nz - 1, piece, K), F32), vm((2, piece, K), F32),
            vm((2, max(1, ny - 1), piece, K), F32), vm((2, 2, nz, piece, K), F32),
            vm((K, 2 * K), F32),
            dma((ny + 1,)), dma((1,)), dma((2, ny)),
            dma((len(sets),)), dma((len(sets),)), dma((2, 5)), dma((2, 5)),
        ],
        compiler_params=pltpu.CompilerParams(
            collective_id=0, has_side_effects=True, vmem_limit_bytes=63 << 20),
    )(seeds, child_map, expanded.reshape(2, ny, chunk, block_cols))


def finish_kernel(q_ref, y2_ref, qw_ref, g_ref, q_out, f_out):
    q_out[...] = q_ref[...]
    f_out[...] = y2_ref[...] - mm(qw_ref[...], g_ref[...])


def finish(q, y2, qw, g):
    out = jax.ShapeDtypeStruct(q.shape, F32)
    return pl.pallas_call(
        finish_kernel,
        out_shape=(out, out),
        in_specs=[pl.BlockSpec(memory_space=pltpu.VMEM)] * 4,
        out_specs=[pl.BlockSpec(memory_space=pltpu.VMEM)] * 2,
        compiler_params=pltpu.CompilerParams(vmem_limit_bytes=63 << 20),
    )(q, y2, qw, g)


def make_body(parent_rows):
    def body(schur_blocks, child_map, round_seeds):
        col_count = lax.axis_size("col")
        ny, nz = GRIDS[col_count]
        leaf_rows = parent_rows // lax.axis_size("row")
        own_rows = leaf_rows // (2 * col_count)
        expanded = expand_rows(schur_blocks[0], child_map, leaf_rows)
        return finish(*fused(expanded, child_map, round_seeds, ny, nz, own_rows, leaf_rows))
    return body


def solution(mesh, parent_rows=24576):
    placed = (P("child", "row", "col"), P(), P())
    return jax.shard_map(
        make_body(parent_rows),
        mesh=mesh,
        in_specs=placed,
        out_specs=(P(("row", "child", "col"), None), P(("row", "child", "col"), None)),
        check_vma=False,
    )
```
